512 devices in a mesh: member: 32 (over x, z_lo), tile: 16 (over y, z_hi, core).
Axes of the slice: x: 4, y: 4, z: 16 (z_hi: 2, z_lo: 8; z = z_hi * 8 + z_lo), core: 2. Of those that a mesh axis runs over, the one named last changes fastest.
Arguments:
- saturation: float32 [32, 128, 64, 128], P('member', 'tile'), may hold values from 0.05 to 0.95
- mobility: float32 [32, 128, 64, 128], P('member', 'tile'), may hold values from 0.5 to 4
- pore_scale: float32 [32, 128, 64, 128], P('member', 'tile'), may hold values from 0.5 to 1.5
- flux_x: float32 [32, 128, 64, 128], P('member', 'tile'), may hold values from -0.15 to 0.15
- flux_y: float32 [32, 128, 64, 128], P('member', 'tile'), may hold values from -0.15 to 0.15
- flux_z: float32 [32, 128, 64, 128], P('member', 'tile'), may hold values from -0.15 to 0.15
- conn_cell: int32 [4096], P('tile'), may hold values from 0 to 65535
- conn_well: int32 [4096], P('tile'), may hold values from 0 to 127
- conn_factor: float32 [4096], P('tile'), may hold values from 0.02 to 0.2
- obs_error: float32 [128, 3], P('tile'), may hold values from 0.3 to 3
Outputs:
- new_saturation: float32 [32, 128, 64, 128], P('member', 'tile')
- well_rates: float32 [32, 128, 3], P('member', 'tile')
- gram: float32 [32, 32], P('member')
The draws below stay inside these ranges and needn't reach their ends.
Inputs may be any that keep to these rules, and one draw needn't show every extreme that they name: `conn_cell`: a cell index within the block of grid rows of the tile that holds the connection, flattened over (row, layer, column). `conn_well`: a well index; any tile may hold connections of any well.
All inputs are finite; a program needn't handle non-finite values.
Results may differ from the reference program's by a relative error of at most 0.0003.
Values sent between devices are 32-bit elements; how exact they have to be, the bound alone decides.
No kernel may reach another device: no remote copies, remote signals or barrier semaphores. Data moves between devices by JAX's collectives and lax.ppermute only.
A program may use at most 64 MiB of HBM per device.

```python
import math
import jax
import jax.numpy as jnp
import numpy as np
from jax import lax

CX = 8
NZ = 64
NY = 128
SUBSTEPS = 3
CONN_DEV = 256
NE = 32
NX = 128
NWELL = 128
CONNS = 4096


def plant(result, stream_key, least, largest):
    longest = result.shape.index(max(result.shape))
    spots = []
    for shift in (0, 1):
        where = [jax.random.randint(jax.random.fold_in(stream_key, axis), (), 0, length) for axis, length in enumerate(result.shape)]
        where[longest] = (where[longest] + shift) % result.shape[longest]
        spots.append(tuple(where))
    return result.at[spots[0]].set(least).at[spots[1]].set(largest)


def block_levels(stream_key, extent, split, least, largest):
    def one(position, shards_of):
        heights = jax.random.uniform(jax.random.fold_in(jax.random.fold_in(stream_key, 6), position), (shards_of,), jnp.float32, least / len(split), largest / len(split))
        return jnp.repeat(jnp.exp(heights), extent[position] // shards_of).reshape((-1,) + (1,) * (len(extent) - position - 1))

    level = one(*split[0])
    for cut in split[1:]:
        level = level * one(*cut)
    return level


def rank_bounds(count, skew):
    weights = [(1 << 20) // math.isqrt(standing ** skew) + 1 for standing in range(1, count + 1)]
    deviation = 1 + sum(weights) // (1 << 30)
    return np.cumsum(np.array([max(1, weight // deviation) for weight in weights]))


def skewed_ids(key, dims, number_of, skew):
    table = rank_bounds(number_of, skew)
    ticket = jax.random.randint(jax.random.fold_in(key, 1), dims, 0, int(table[number_of - 1]))
    standing = jnp.searchsorted(jnp.asarray(table, jnp.int32), ticket, side="right")
    return jax.random.permutation(jax.random.fold_in(key, 2), number_of)[standing].astype(jnp.int32)


def setup_inputs(seed: int = 0) -> dict:
    seeds = jax.random.split(jax.random.key(seed), 11)
    return {
        "saturation": jnp.clip(0.05 + 0.9 * jax.random.uniform(seeds[0], (NE, NX, NZ, NY), jnp.float32) ** block_levels(seeds[0], (NE, NX, NZ, NY), ((0, 32), (1, 16)), -0.2, 0.2), 0.05, 0.95),
        "mobility": jnp.clip(jnp.exp(math.log(4.0) - 2.0794415 * jax.random.uniform(seeds[1], (NE, NX, NZ, NY), jnp.float32) ** block_levels(seeds[1], (NE, NX, NZ, NY), ((0, 32), (1, 16)), -0.2, 0.2)), 0.5, 4.0),
        "pore_scale": jnp.clip(jnp.exp(math.log(1.5) - 1.0986123 * jax.random.uniform(seeds[2], (NE, NX, NZ, NY), jnp.float32) ** block_levels(seeds[2], (NE, NX, NZ, NY), ((0, 32), (1, 16)), -0.2, 0.2)), 0.5, 1.5),
        "flux_x": jnp.clip(jax.random.uniform(seeds[3], (NE, NX, NZ, NY), jnp.float32, -0.15, 0.15) * block_levels(seeds[3], (NE, NX, NZ, NY), ((0, 32), (1, 16)), -0.4, 0.0), -0.15, 0.15),
        "flux_y": jnp.clip(jax.random.uniform(seeds[4], (NE, NX, NZ, NY), jnp.float32, -0.15, 0.15) * block_levels(seeds[4], (NE, NX, NZ, NY), ((0, 32), (1, 16)), -0.4, 0.0), -0.15, 0.15),
        "flux_z": jnp.clip(jax.random.uniform(seeds[5], (NE, NX, NZ, NY), jnp.float32, -0.15, 0.15) * block_levels(seeds[5], (NE, NX, NZ, NY), ((0, 32), (1, 16)), -0.4, 0.0), -0.15, 0.15),
        "conn_cell": plant(jax.random.randint(seeds[6], (CONNS,), 0, CX * NZ * NY), jax.random.fold_in(seeds[6], 1), 0, (CX * NZ * NY) - 1).astype(jnp.int32),
        "conn_well": plant(skewed_ids(seeds[7], (CONNS,), NWELL, 2), jax.random.fold_in(seeds[7], 3), 0, NWELL - 1).astype(jnp.int32),
        "conn_factor": jnp.clip(jnp.exp(math.log(0.2) - 2.3025851 * jax.random.uniform(seeds[8], (CONNS,), jnp.float32) ** block_levels(seeds[8], (CONNS,), ((0, 16),), -0.2, 0.2)), 0.02, 0.2),
        "obs_error": jnp.clip(jnp.exp(math.log(3.0) - 2.3025851 * jax.random.uniform(seeds[9], (NWELL, SUBSTEPS), jnp.float32) ** block_levels(seeds[9], (NWELL, SUBSTEPS), ((0, 16),), -0.2, 0.2)), 0.3, 3.0),
    }


def frac(sat, mob):
    wet = sat * sat
    dry = (1.0 - sat) * (1.0 - sat)
    return wet / (wet + mob * dry)


def lower(field, axis):
    count = field.shape[axis]
    zero = jnp.zeros_like(lax.slice_in_dim(field, 0, 1, axis=axis))
    return jnp.concatenate([zero, lax.slice_in_dim(field, 0, count - 1, axis=axis)], axis=axis)


def upper(field, axis):
    count = field.shape[axis]
    zero = jnp.zeros_like(lax.slice_in_dim(field, 0, 1, axis=axis))
    return jnp.concatenate([lax.slice_in_dim(field, 1, count, axis=axis), zero], axis=axis)


def divergence(flow, flux, axis):
    face = jnp.maximum(flux, 0.0) * lower(flow, axis) + jnp.minimum(flux, 0.0) * flow
    return upper(face, axis) - face


def masked(flux, axis):
    place = lax.broadcasted_iota(jnp.int32, flux.shape, axis)
    return jnp.where(place > 0, flux, jnp.zeros_like(flux))


def reference(saturation, mobility, pore_scale, flux_x, flux_y, flux_z, conn_cell, conn_well, conn_factor, obs_error):
    members = saturation.shape[0]
    tile_of = (jnp.arange(CONNS, dtype=jnp.int32) // CONN_DEV).astype(jnp.int32)
    cells = (tile_of * (CX * NZ * NY) + conn_cell).astype(jnp.int32)

    def member_run(items):
        sat, mob, pore, qx, qy, qz = items
        qx = masked(qx, 0)
        qz = masked(qz, 1)
        qy = masked(qy, 2)
        mob_flat = mob.reshape(-1)[cells]
        parts = []
        for step in range(SUBSTEPS):
            flow = frac(sat, mob)
            total = divergence(flow, qx, 0) + divergence(flow, qz, 1) + divergence(flow, qy, 2)
            sat = sat - pore * total
            parts.append(conn_factor * frac(sat.reshape(-1)[cells], mob_flat))
        return sat, jnp.stack(parts, -1)

    new_saturation, contrib = lax.map(member_run, (saturation, mobility, pore_scale, flux_x, flux_y, flux_z))
    rates = jax.ops.segment_sum(jnp.transpose(contrib, (1, 0, 2)), conn_well, num_segments=NWELL)
    well_rates = jnp.transpose(rates, (1, 0, 2))
    data = (well_rates / obs_error[None]).reshape(members, -1)
    centered = data - jnp.mean(data, axis=0, keepdims=True)
    gram = jnp.dot(centered, centered.T, precision=lax.Precision.HIGHEST) / (members - 1.0)
    return new_saturation, well_rates, gram
```

```python
import jax
import jax.numpy as jnp
from jax import lax
from jax.experimental import pallas as pl
from jax.experimental.pallas import tpu as pltpu
from jax.sharding import Mesh
from jax.sharding import PartitionSpec as P

SUBSTEPS = 3
AXES = ("x", "zl", "y", "zh", "c")
SIZES = (4, 8, 4, 2, 2)
MEMBER = ("x", "zl")
TILE = ("y", "zh", "c")
LINE = ("zl", "zh", "c")
PLANE = ("x", "y")
UP_ROWS = 8
DOWN_ROWS = 9
HIGHEST = lax.Precision.HIGHEST


def frac(sat, mob):
    wet = sat * sat
    dry = (1.0 - sat) * (1.0 - sat)
    return wet / (wet + mob * dry)


def inner(flux, axis):
    return jnp.where(lax.broadcasted_iota(jnp.int32, flux.shape, axis) > 0, flux, 0.0)


def spread(flow, flux, axis):
    count = flow.shape[axis]
    face = jnp.maximum(flux, 0.0) * pltpu.roll(flow, 1, axis) + jnp.minimum(flux, 0.0) * flow
    return pltpu.roll(face, count - 1, axis) - face


def across(flux, below, here):
    return jnp.maximum(flux, 0.0) * below + jnp.minimum(flux, 0.0) * here


def edge_kernel(sat, mob, pore, qx, qy, qz, up, down):
    f = {i: frac(sat[i], mob[i]) for i in (0, 1, 2, 5, 6, 7)}

    def face(i):
        return across(qx[i], f[i - 1], f[i])

    def advanced(i, low, high):
        total = (
            high - low + spread(f[i], inner(qz[i], 0), 0) + spread(f[i], inner(qy[i], 1), 1)
        )
        return frac(sat[i] - pore[i] * total, mob[i])

    face_1 = face(1)
    face_7 = face(7)
    flow_1 = advanced(1, face_1, face(2))
    flow_6 = advanced(6, face(6), face_7)
    for row, out in ((7, up), (0, down)):
        out[0] = sat[row]
        out[1] = mob[row]
        out[2] = pore[row]
        out[3] = qz[row]
        out[4] = qy[row]
    up[5] = face_7
    up[6] = jnp.maximum(qx[7], 0.0) * flow_6
    up[7] = jnp.minimum(qx[7], 0.0)
    down[5] = qx[0]
    down[6] = face_1
    down[7] = jnp.maximum(qx[1], 0.0)
    down[8] = jnp.minimum(qx[1], 0.0) * flow_1


def main_kernel(
    sat, mob, pore, qx, qy, qz, low, high, cell, well, factor, obs, where, new_sat, shares, s, f
):
    tile = where[0]
    last = where[1]
    rows = sat.shape[0]
    layers, columns = sat.shape[1], sat.shape[2]
    cells = rows * layers

    def at(i, own, k):
        if i < 0:
            return low[k]
        if i == rows:
            return high[k]
        return own[i]

    def mob_at(i):
        if i < 0:
            return jnp.where(tile > 0, low[1], 1.0)
        if i == rows:
            return jnp.where(tile < last, high[1], 1.0)
        return mob[i]

    def qx_at(i):
        if i == 0:
            return jnp.where(tile > 0, qx[0], 0.0)
        if i == rows:
            return high[5]
        return qx[i]

    row_of = cell[...] // columns
    column_of = cell[...] - row_of * columns
    count = cell.shape[1]
    pick_row = (lax.broadcasted_iota(jnp.int32, (cells, count), 0) == row_of).astype(jnp.float32)
    pick_column = lax.broadcasted_iota(jnp.int32, (columns, count), 0) == column_of
    picked = []
    for step in range(SUBSTEPS):
        for i in range(-1, rows + 1):
            now = at(i, sat, 0) if step == 0 else s[i + 1]
            f[i + 1] = frac(now, mob_at(i))
        first, stop = (0, rows) if step == SUBSTEPS - 1 else (-1, rows + 1)
        if first == 0:
            face = across(qx_at(0), f[0], f[1])
        elif step == 0:
            face = low[5]
        else:
            face = low[6] + low[7] * f[0]
        for i in range(first, stop):
            if i < rows:
                above = across(qx_at(i + 1), f[i + 1], f[i + 2])
            elif step == 0:
                above = high[6]
            else:
                above = high[7] * f[i + 1] + high[8]
            flow = f[i + 1]
            total = (
                above
                - face
                + spread(flow, inner(at(i, qz, 3), 0), 0)
                + spread(flow, inner(at(i, qy, 4), 1), 1)
            )
            face = above
            now = at(i, sat, 0) if step == 0 else s[i + 1]
            moved = now - at(i, pore, 2) * total
            if step < SUBSTEPS - 1:
                s[i + 1] = moved
            else:
                new_sat[i] = moved
                f[i + 1] = frac(moved, mob[i])
        if step < SUBSTEPS - 1:
            flows = jnp.concatenate([frac(s[i + 1], mob[i]) for i in range(rows)], axis=0)
        else:
            flows = jnp.concatenate([f[i + 1] for i in range(rows)], axis=0)
        rows_of = lax.dot_general(
            flows, pick_row, (((0,), (0,)), ((), ())), precision=HIGHEST,
            preferred_element_type=jnp.float32,
        )
        picked.append(jnp.sum(jnp.where(pick_column, rows_of, 0.0), axis=0, keepdims=True))
    contrib = jnp.concatenate(picked, axis=0) * factor[...]
    wells = shares.shape[2]
    by_well = (lax.broadcasted_iota(jnp.int32, (wells, count), 0) == well[...]).astype(jnp.float32)
    rates = lax.dot_general(
        contrib, by_well, (((1,), (1,)), ((), ())), precision=HIGHEST,
        preferred_element_type=jnp.float32,
    )
    mine = obs.shape[0]
    lane = lax.broadcasted_iota(jnp.int32, (mine, wells), 1)
    sublane = lax.broadcasted_iota(jnp.int32, (mine, wells), 0)
    place = lane == sublane + tile * mine
    errors = [
        jnp.sum(jnp.where(place, obs[:, k : k + 1], 0.0), axis=0, keepdims=True)
        for k in range(SUBSTEPS)
    ]
    share = jnp.concatenate([rates] + errors + [jnp.zeros((2, wells), jnp.float32)], axis=0)
    shares[...] = jnp.broadcast_to(share[None], shares.shape)


def line_kernel(parts, out, t):
    members = 8
    per = parts.shape[0] // members
    for m in range(members):
        total = parts[m * per]
        for j in range(1, per):
            total = total + parts[m * per + j]
        t[8 * m : 8 * m + 8] = total
    block = jnp.concatenate(
        [t[pl.ds(k, members, stride=8), :] for k in range(SUBSTEPS)]
        + [t[SUBSTEPS : 2 * SUBSTEPS], jnp.zeros((5, t.shape[1]), jnp.float32)],
        axis=0,
    )
    out[...] = jnp.broadcast_to(block[None], out.shape)


def gram_kernel(parts, where, rates_out, gram):
    tile = where[0]
    own_x = where[2]
    own_z = where[3]
    groups, per, layer = 4, 4, 8
    sums = []
    for g in range(groups):
        total = parts[g * per]
        for j in range(1, per):
            total = total + parts[g * per + j]
        sums.append(total)
    ensemble = groups * layer
    mask_z = lax.broadcasted_iota(jnp.int32, (layer, sums[0].shape[1]), 0) == own_z
    line = jnp.zeros(gram.shape, jnp.float32)
    wells = rates_out.shape[2]
    pick = (
        lax.broadcasted_iota(jnp.int32, (wells, sums[0].shape[1]), 1)
        == lax.broadcasted_iota(jnp.int32, (wells, sums[0].shape[1]), 0) + tile * wells
    ).astype(jnp.float32)
    for k in range(SUBSTEPS):
        rates = [total[k * layer : (k + 1) * layer] for total in sums]
        error = sums[0][SUBSTEPS * layer + k : SUBSTEPS * layer + k + 1]
        mine = jnp.zeros_like(rates[0])
        for g in range(groups):
            mine = jnp.where(jnp.logical_and(mask_z, own_x == g), rates[g], mine)
        mine = jnp.sum(mine, axis=0, keepdims=True)
        rates_out[k] = lax.dot_general(
            mine, pick, (((1,), (1,)), ((), ())), precision=HIGHEST,
            preferred_element_type=jnp.float32,
        )
        data = [rate / error for rate in rates]
        mean = jnp.sum(sum(data[1:], data[0]), axis=0, keepdims=True) / ensemble
        centered = jnp.concatenate(data, axis=0) - mean
        own = mine / error - mean
        line = line + lax.dot_general(
            own, centered, (((1,), (1,)), ((), ())), precision=HIGHEST,
            preferred_element_type=jnp.float32,
        )
    gram[...] = line / (ensemble - 1.0)


VMEM = pl.BlockSpec(memory_space=pltpu.VMEM)
SMEM = pl.BlockSpec(memory_space=pltpu.SMEM)


def shape(*dims):
    return jax.ShapeDtypeStruct(dims, jnp.float32)


def body(
    saturation,
    mobility,
    pore_scale,
    flux_x,
    flux_y,
    flux_z,
    conn_cell,
    conn_well,
    conn_factor,
    obs_error,
):
    rows, layers, columns = saturation.shape[1:]
    fields = [
        a.reshape(rows, layers, columns)
        for a in (saturation, mobility, pore_scale, flux_x, flux_y, flux_z)
    ]
    tiles = lax.axis_size(TILE)
    tile = lax.axis_index(TILE)
    where = jnp.stack(
        [tile, jnp.full_like(tile, tiles - 1), lax.axis_index("x"), lax.axis_index("zl")]
    ).astype(jnp.int32)
    up, down = pl.pallas_call(
        edge_kernel,
        out_shape=(shape(UP_ROWS, layers, columns), shape(DOWN_ROWS, layers, columns)),
        in_specs=[VMEM] * 6,
        out_specs=(VMEM, VMEM),
        name="edges",
    )(*fields)
    low = lax.ppermute(up, TILE, [(i, i + 1) for i in range(tiles - 1)])
    high = lax.ppermute(down, TILE, [(i + 1, i) for i in range(tiles - 1)])
    wells = obs_error.shape[0] * tiles
    count = conn_cell.shape[0]
    new_saturation, shares = pl.pallas_call(
        main_kernel,
        out_shape=(shape(rows, layers, columns), shape(32, 8, wells)),
        in_specs=[VMEM] * 12 + [SMEM],
        out_specs=(VMEM, VMEM),
        scratch_shapes=[
            pltpu.VMEM((rows + 2, layers, columns), jnp.float32),
            pltpu.VMEM((rows + 2, layers, columns), jnp.float32),
        ],
        compiler_params=pltpu.CompilerParams(vmem_limit_bytes=32 * 1024 * 1024),
        name="transport",
    )(
        *fields,
        low,
        high,
        conn_cell.reshape(1, count),
        conn_well.reshape(1, count),
        conn_factor.reshape(1, count),
        obs_error,
        where,
    )
    line = lax.all_to_all(shares, LINE, 0, 0)
    spreads = pl.pallas_call(
        line_kernel,
        out_shape=shape(16, 32, wells),
        in_specs=[VMEM],
        out_specs=VMEM,
        scratch_shapes=[pltpu.VMEM((64, wells), jnp.float32)],
        name="line_sums",
    )(line)
    plane = lax.all_to_all(spreads, PLANE, 0, 0)
    rates, gram = pl.pallas_call(
        gram_kernel,
        out_shape=(shape(SUBSTEPS, 1, obs_error.shape[0]), shape(1, 32)),
        in_specs=[VMEM, SMEM],
        out_specs=(VMEM, VMEM),
        name="gram_row",
    )(plane, where)
    return (
        new_saturation.reshape(saturation.shape),
        jnp.transpose(rates, (1, 2, 0)),
        gram,
    )


def solution(mesh):
    split = Mesh(mesh.devices.reshape(SIZES), AXES)
    in_specs = (P(MEMBER, TILE, None, None),) * 6 + (P(TILE),) * 3 + (P(TILE, None),)
    out_specs = (P(MEMBER, TILE, None, None), P(MEMBER, TILE, None), P(MEMBER, None))
    return jax.shard_map(body, mesh=split, in_specs=in_specs, out_specs=out_specs, check_vma=False)
```

```python
import jax
import jax.numpy as jnp
from jax import lax
from jax.experimental import pallas as pl
from jax.experimental.pallas import tpu as pltpu
from jax.sharding import Mesh
from jax.sharding import PartitionSpec as P

SUBSTEPS = 3
AXES = ("x", "zl", "y", "zh", "c")
SIZES = (4, 8, 4, 2, 2)
MEMBER = ("x", "zl")
TILE = ("y", "zh", "c")
LINE = ("zl", "zh", "c")
PLANE = ("x", "y")
UP_ROWS = 7
DOWN_ROWS = 8
HIGHEST = lax.Precision.HIGHEST


def frac(sat, mob):
    wet = sat * sat
    dry = (1.0 - sat) * (1.0 - sat)
    return wet / (wet + mob * dry)


def inner(flux, axis):
    return jnp.where(lax.broadcasted_iota(jnp.int32, flux.shape, axis) > 0, flux, 0.0)


def across(flux, below, here):
    return flux * jnp.where(flux > 0.0, below, here)


def spread(flow, flux, axis):
    face = across(flux, pltpu.roll(flow, 1, axis), flow)
    return pltpu.roll(face, flow.shape[axis] - 1, axis) - face


def edge_kernel(sat, mob, pore, qx, qy, qz, up, down, s, m, p, x, y, z, made, raw_sem, in_sem, out_sem):
    loads = [
        pltpu.make_async_copy(sat, s, in_sem.at[0]),
        pltpu.make_async_copy(mob, m, in_sem.at[1]),
        pltpu.make_async_copy(qx.at[pl.ds(1, 7)], x.at[pl.ds(1, 7)], in_sem.at[2]),
    ]
    for k, (field, held) in enumerate(((pore, p), (qy, y), (qz, z))):
        for j, row in enumerate((1, 6)):
            loads.append(
                pltpu.make_async_copy(field.at[row], held.at[j], in_sem.at[3 + 2 * k + j])
            )
    for load in loads:
        load.start()
    raws = []
    for row, out, base in ((7, up, 0), (0, down, UP_ROWS)):
        for k, field in enumerate((sat, mob, pore, qz, qy)):
            raws.append(pltpu.make_async_copy(field.at[row], out.at[k], raw_sem.at[base + k]))
    raws.append(pltpu.make_async_copy(qx.at[0], down.at[5], raw_sem.at[5]))
    for raw in raws:
        raw.start()
    for load in loads:
        load.wait()
    f = {i: frac(s[i], m[i]) for i in (0, 1, 2, 5, 6, 7)}

    def face(i):
        return across(x[i], f[i - 1], f[i])

    def advanced(i, j, low, high):
        total = (
            high - low + spread(f[i], inner(z[j], 0), 0) + spread(f[i], inner(y[j], 1), 1)
        )
        return frac(s[i] - p[j] * total, m[i])

    face_1 = face(1)
    face_7 = face(7)
    made[0] = face_7
    made[1] = jnp.maximum(x[7], 0.0) * advanced(6, 1, face(6), face_7)
    up_copy = pltpu.make_async_copy(made.at[pl.ds(0, 2)], up.at[pl.ds(5, 2)], out_sem.at[0])
    up_copy.start()
    made[2] = face_1
    made[3] = jnp.minimum(x[1], 0.0) * advanced(1, 0, face_1, face(2))
    down_copy = pltpu.make_async_copy(made.at[pl.ds(2, 2)], down.at[pl.ds(6, 2)], out_sem.at[1])
    down_copy.start()
    for raw in raws:
        raw.wait()
    up_copy.wait()
    down_copy.wait()


def main_kernel(
    sat, mob, pore, qx, qy, qz, low, high, cell, well, factor, obs, where, new_sat, shares, s, f, outer
):
    tile = where[0]
    last = where[1]
    rows, layers, columns = sat.shape
    cells = rows * layers

    def at(i, own, k):
        if i < 0:
            return low[k]
        if i == rows:
            return high[k]
        return own[i]

    def guarded(i, own, k, missing):
        if i < 0:
            return jnp.where(tile > 0, low[k], missing)
        if i == rows:
            return jnp.where(tile < last, high[k], missing)
        return own[i]

    def mob_at(i):
        return guarded(i, mob, 1, 1.0)

    def qx_at(i):
        if i == 0:
            return jnp.where(tile > 0, qx[0], 0.0)
        if i == rows:
            return high[5]
        return qx[i]

    count = cell.shape[1]
    row_of = cell[...] // columns
    column_of = cell[...] - row_of * columns
    pick_row = (lax.broadcasted_iota(jnp.int32, (cells, count), 0) == row_of).astype(jnp.float32)
    pick_column = lax.broadcasted_iota(jnp.int32, (columns, count), 0) == column_of
    picked = []
    for step in range(SUBSTEPS):
        for i in range(-1, rows + 1):
            if step == 0:
                f[i + 1] = frac(guarded(i, sat, 0, 0.5), mob_at(i))
            elif step == 1 or i in (-1, rows):
                f[i + 1] = frac(s[i + 1], mob_at(i))
            else:
                f[i + 1] = frac(s[i + 1], mob[i])
        if step == 0:
            outer[0] = jnp.minimum(low[5], 0.0) / f[0]
            outer[1] = jnp.maximum(high[6], 0.0) / f[rows + 1]
        if step > 0:
            flows = jnp.concatenate([f[i + 1] for i in range(rows)], axis=0)
            picked.append(pick(flows, pick_row, pick_column))
        first, stop = (0, rows) if step == SUBSTEPS - 1 else (-1, rows + 1)
        if first == 0:
            face = across(qx_at(0), f[0], f[1])
        elif step == 0:
            face = low[5]
        else:
            face = low[6] + outer[0] * f[0]
        for i in range(first, stop):
            if i < rows:
                above = across(qx_at(i + 1), f[i + 1], f[i + 2])
            elif step == 0:
                above = high[6]
            else:
                above = outer[1] * f[i + 1] + high[7]
            flow = f[i + 1]
            total = (
                above
                - face
                + spread(flow, inner(at(i, qz, 3), 0), 0)
                + spread(flow, inner(at(i, qy, 4), 1), 1)
            )
            face = above
            now = guarded(i, sat, 0, 0.5) if step == 0 else s[i + 1]
            moved = now - at(i, pore, 2) * total
            if step < SUBSTEPS - 1:
                s[i + 1] = moved
            else:
                new_sat[i] = moved
                f[i + 1] = frac(moved, mob[i])
    flows = jnp.concatenate([f[i + 1] for i in range(rows)], axis=0)
    picked.append(pick(flows, pick_row, pick_column))
    contrib = jnp.concatenate(picked, axis=0) * factor[...]
    wells = shares.shape[1]
    by_well = (lax.broadcasted_iota(jnp.int32, (wells, count), 0) == well[...]).astype(jnp.float32)
    rates = lax.dot_general(
        contrib, by_well, (((1,), (1,)), ((), ())), precision=HIGHEST,
        preferred_element_type=jnp.float32,
    )
    mine = obs.shape[1]
    errors = jnp.concatenate(
        [obs[k : k + 1, :] for k in range(SUBSTEPS)]
        + [jnp.zeros((1, wells - SUBSTEPS * mine), jnp.float32)],
        axis=1,
    )
    share = jnp.concatenate([rates, errors] * 2, axis=0)
    for j in range(shares.shape[0] // 8):
        shares[8 * j : 8 * j + 8, :] = share


def pick(flows, pick_row, pick_column):
    rows_of = lax.dot_general(
        flows, pick_row, (((0,), (0,)), ((), ())), precision=HIGHEST,
        preferred_element_type=jnp.float32,
    )
    return jnp.sum(jnp.where(pick_column, rows_of, 0.0), axis=0, keepdims=True)


def line_kernel(parts, out):
    members, per = 8, 4
    width = SUBSTEPS + 1
    rows = []
    for k in range(SUBSTEPS):
        total = parts[pl.ds(k, members, stride=per * width), :]
        for j in range(1, per):
            total = total + parts[pl.ds(width * j + k, members, stride=per * width), :]
        rows.append(total)
    errors = [parts[width * j + SUBSTEPS : width * j + SUBSTEPS + 1, :] for j in range(per)]
    rows.append(jnp.concatenate(errors * 2, axis=0))
    for j in range(out.shape[0]):
        for k, row in enumerate(rows):
            out[j, members * k : members * (k + 1), :] = row


def gram_kernel(parts, where, rates_out, gram):
    tile = where[0]
    own_x = where[2]
    own_z = where[3]
    groups, per, layer = 4, 4, 8
    rows = SUBSTEPS * layer
    wells = parts.shape[2]
    mine = rates_out.shape[2]
    sums = []
    for g in range(groups):
        total = parts[g * per, :rows]
        for j in range(1, per):
            total = total + parts[g * per + j, :rows]
        sums.append(total)
    packed = jnp.concatenate([parts[y, rows : rows + per] for y in range(per)], axis=0)
    tiles = packed.shape[0]
    lane = lax.broadcasted_iota(jnp.int32, packed.shape, 1)
    home = lane // mine == lax.broadcasted_iota(jnp.int32, packed.shape, 0)
    errors = []
    for k in range(SUBSTEPS):
        front = packed if k == 0 else pltpu.roll(packed, wells - mine * k, 1)
        moved = pltpu.roll(front, 0, 1, stride=mine, stride_axis=0)
        errors.append(jnp.sum(jnp.where(home, moved, 0.0), axis=0, keepdims=True))
    ensemble = groups * layer
    own = sums[0]
    for g in range(1, groups):
        own = jnp.where(own_x == g, sums[g], own)
    mask_z = lax.broadcasted_iota(jnp.int32, (layer, wells), 0) == own_z
    own_rates = []
    own_centered = []
    centered = []
    for k in range(SUBSTEPS):
        part = slice(k * layer, (k + 1) * layer)
        data = [total[part] / errors[k] for total in sums]
        mean = jnp.sum(data[0] + data[1] + data[2] + data[3], axis=0, keepdims=True) / ensemble
        centered.append(jnp.concatenate([d - mean for d in data], axis=0))
        row = jnp.sum(jnp.where(mask_z, own[part], 0.0), axis=0, keepdims=True)
        own_rates.append(row)
        own_centered.append(row / errors[k] - mean)
    gram[...] = lax.dot_general(
        jnp.concatenate(own_centered, axis=1),
        jnp.concatenate(centered, axis=1),
        (((1,), (1,)), ((), ())),
        precision=HIGHEST,
        preferred_element_type=jnp.float32,
    ) / (ensemble - 1.0)
    select = (
        lax.broadcasted_iota(jnp.int32, (mine, wells), 1)
        == lax.broadcasted_iota(jnp.int32, (mine, wells), 0) + tile * mine
    ).astype(jnp.float32)
    chosen = lax.dot_general(
        jnp.concatenate(own_rates, axis=0), select, (((1,), (1,)), ((), ())), precision=HIGHEST,
        preferred_element_type=jnp.float32,
    )
    for k in range(SUBSTEPS):
        rates_out[k] = chosen[k : k + 1]


VMEM = pl.BlockSpec(memory_space=pltpu.VMEM)
ANY = pl.BlockSpec(memory_space=pl.ANY)
SMEM = pl.BlockSpec(memory_space=pltpu.SMEM)


def shape(*dims):
    return jax.ShapeDtypeStruct(dims, jnp.float32)


def body(
    saturation,
    mobility,
    pore_scale,
    flux_x,
    flux_y,
    flux_z,
    conn_cell,
    conn_well,
    conn_factor,
    obs_error,
):
    rows, layers, columns = saturation.shape[1:]
    fields = [
        a.reshape(rows, layers, columns)
        for a in (saturation, mobility, pore_scale, flux_x, flux_y, flux_z)
    ]
    tiles = lax.axis_size(TILE)
    tile = lax.axis_index(TILE)
    where = jnp.stack(
        [tile, jnp.full_like(tile, tiles - 1), lax.axis_index("x"), lax.axis_index("zl")]
    ).astype(jnp.int32)
    up, down = pl.pallas_call(
        edge_kernel,
        out_shape=(shape(UP_ROWS, layers, columns), shape(DOWN_ROWS, layers, columns)),
        in_specs=[ANY] * 6,
        out_specs=(ANY, ANY),
        scratch_shapes=[pltpu.VMEM((rows, layers, columns), jnp.float32)] * 2
        + [pltpu.VMEM((2, layers, columns), jnp.float32)]
        + [pltpu.VMEM((rows, layers, columns), jnp.float32)]
        + [pltpu.VMEM((2, layers, columns), jnp.float32)] * 2
        + [pltpu.VMEM((4, layers, columns), jnp.float32)]
        + [pltpu.SemaphoreType.DMA((12,)), pltpu.SemaphoreType.DMA((9,)), pltpu.SemaphoreType.DMA((2,))],
        name="edges",
    )(*fields)
    low = lax.ppermute(up, TILE, [(i, i + 1) for i in range(tiles - 1)])
    high = lax.ppermute(down, TILE, [(i + 1, i) for i in range(tiles - 1)])
    wells = obs_error.shape[0] * tiles
    count = conn_cell.shape[0]
    new_saturation, shares = pl.pallas_call(
        main_kernel,
        out_shape=(shape(rows, layers, columns), shape(128, wells)),
        in_specs=[VMEM] * 12 + [SMEM],
        out_specs=(VMEM, VMEM),
        scratch_shapes=[
            pltpu.VMEM((rows + 2, layers, columns), jnp.float32),
            pltpu.VMEM((rows + 2, layers, columns), jnp.float32),
            pltpu.VMEM((2, layers, columns), jnp.float32),
        ],
        compiler_params=pltpu.CompilerParams(vmem_limit_bytes=32 * 1024 * 1024),
        name="transport",
    )(
        *fields,
        low,
        high,
        conn_cell.reshape(1, count),
        conn_well.reshape(1, count),
        conn_factor.reshape(1, count),
        obs_error.T,
        where,
    )
    line = lax.all_to_all(shares.reshape(32, 4, wells), LINE, 0, 0)
    spreads = pl.pallas_call(
        line_kernel,
        out_shape=shape(16, 32, wells),
        in_specs=[VMEM],
        out_specs=VMEM,
        name="line_sums",
    )(line.reshape(128, wells))
    plane = lax.all_to_all(spreads, PLANE, 0, 0)
    rates, gram = pl.pallas_call(
        gram_kernel,
        out_shape=(shape(SUBSTEPS, 1, obs_error.shape[0]), shape(1, 32)),
        in_specs=[VMEM, SMEM],
        out_specs=(VMEM, VMEM),
        name="gram_row",
    )(plane, where)
    return (
        new_saturation.reshape(saturation.shape),
        jnp.transpose(rates, (1, 2, 0)),
        gram,
    )


def solution(mesh):
    split = Mesh(mesh.devices.reshape(SIZES), AXES)
    in_specs = (P(MEMBER, TILE, None, None),) * 6 + (P(TILE),) * 3 + (P(TILE, None),)
    out_specs = (P(MEMBER, TILE, None, None), P(MEMBER, TILE, None), P(MEMBER, None))
    return jax.shard_map(body, mesh=split, in_specs=in_specs, out_specs=out_specs, check_vma=False)
```

```python
import jax
import jax.numpy as jnp
from jax import lax
from jax.experimental import pallas as pl
from jax.experimental.pallas import tpu as pltpu
from jax.sharding import Mesh
from jax.sharding import PartitionSpec as P

SUBSTEPS = 3
AXES = ("x", "zl", "y", "zh", "c")
SIZES = (4, 8, 4, 2, 2)
MEMBER = ("x", "zl")
TILE = ("y", "zh", "c")
LINE = ("zl", "zh", "c")
PLANE = ("x", "y")
UP_ROWS = 7
DOWN_ROWS = 8
HIGHEST = lax.Precision.HIGHEST


def frac(sat, mob):
    wet = sat * sat
    dry = (1.0 - sat) * (1.0 - sat)
    return wet / (wet + mob * dry)


def inner(flux, axis):
    return jnp.where(lax.broadcasted_iota(jnp.int32, flux.shape, axis) > 0, flux, 0.0)


def across(flux, below, here):
    return flux * jnp.where(flux > 0.0, below, here)


def spread(flow, flux, axis):
    face = across(flux, pltpu.roll(flow, 1, axis), flow)
    return pltpu.roll(face, flow.shape[axis] - 1, axis) - face


def moved(sat, pore, net, flow, flux_z, flux_y):
    return sat - pore * (
        net + spread(flow, inner(flux_z, 0), 0) + spread(flow, inner(flux_y, 1), 1)
    )


def edge_kernel(sat, mob, pore, qx, qy, qz, up, down, s, m, p, x, y, z, made, in_sem, out_sem):
    loads = []
    for k, (field, held) in enumerate(((sat, s), (mob, m), (qx, x), (pore, p), (qy, y), (qz, z))):
        for j, start in enumerate((0, 5)):
            part = pl.ds(start, 3)
            loads.append(
                pltpu.make_async_copy(field.at[part], held.at[part], in_sem.at[2 * k + j])
            )
    for load in loads:
        load.start()
    for load in loads:
        load.wait()

    f = [frac(s[i], m[i]) for i in range(3)]
    face_1 = across(x[1], f[0], f[1])
    flow_1 = frac(moved(s[1], p[1], across(x[2], f[1], f[2]) - face_1, f[1], z[1], y[1]), m[1])
    for k, held in enumerate((s, m, p, z, y, x)):
        made[k] = held[0]
    made[6] = face_1
    made[7] = jnp.minimum(x[1], 0.0) * flow_1
    down_copy = pltpu.make_async_copy(made.at[pl.ds(0, DOWN_ROWS)], down, out_sem.at[0])
    down_copy.start()

    f = {i: frac(s[i], m[i]) for i in range(5, 8)}
    face_7 = across(x[7], f[6], f[7])
    flow_6 = frac(moved(s[6], p[6], face_7 - across(x[6], f[5], f[6]), f[6], z[6], y[6]), m[6])
    for k, held in enumerate((s, m, p, z, y)):
        made[DOWN_ROWS + k] = held[7]
    made[DOWN_ROWS + 5] = face_7
    made[DOWN_ROWS + 6] = jnp.maximum(x[7], 0.0) * flow_6
    up_copy = pltpu.make_async_copy(made.at[pl.ds(DOWN_ROWS, UP_ROWS)], up, out_sem.at[1])
    up_copy.start()
    down_copy.wait()
    up_copy.wait()


OUTER = ((0, 7), (1, 6), (2, 5))
INNER = ((3, 4), (2, 5), (1, 6))


def one_hot(row_of, pairs, layers):
    lane = lax.broadcasted_iota(jnp.int32, row_of.shape, 1)
    hots = []
    for first, second in pairs:
        target = jnp.where(lane < layers, lane + first * layers, lane + (second - 1) * layers)
        hots.append(jnp.where(row_of == target, 1.0, 0.0).astype(jnp.bfloat16))
    return jnp.concatenate(hots, axis=1)


def rates_of(flows, hot, mask, weight):
    stack = jnp.concatenate(flows, axis=0)
    big = stack.astype(jnp.bfloat16)
    rest = stack - big.astype(jnp.float32)
    middle = rest.astype(jnp.bfloat16)
    small = (rest - middle.astype(jnp.float32)).astype(jnp.bfloat16)
    found = mask * sum(
        jnp.dot(hot[:, : stack.shape[0]], part, preferred_element_type=jnp.float32)
        for part in (small, middle, big)
    )
    picked = jnp.sum(found, axis=1, keepdims=True)
    return jnp.sum(weight * picked, axis=0, keepdims=True)


def inside_kernel(
    sat, mob, pore, qx, qy, qz, cell, well, factor, obs, after, mids, middle, early, hot, mask, weight
):
    rows, layers, columns = sat.shape
    count = cell.shape[1]

    def column_of(row):
        return jnp.concatenate(
            [
                jnp.transpose(jnp.broadcast_to(row[:, j : j + columns], (columns, columns)))
                for j in range(0, count, columns)
            ],
            axis=0,
        )

    cells = column_of(cell[...])
    row_of = lax.div(cells, columns)
    lane = lax.broadcasted_iota(jnp.int32, cells.shape, 1)
    mask[...] = jnp.where(cells - row_of * columns == lane, 1.0, 0.0)
    hot[...] = one_hot(row_of, OUTER, layers)
    near = one_hot(row_of, INNER, layers)
    weight[...] = jnp.where(column_of(well[...]) == lane, column_of(factor[...]), 0.0)

    f = [frac(sat[i], mob[i]) for i in range(rows)]
    face = {i: across(qx[i], f[i - 1], f[i]) for i in range(1, rows)}
    mids[0] = f[0]
    mids[1] = f[7]
    mids[2] = moved(sat[0], pore[0], face[1], f[0], qz[0], qy[0])
    mids[3] = moved(sat[7], pore[7], -face[7], f[7], qz[7], qy[7])
    s = {i: moved(sat[i], pore[i], face[i + 1] - face[i], f[i], qz[i], qy[i]) for i in range(1, 7)}
    f = {i: frac(s[i], mob[i]) for i in range(1, 7)}
    rates = [rates_of([f[i] for pair in INNER for i in pair], near, mask[...], weight[...])]
    face = {i: across(qx[i], f[i - 1], f[i]) for i in range(2, 7)}
    mids[4] = f[1]
    mids[5] = f[6]
    mids[6] = moved(s[1], pore[1], face[2], f[1], qz[1], qy[1])
    mids[7] = moved(s[6], pore[6], -face[6], f[6], qz[6], qy[6])
    s = {i: moved(s[i], pore[i], face[i + 1] - face[i], f[i], qz[i], qy[i]) for i in range(2, 6)}
    f = {i: frac(s[i], mob[i]) for i in range(2, 6)}
    rates.append(rates_of([f[i] for pair in INNER[:2] for i in pair], near, mask[...], weight[...]))
    face = {i: across(qx[i], f[i - 1], f[i]) for i in range(3, 6)}
    mids[8] = f[2]
    mids[9] = f[5]
    mids[10] = moved(s[2], pore[2], face[3], f[2], qz[2], qy[2])
    mids[11] = moved(s[5], pore[5], -face[5], f[5], qz[5], qy[5])
    last = [moved(s[i], pore[i], face[i + 1] - face[i], f[i], qz[i], qy[i]) for i in (3, 4)]
    for j in range(2):
        middle[j] = last[j]
    flows = [frac(last[j], mob[3 + j]) for j in range(2)]
    rates.append(rates_of(flows, near, mask[...], weight[...]))
    errors = jnp.concatenate(
        [obs[k : k + 1, :] for k in range(SUBSTEPS)]
        + [jnp.zeros((1, columns - SUBSTEPS * obs.shape[1]), jnp.float32)],
        axis=1,
    )
    early[...] = jnp.concatenate(rates + [errors], axis=0)


def outside_kernel(
    mob, pore, qx, qy, qz, low, high, mids, middle, early, hot, mask, weight, where, new_sat, shares
):
    tile = where[0]
    last = where[1]
    has_low = tile > 0
    has_high = tile < last
    below = jnp.where(has_low, low[0], 0.5)
    below_mob = jnp.where(has_low, low[1], 1.0)
    above = jnp.where(has_high, high[0], 0.5)
    above_mob = jnp.where(has_high, high[1], 1.0)
    x = {i: qx[i] for i in range(1, 8)}
    x[0] = jnp.where(has_low, qx[0], 0.0)
    x[8] = high[5]
    z = {i: qz[i] for i in (0, 1, 6, 7)}
    z[-1], z[8] = low[3], high[3]
    y = {i: qy[i] for i in (0, 1, 6, 7)}
    y[-1], y[8] = low[4], high[4]
    p = {i: pore[i] for i in (0, 1, 2, 5, 6, 7)}
    p[-1], p[8] = low[2], high[2]
    m = {i: mob[i] for i in (0, 1, 2, 5, 6, 7)}
    m[-1], m[8] = below_mob, above_mob

    f = {-1: frac(below, below_mob), 0: mids[0], 7: mids[1], 8: frac(above, above_mob)}
    out_low = jnp.minimum(low[5], 0.0) / f[-1]
    out_high = jnp.maximum(high[6], 0.0) / f[8]
    face = {i: across(x[i], f[i - 1], f[i]) for i in (0, 8)}
    s = {
        -1: moved(below, p[-1], face[0] - low[5], f[-1], z[-1], y[-1]),
        0: mids[2] + p[0] * face[0],
        7: mids[3] - p[7] * face[8],
        8: moved(above, p[8], high[6] - face[8], f[8], z[8], y[8]),
    }

    f = {i: frac(s[i], m[i]) for i in (-1, 0, 7, 8)}
    rates = [rates_of([f[0], f[7]], hot, mask[...], weight[...])]
    f[1], f[6] = mids[4], mids[5]
    face = {i: across(x[i], f[i - 1], f[i]) for i in (0, 1, 7, 8)}
    face[-1] = low[6] + out_low * f[-1]
    face[9] = out_high * f[8] + high[7]
    s = {i: moved(s[i], p[i], face[i + 1] - face[i], f[i], z[i], y[i]) for i in (-1, 0, 7, 8)}
    s[1] = mids[6] + p[1] * face[1]
    s[6] = mids[7] - p[6] * face[7]

    f = {i: frac(s[i], m[i]) for i in (-1, 0, 1, 6, 7, 8)}
    rates.append(rates_of([f[0], f[7], f[1], f[6]], hot, mask[...], weight[...]))
    f[2], f[5] = mids[8], mids[9]
    face = {i: across(x[i], f[i - 1], f[i]) for i in (0, 1, 2, 6, 7, 8)}
    s = {i: moved(s[i], p[i], face[i + 1] - face[i], f[i], z[i], y[i]) for i in (0, 1, 6, 7)}
    s[2] = mids[10] + p[2] * face[2]
    s[5] = mids[11] - p[5] * face[6]
    for i in (0, 1, 2, 5, 6, 7):
        new_sat[i] = s[i]
    for j in range(2):
        new_sat[3 + j] = middle[j]
    f = {i: frac(s[i], m[i]) for i in (0, 1, 2, 5, 6, 7)}
    rates.append(
        rates_of([f[i] for pair in OUTER for i in pair], hot, mask[...], weight[...])
    )
    zero = jnp.zeros_like(rates[0])
    share = early[...] + jnp.concatenate(rates + [zero], axis=0)
    share = jnp.concatenate([share, share], axis=0)
    for j in range(shares.shape[0] // 8):
        shares[8 * j : 8 * j + 8, :] = share


def line_kernel(parts, out):
    members, per = 8, 4
    width = SUBSTEPS + 1
    rows = []
    for k in range(SUBSTEPS):
        total = parts[pl.ds(k, members, stride=per * width), :]
        for j in range(1, per):
            total = total + parts[pl.ds(width * j + k, members, stride=per * width), :]
        rows.append(total)
    errors = [parts[width * j + SUBSTEPS : width * j + SUBSTEPS + 1, :] for j in range(per)]
    rows.append(jnp.concatenate(errors * 2, axis=0))
    for j in range(out.shape[0]):
        for k, row in enumerate(rows):
            out[j, members * k : members * (k + 1), :] = row


def gram_kernel(parts, where, rates_out, gram):
    tile = where[0]
    own_x = where[2]
    own_z = where[3]
    groups, per, layer = 4, 4, 8
    rows = SUBSTEPS * layer
    wells = parts.shape[2]
    mine = rates_out.shape[2]
    sums = []
    for g in range(groups):
        total = parts[g * per, :rows]
        for j in range(1, per):
            total = total + parts[g * per + j, :rows]
        sums.append(total)
    packed = jnp.concatenate([parts[y, rows : rows + per] for y in range(per)], axis=0)
    tiles = packed.shape[0]
    lane = lax.broadcasted_iota(jnp.int32, packed.shape, 1)
    home = lane // mine == lax.broadcasted_iota(jnp.int32, packed.shape, 0)
    errors = []
    for k in range(SUBSTEPS):
        front = packed if k == 0 else pltpu.roll(packed, wells - mine * k, 1)
        moved = pltpu.roll(front, 0, 1, stride=mine, stride_axis=0)
        errors.append(jnp.sum(jnp.where(home, moved, 0.0), axis=0, keepdims=True))
    ensemble = groups * layer
    own = sums[0]
    for g in range(1, groups):
        own = jnp.where(own_x == g, sums[g], own)
    mask_z = lax.broadcasted_iota(jnp.int32, (layer, wells), 0) == own_z
    own_rates = []
    own_centered = []
    centered = []
    for k in range(SUBSTEPS):
        part = slice(k * layer, (k + 1) * layer)
        data = [total[part] / errors[k] for total in sums]
        mean = jnp.sum(data[0] + data[1] + data[2] + data[3], axis=0, keepdims=True) / ensemble
        centered.append(jnp.concatenate([d - mean for d in data], axis=0))
        row = jnp.sum(jnp.where(mask_z, own[part], 0.0), axis=0, keepdims=True)
        own_rates.append(row)
        own_centered.append(row / errors[k] - mean)
    gram[...] = lax.dot_general(
        jnp.concatenate(own_centered, axis=1),
        jnp.concatenate(centered, axis=1),
        (((1,), (1,)), ((), ())),
        precision=HIGHEST,
        preferred_element_type=jnp.float32,
    ) / (ensemble - 1.0)
    select = (
        lax.broadcasted_iota(jnp.int32, (mine, wells), 1)
        == lax.broadcasted_iota(jnp.int32, (mine, wells), 0) + tile * mine
    ).astype(jnp.float32)
    chosen = lax.dot_general(
        jnp.concatenate(own_rates, axis=0), select, (((1,), (1,)), ((), ())), precision=HIGHEST,
        preferred_element_type=jnp.float32,
    )
    for k in range(SUBSTEPS):
        rates_out[k] = chosen[k : k + 1]


VMEM = pl.BlockSpec(memory_space=pltpu.VMEM)
ANY = pl.BlockSpec(memory_space=pl.ANY)
SMEM = pl.BlockSpec(memory_space=pltpu.SMEM)


def shape(*dims):
    return jax.ShapeDtypeStruct(dims, jnp.float32)


def body(
    saturation,
    mobility,
    pore_scale,
    flux_x,
    flux_y,
    flux_z,
    conn_cell,
    conn_well,
    conn_factor,
    obs_error,
):
    rows, layers, columns = saturation.shape[1:]
    fields = [
        a.reshape(rows, layers, columns)
        for a in (saturation, mobility, pore_scale, flux_x, flux_y, flux_z)
    ]
    tiles = lax.axis_size(TILE)
    tile = lax.axis_index(TILE)
    where = jnp.stack(
        [tile, jnp.full_like(tile, tiles - 1), lax.axis_index("x"), lax.axis_index("zl")]
    ).astype(jnp.int32)
    up, down = pl.pallas_call(
        edge_kernel,
        out_shape=(shape(UP_ROWS, layers, columns), shape(DOWN_ROWS, layers, columns)),
        in_specs=[ANY] * 6,
        out_specs=(ANY, ANY),
        scratch_shapes=[pltpu.VMEM((rows, layers, columns), jnp.float32)] * 6
        + [pltpu.VMEM((UP_ROWS + DOWN_ROWS, layers, columns), jnp.float32)]
        + [pltpu.SemaphoreType.DMA((12,)), pltpu.SemaphoreType.DMA((2,))],
        name="edges",
    )(*fields)
    low = lax.ppermute(up, TILE, [(i, i + 1) for i in range(tiles - 1)])
    high = lax.ppermute(down, TILE, [(i + 1, i) for i in range(tiles - 1)])
    wells = obs_error.shape[0] * tiles
    count = conn_cell.shape[0]
    sat, mob, pore, qx, qy, qz = fields
    mids, middle, early, hot, mask, weight = pl.pallas_call(
        inside_kernel,
        out_shape=(
            shape(12, layers, columns),
            shape(2, layers, columns),
            shape(SUBSTEPS + 1, wells),
            jax.ShapeDtypeStruct((count, 6 * layers), jnp.bfloat16),
            shape(count, columns),
            shape(count, wells),
        ),
        in_specs=[VMEM] * 10 + [ANY],
        out_specs=(VMEM,) * 6,
        compiler_params=pltpu.CompilerParams(vmem_limit_bytes=32 * 1024 * 1024),
        name="inside",
    )(
        *fields,
        conn_cell.reshape(1, count),
        conn_well.reshape(1, count),
        conn_factor.reshape(1, count),
        obs_error.T,
        up,
    )
    new_saturation, shares = pl.pallas_call(
        outside_kernel,
        out_shape=(shape(rows, layers, columns), shape(128, wells)),
        in_specs=[VMEM] * 13 + [SMEM],
        out_specs=(VMEM, VMEM),
        compiler_params=pltpu.CompilerParams(vmem_limit_bytes=32 * 1024 * 1024),
        name="outside",
    )(mob, pore, qx, qy, qz, low, high, mids, middle, early, hot, mask, weight, where)
    line = lax.all_to_all(shares.reshape(32, 4, wells), LINE, 0, 0)
    spreads = pl.pallas_call(
        line_kernel,
        out_shape=shape(16, 32, wells),
        in_specs=[VMEM],
        out_specs=VMEM,
        name="line_sums",
    )(line.reshape(128, wells))
    plane = lax.all_to_all(spreads, PLANE, 0, 0)
    rates, gram = pl.pallas_call(
        gram_kernel,
        out_shape=(shape(SUBSTEPS, 1, obs_error.shape[0]), shape(1, 32)),
        in_specs=[VMEM, SMEM],
        out_specs=(VMEM, VMEM),
        name="gram_row",
    )(plane, where)
    return (
        new_saturation.reshape(saturation.shape),
        jnp.transpose(rates, (1, 2, 0)),
        gram,
    )


def solution(mesh):
    split = Mesh(mesh.devices.reshape(SIZES), AXES)
    in_specs = (P(MEMBER, TILE, None, None),) * 6 + (P(TILE),) * 3 + (P(TILE, None),)
    out_specs = (P(MEMBER, TILE, None, None), P(MEMBER, TILE, None), P(MEMBER, None))
    return jax.shard_map(body, mesh=split, in_specs=in_specs, out_specs=out_specs, check_vma=False)
```

```python
import jax
import jax.numpy as jnp
from jax import lax
from jax.experimental import pallas as pl
from jax.experimental.pallas import tpu as pltpu
from jax.sharding import Mesh
from jax.sharding import PartitionSpec as P

SUBSTEPS = 3
AXES = ("x", "zl", "y", "zh", "c")
SIZES = (4, 8, 4, 2, 2)
MEMBER = ("x", "zl")
TILE = ("y", "zh", "c")
LINE = ("zl", "zh", "c")
PLANE = ("x", "y")
UP_ROWS = 7
DOWN_ROWS = 8
HIGHEST = lax.Precision.HIGHEST


def frac(sat, mob):
    wet = sat * sat
    dry = (1.0 - sat) * (1.0 - sat)
    return wet / (wet + mob * dry)


def inner(flux, axis):
    return jnp.where(lax.broadcasted_iota(jnp.int32, flux.shape, axis) > 0, flux, 0.0)


def across(flux, below, here):
    return flux * jnp.where(flux > 0.0, below, here)


def spread(flow, flux, axis):
    face = across(flux, pltpu.roll(flow, 1, axis), flow)
    return pltpu.roll(face, flow.shape[axis] - 1, axis) - face


def moved(sat, pore, net, flow, flux_z, flux_y):
    return sat - pore * (
        net + spread(flow, inner(flux_z, 0), 0) + spread(flow, inner(flux_y, 1), 1)
    )


def edge_kernel(sat, mob, pore, qx, qy, qz, up, down, s, m, p, x, y, z, in_sem):
    loads = []
    for j, start in enumerate((0, 5)):
        for k, (field, near) in enumerate(
            ((sat, s), (mob, m), (qx, x), (qy, y), (qz, z), (pore, p))
        ):
            part = pl.ds(start, 3)
            loads.append(
                pltpu.make_async_copy(field.at[part], near.at[part], in_sem.at[6 * j + k])
            )
    for load in loads:
        load.start()
    for load in loads[:6]:
        load.wait()
    f = [frac(s[i], m[i]) for i in range(3)]
    face_1 = across(x[1], f[0], f[1])
    flow_1 = frac(moved(s[1], p[1], across(x[2], f[1], f[2]) - face_1, f[1], z[1], y[1]), m[1])
    for k, near in enumerate((s, m, p, z, y, x)):
        down[k] = near[0]
    down[6] = face_1
    down[7] = jnp.minimum(x[1], 0.0) * flow_1
    for load in loads[6:]:
        load.wait()
    f = {i: frac(s[i], m[i]) for i in range(5, 8)}
    face_7 = across(x[7], f[6], f[7])
    flow_6 = frac(moved(s[6], p[6], face_7 - across(x[6], f[5], f[6]), f[6], z[6], y[6]), m[6])
    for k, near in enumerate((s, m, p, z, y)):
        up[k] = near[7]
    up[5] = face_7
    up[6] = jnp.maximum(x[7], 0.0) * flow_6


OUTER = ((0, 7), (1, 6), (2, 5))
INNER = ((3, 4), (2, 5), (1, 6))


def one_hot(row_of, pairs, layers):
    lane = lax.broadcasted_iota(jnp.int32, row_of.shape, 1)
    hots = []
    for first, second in pairs:
        target = jnp.where(lane < layers, lane + first * layers, lane + (second - 1) * layers)
        hots.append(jnp.where(row_of == target, 1.0, 0.0).astype(jnp.bfloat16))
    return jnp.concatenate(hots, axis=1)


def rates_of(flows, hot, mask, weight):
    stack = jnp.concatenate(flows, axis=0)
    big = stack.astype(jnp.bfloat16)
    rest = stack - big.astype(jnp.float32)
    middle = rest.astype(jnp.bfloat16)
    small = (rest - middle.astype(jnp.float32)).astype(jnp.bfloat16)
    found = mask * sum(
        jnp.dot(hot[:, : stack.shape[0]], part, preferred_element_type=jnp.float32)
        for part in (small, middle, big)
    )
    picked = jnp.sum(found, axis=1, keepdims=True)
    return jnp.sum(weight * picked, axis=0, keepdims=True)


def inside_kernel(
    sat, mob, pore, qx, qy, qz, cell, well, factor, obs, after, mids, middle, early, hot, mask, weight
):
    rows, layers, columns = sat.shape
    count = cell.shape[1]

    def column_of(row):
        return jnp.concatenate(
            [
                jnp.transpose(jnp.broadcast_to(row[:, j : j + columns], (columns, columns)))
                for j in range(0, count, columns)
            ],
            axis=0,
        )

    cells = column_of(cell[...])
    row_of = lax.div(cells, columns)
    lane = lax.broadcasted_iota(jnp.int32, cells.shape, 1)
    mask[...] = jnp.where(cells - row_of * columns == lane, 1.0, 0.0)
    hot[...] = one_hot(row_of, OUTER, layers)
    near = one_hot(row_of, INNER, layers)
    weight[...] = jnp.where(column_of(well[...]) == lane, column_of(factor[...]), 0.0)

    f = [frac(sat[i], mob[i]) for i in range(rows)]
    face = {i: across(qx[i], f[i - 1], f[i]) for i in range(1, rows)}
    mids[0] = f[0]
    mids[1] = f[7]
    mids[2] = moved(sat[0], pore[0], face[1], f[0], qz[0], qy[0])
    mids[3] = moved(sat[7], pore[7], -face[7], f[7], qz[7], qy[7])
    s = {i: moved(sat[i], pore[i], face[i + 1] - face[i], f[i], qz[i], qy[i]) for i in range(1, 7)}
    f = {i: frac(s[i], mob[i]) for i in range(1, 7)}
    rates = [rates_of([f[i] for pair in INNER for i in pair], near, mask[...], weight[...])]
    face = {i: across(qx[i], f[i - 1], f[i]) for i in range(2, 7)}
    mids[4] = f[1]
    mids[5] = f[6]
    mids[6] = moved(s[1], pore[1], face[2], f[1], qz[1], qy[1])
    mids[7] = moved(s[6], pore[6], -face[6], f[6], qz[6], qy[6])
    s = {i: moved(s[i], pore[i], face[i + 1] - face[i], f[i], qz[i], qy[i]) for i in range(2, 6)}
    f = {i: frac(s[i], mob[i]) for i in range(2, 6)}
    rates.append(rates_of([f[i] for pair in INNER[:2] for i in pair], near, mask[...], weight[...]))
    face = {i: across(qx[i], f[i - 1], f[i]) for i in range(3, 6)}
    mids[8] = f[2]
    mids[9] = f[5]
    mids[10] = moved(s[2], pore[2], face[3], f[2], qz[2], qy[2])
    mids[11] = moved(s[5], pore[5], -face[5], f[5], qz[5], qy[5])
    last = [moved(s[i], pore[i], face[i + 1] - face[i], f[i], qz[i], qy[i]) for i in (3, 4)]
    for j in range(2):
        middle[j] = last[j]
    flows = [frac(last[j], mob[3 + j]) for j in range(2)]
    rates.append(rates_of(flows, near, mask[...], weight[...]))
    errors = jnp.concatenate(
        [obs[k : k + 1, :] for k in range(SUBSTEPS)]
        + [jnp.zeros((1, columns - SUBSTEPS * obs.shape[1]), jnp.float32)],
        axis=1,
    )
    early[...] = jnp.concatenate(rates + [errors], axis=0)


def outside_kernel(
    mob, pore, qx, qy, qz, low, high, mids, middle, early, hot, mask, weight, where, new_sat, shares
):
    tile = where[0]
    last = where[1]
    has_low = tile > 0
    has_high = tile < last
    below = jnp.where(has_low, low[0], 0.5)
    below_mob = jnp.where(has_low, low[1], 1.0)
    above = jnp.where(has_high, high[0], 0.5)
    above_mob = jnp.where(has_high, high[1], 1.0)
    x = {i: qx[i] for i in range(1, 8)}
    x[0] = jnp.where(has_low, qx[0], 0.0)
    x[8] = high[5]
    z = {i: qz[i] for i in (0, 1, 6, 7)}
    z[-1], z[8] = low[3], high[3]
    y = {i: qy[i] for i in (0, 1, 6, 7)}
    y[-1], y[8] = low[4], high[4]
    p = {i: pore[i] for i in (0, 1, 2, 5, 6, 7)}
    p[-1], p[8] = low[2], high[2]
    m = {i: mob[i] for i in (0, 1, 2, 5, 6, 7)}
    m[-1], m[8] = below_mob, above_mob

    f = {-1: frac(below, below_mob), 0: mids[0], 7: mids[1], 8: frac(above, above_mob)}
    out_low = jnp.minimum(low[5], 0.0) / f[-1]
    out_high = jnp.maximum(high[6], 0.0) / f[8]
    face = {i: across(x[i], f[i - 1], f[i]) for i in (0, 8)}
    s = {
        -1: moved(below, p[-1], face[0] - low[5], f[-1], z[-1], y[-1]),
        0: mids[2] + p[0] * face[0],
        7: mids[3] - p[7] * face[8],
        8: moved(above, p[8], high[6] - face[8], f[8], z[8], y[8]),
    }

    f = {i: frac(s[i], m[i]) for i in (-1, 0, 7, 8)}
    rates = [rates_of([f[0], f[7]], hot, mask[...], weight[...])]
    f[1], f[6] = mids[4], mids[5]
    face = {i: across(x[i], f[i - 1], f[i]) for i in (0, 1, 7, 8)}
    face[-1] = low[6] + out_low * f[-1]
    face[9] = out_high * f[8] + high[7]
    s = {i: moved(s[i], p[i], face[i + 1] - face[i], f[i], z[i], y[i]) for i in (-1, 0, 7, 8)}
    s[1] = mids[6] + p[1] * face[1]
    s[6] = mids[7] - p[6] * face[7]

    f = {i: frac(s[i], m[i]) for i in (-1, 0, 1, 6, 7, 8)}
    rates.append(rates_of([f[0], f[7], f[1], f[6]], hot, mask[...], weight[...]))
    f[2], f[5] = mids[8], mids[9]
    face = {i: across(x[i], f[i - 1], f[i]) for i in (0, 1, 2, 6, 7, 8)}
    s = {i: moved(s[i], p[i], face[i + 1] - face[i], f[i], z[i], y[i]) for i in (0, 1, 6, 7)}
    s[2] = mids[10] + p[2] * face[2]
    s[5] = mids[11] - p[5] * face[6]
    for i in (0, 1, 2, 5, 6, 7):
        new_sat[i] = s[i]
    for j in range(2):
        new_sat[3 + j] = middle[j]
    f = {i: frac(s[i], m[i]) for i in (0, 1, 2, 5, 6, 7)}
    rates.append(
        rates_of([f[i] for pair in OUTER for i in pair], hot, mask[...], weight[...])
    )
    zero = jnp.zeros_like(rates[0])
    share = early[...] + jnp.concatenate(rates + [zero], axis=0)
    share = jnp.concatenate([share, share], axis=0)
    for j in range(shares.shape[0] // 8):
        shares[8 * j : 8 * j + 8, :] = share


def line_kernel(parts, out):
    members, per = 8, 4
    width = SUBSTEPS + 1
    rows = []
    for k in range(SUBSTEPS):
        total = parts[pl.ds(k, members, stride=per * width), :]
        for j in range(1, per):
            total = total + parts[pl.ds(width * j + k, members, stride=per * width), :]
        rows.append(total)
    errors = [parts[width * j + SUBSTEPS : width * j + SUBSTEPS + 1, :] for j in range(per)]
    rows.append(jnp.concatenate(errors * 2, axis=0))
    for j in range(out.shape[0]):
        for k, row in enumerate(rows):
            out[j, members * k : members * (k + 1), :] = row


def gram_kernel(parts, where, rates_out, gram):
    tile = where[0]
    own_x = where[2]
    own_z = where[3]
    groups, per, layer = 4, 4, 8
    rows = SUBSTEPS * layer
    wells = parts.shape[2]
    mine = rates_out.shape[2]
    sums = []
    for g in range(groups):
        total = parts[g * per, :rows]
        for j in range(1, per):
            total = total + parts[g * per + j, :rows]
        sums.append(total)
    packed = jnp.concatenate([parts[y, rows : rows + per] for y in range(per)], axis=0)
    tiles = packed.shape[0]
    lane = lax.broadcasted_iota(jnp.int32, packed.shape, 1)
    home = lane // mine == lax.broadcasted_iota(jnp.int32, packed.shape, 0)
    errors = []
    for k in range(SUBSTEPS):
        front = packed if k == 0 else pltpu.roll(packed, wells - mine * k, 1)
        moved = pltpu.roll(front, 0, 1, stride=mine, stride_axis=0)
        errors.append(jnp.sum(jnp.where(home, moved, 0.0), axis=0, keepdims=True))
    ensemble = groups * layer
    own = sums[0]
    for g in range(1, groups):
        own = jnp.where(own_x == g, sums[g], own)
    mask_z = lax.broadcasted_iota(jnp.int32, (layer, wells), 0) == own_z
    own_rates = []
    own_centered = []
    centered = []
    for k in range(SUBSTEPS):
        part = slice(k * layer, (k + 1) * layer)
        data = [total[part] / errors[k] for total in sums]
        mean = jnp.sum(data[0] + data[1] + data[2] + data[3], axis=0, keepdims=True) / ensemble
        centered.append(jnp.concatenate([d - mean for d in data], axis=0))
        row = jnp.sum(jnp.where(mask_z, own[part], 0.0), axis=0, keepdims=True)
        own_rates.append(row)
        own_centered.append(row / errors[k] - mean)
    gram[...] = lax.dot_general(
        jnp.concatenate(own_centered, axis=1),
        jnp.concatenate(centered, axis=1),
        (((1,), (1,)), ((), ())),
        precision=HIGHEST,
        preferred_element_type=jnp.float32,
    ) / (ensemble - 1.0)
    select = (
        lax.broadcasted_iota(jnp.int32, (mine, wells), 1)
        == lax.broadcasted_iota(jnp.int32, (mine, wells), 0) + tile * mine
    ).astype(jnp.float32)
    chosen = lax.dot_general(
        jnp.concatenate(own_rates, axis=0), select, (((1,), (1,)), ((), ())), precision=HIGHEST,
        preferred_element_type=jnp.float32,
    )
    for k in range(SUBSTEPS):
        rates_out[k] = chosen[k : k + 1]


VMEM = pl.BlockSpec(memory_space=pltpu.VMEM)
ANY = pl.BlockSpec(memory_space=pl.ANY)
SMEM = pl.BlockSpec(memory_space=pltpu.SMEM)


def shape(*dims):
    return jax.ShapeDtypeStruct(dims, jnp.float32)


def held(*dims):
    return pltpu.VMEM(dims, jnp.float32)


def body(
    saturation,
    mobility,
    pore_scale,
    flux_x,
    flux_y,
    flux_z,
    conn_cell,
    conn_well,
    conn_factor,
    obs_error,
):
    rows, layers, columns = saturation.shape[1:]
    fields = [
        a.reshape(rows, layers, columns)
        for a in (saturation, mobility, pore_scale, flux_x, flux_y, flux_z)
    ]
    tiles = lax.axis_size(TILE)
    tile = lax.axis_index(TILE)
    where = jnp.stack(
        [tile, jnp.full_like(tile, tiles - 1), lax.axis_index("x"), lax.axis_index("zl")]
    ).astype(jnp.int32)
    up, down = pl.pallas_call(
        edge_kernel,
        out_shape=(held(UP_ROWS, layers, columns), held(DOWN_ROWS, layers, columns)),
        in_specs=[ANY] * 6,
        out_specs=(VMEM, VMEM),
        scratch_shapes=[pltpu.VMEM((rows, layers, columns), jnp.float32)] * 6
        + [pltpu.SemaphoreType.DMA((12,))],
        name="edges",
    )(*fields)
    low = lax.ppermute(up, TILE, [(i, i + 1) for i in range(tiles - 1)])
    high = lax.ppermute(down, TILE, [(i + 1, i) for i in range(tiles - 1)])
    wells = obs_error.shape[0] * tiles
    count = conn_cell.shape[0]
    sat, mob, pore, qx, qy, qz = fields
    mids, middle, early, hot, mask, weight = pl.pallas_call(
        inside_kernel,
        out_shape=(
            shape(12, layers, columns),
            shape(2, layers, columns),
            shape(SUBSTEPS + 1, wells),
            jax.ShapeDtypeStruct((count, 6 * layers), jnp.bfloat16),
            shape(count, columns),
            shape(count, wells),
        ),
        in_specs=[VMEM] * 10 + [ANY],
        out_specs=(VMEM,) * 6,
        compiler_params=pltpu.CompilerParams(vmem_limit_bytes=32 * 1024 * 1024),
        name="inside",
    )(
        *fields,
        conn_cell.reshape(1, count),
        conn_well.reshape(1, count),
        conn_factor.reshape(1, count),
        obs_error.T,
        up,
    )
    new_saturation, shares = pl.pallas_call(
        outside_kernel,
        out_shape=(held(rows, layers, columns), held(128, wells)),
        in_specs=[VMEM] * 13 + [SMEM],
        out_specs=(VMEM, VMEM),
        compiler_params=pltpu.CompilerParams(vmem_limit_bytes=32 * 1024 * 1024),
        name="outside",
    )(mob, pore, qx, qy, qz, low, high, mids, middle, early, hot, mask, weight, where)
    line = lax.all_to_all(shares.reshape(32, 4, wells), LINE, 0, 0)
    (spreads,) = pl.pallas_call(
        line_kernel,
        out_shape=(held(16, 32, wells),),
        in_specs=[VMEM],
        out_specs=(VMEM,),
        name="line_sums",
    )(line.reshape(128, wells))
    plane = pltpu.with_memory_space_constraint(lax.all_to_all(spreads, PLANE, 0, 0), pltpu.VMEM)
    rates, gram = pl.pallas_call(
        gram_kernel,
        out_shape=(shape(SUBSTEPS, 1, obs_error.shape[0]), shape(1, 32)),
        in_specs=[VMEM, SMEM],
        out_specs=(VMEM, VMEM),
        name="gram_row",
    )(plane, where)
    return (
        new_saturation.reshape(saturation.shape),
        jnp.transpose(rates, (1, 2, 0)),
        gram,
    )


def solution(mesh):
    split = Mesh(mesh.devices.reshape(SIZES), AXES)
    in_specs = (P(MEMBER, TILE, None, None),) * 6 + (P(TILE),) * 3 + (P(TILE, None),)
    out_specs = (P(MEMBER, TILE, None, None), P(MEMBER, TILE, None), P(MEMBER, None))
    return jax.shard_map(body, mesh=split, in_specs=in_specs, out_specs=out_specs, check_vma=False)
```

```python
import jax
import jax.numpy as jnp
from jax import lax
from jax.experimental import pallas as pl
from jax.experimental.pallas import tpu as pltpu
from jax.sharding import Mesh
from jax.sharding import PartitionSpec as P

SUBSTEPS = 3
AXES = ("x", "zl", "y", "zh", "c")
SIZES = (4, 8, 4, 2, 2)
MEMBER = ("x", "zl")
TILE = ("y", "zh", "c")
LINE = ("zl", "zh", "c")
PLANE = ("x", "y")
EDGE_ROWS = 8
HIGHEST = lax.Precision.HIGHEST


def frac(sat, mob):
    wet = sat * sat
    dry = (1.0 - sat) * (1.0 - sat)
    return wet / (wet + mob * dry)


def inner(flux, axis):
    return jnp.where(lax.broadcasted_iota(jnp.int32, flux.shape, axis) > 0, flux, 0.0)


def across(flux, below, here):
    return flux * jnp.where(flux > 0.0, below, here)


def spread(flow, flux, axis):
    face = across(flux, pltpu.roll(flow, 1, axis), flow)
    return pltpu.roll(face, flow.shape[axis] - 1, axis) - face


def moved(sat, pore, net, flow, flux_z, flux_y):
    return sat - pore * (
        net + spread(flow, inner(flux_z, 0), 0) + spread(flow, inner(flux_y, 1), 1)
    )


def edge_kernel(sat, mob, pore, qx, qy, qz, far_out, near_out, s, m, p, x, y, z, in_sem):
    first_core = lax.axis_index("c") == 0
    loads = []
    for j, start in enumerate((0, 5)):
        for k, (field, near) in enumerate(
            ((sat, s), (mob, m), (qx, x), (qy, y), (qz, z), (pore, p))
        ):
            part = pl.ds(start, 3)
            loads.append(
                pltpu.make_async_copy(field.at[part], near.at[part], in_sem.at[6 * j + k])
            )
    for load in loads:
        load.start()
    for load in loads:
        load.wait()
    f = [frac(s[i], m[i]) for i in range(3)]
    face_1 = across(x[1], f[0], f[1])
    flow_1 = frac(moved(s[1], p[1], across(x[2], f[1], f[2]) - face_1, f[1], z[1], y[1]), m[1])
    down = [field[0] for field in (s, m, p, z, y, x)]
    down += [face_1, jnp.minimum(x[1], 0.0) * flow_1]
    f = {i: frac(s[i], m[i]) for i in range(5, 8)}
    face_7 = across(x[7], f[6], f[7])
    flow_6 = frac(moved(s[6], p[6], face_7 - across(x[6], f[5], f[6]), f[6], z[6], y[6]), m[6])
    up = [field[7] for field in (s, m, p, z, y)]
    up += [face_7, jnp.maximum(x[7], 0.0) * flow_6, jnp.zeros_like(face_7)]
    for k in range(EDGE_ROWS):
        near_out[k] = jnp.where(first_core, up[k], down[k])
        far_out[k] = jnp.where(first_core, down[k], up[k])


OUTER = ((0, 7), (1, 6), (2, 5))
INNER = ((3, 4), (2, 5), (1, 6))


def one_hot(row_of, pairs, layers):
    lane = lax.broadcasted_iota(jnp.int32, row_of.shape, 1)
    hots = []
    for first, second in pairs:
        target = jnp.where(lane < layers, lane + first * layers, lane + (second - 1) * layers)
        hots.append(jnp.where(row_of == target, 1.0, 0.0).astype(jnp.bfloat16))
    return jnp.concatenate(hots, axis=1)


def rates_of(flows, hot, mask, weight):
    stack = jnp.concatenate(flows, axis=0)
    big = stack.astype(jnp.bfloat16)
    rest = stack - big.astype(jnp.float32)
    middle = rest.astype(jnp.bfloat16)
    small = (rest - middle.astype(jnp.float32)).astype(jnp.bfloat16)
    found = mask * sum(
        jnp.dot(hot[:, : stack.shape[0]], part, preferred_element_type=jnp.float32)
        for part in (small, middle, big)
    )
    picked = jnp.sum(found, axis=1, keepdims=True)
    return jnp.sum(weight * picked, axis=0, keepdims=True)


def inside_kernel(
    sat, mob, pore, qx, qy, qz, cell, well, factor, obs, after, other, mids, middle, early, hot, mask, weight
):
    rows, layers, columns = sat.shape
    count = cell.shape[1]

    def column_of(row):
        return jnp.concatenate(
            [
                jnp.transpose(jnp.broadcast_to(row[:, j : j + columns], (columns, columns)))
                for j in range(0, count, columns)
            ],
            axis=0,
        )

    cells = column_of(cell[...])
    row_of = lax.div(cells, columns)
    lane = lax.broadcasted_iota(jnp.int32, cells.shape, 1)
    mask[...] = jnp.where(cells - row_of * columns == lane, 1.0, 0.0)
    hot[...] = one_hot(row_of, OUTER, layers)
    near = one_hot(row_of, INNER, layers)
    weight[...] = jnp.where(column_of(well[...]) == lane, column_of(factor[...]), 0.0)

    f = [frac(sat[i], mob[i]) for i in range(rows)]
    face = {i: across(qx[i], f[i - 1], f[i]) for i in range(1, rows)}
    mids[0] = f[0]
    mids[1] = f[7]
    mids[2] = moved(sat[0], pore[0], face[1], f[0], qz[0], qy[0])
    mids[3] = moved(sat[7], pore[7], -face[7], f[7], qz[7], qy[7])
    s = {i: moved(sat[i], pore[i], face[i + 1] - face[i], f[i], qz[i], qy[i]) for i in range(1, 7)}
    f = {i: frac(s[i], mob[i]) for i in range(1, 7)}
    rates = [rates_of([f[i] for pair in INNER for i in pair], near, mask[...], weight[...])]
    face = {i: across(qx[i], f[i - 1], f[i]) for i in range(2, 7)}
    mids[4] = f[1]
    mids[5] = f[6]
    mids[6] = moved(s[1], pore[1], face[2], f[1], qz[1], qy[1])
    mids[7] = moved(s[6], pore[6], -face[6], f[6], qz[6], qy[6])
    s = {i: moved(s[i], pore[i], face[i + 1] - face[i], f[i], qz[i], qy[i]) for i in range(2, 6)}
    f = {i: frac(s[i], mob[i]) for i in range(2, 6)}
    rates.append(rates_of([f[i] for pair in INNER[:2] for i in pair], near, mask[...], weight[...]))
    face = {i: across(qx[i], f[i - 1], f[i]) for i in range(3, 6)}
    mids[8] = f[2]
    mids[9] = f[5]
    mids[10] = moved(s[2], pore[2], face[3], f[2], qz[2], qy[2])
    mids[11] = moved(s[5], pore[5], -face[5], f[5], qz[5], qy[5])
    last = [moved(s[i], pore[i], face[i + 1] - face[i], f[i], qz[i], qy[i]) for i in (3, 4)]
    for j in range(2):
        middle[j] = last[j]
    flows = [frac(last[j], mob[3 + j]) for j in range(2)]
    rates.append(rates_of(flows, near, mask[...], weight[...]))
    errors = jnp.concatenate(
        [obs[k : k + 1, :] for k in range(SUBSTEPS)]
        + [jnp.zeros((1, columns - SUBSTEPS * obs.shape[1]), jnp.float32)],
        axis=1,
    )
    early[...] = jnp.concatenate(rates + [errors], axis=0)


def outside_kernel(
    mob, pore, qx, qy, qz, far, near, mids, middle, early, hot, mask, weight, where, new_sat, shares
):
    tile = where[0]
    last = where[1]
    has_low = tile > 0
    has_high = tile < last
    first_core = where[4] == 0
    low = [jnp.where(first_core, far[k], near[k]) for k in range(EDGE_ROWS - 1)]
    high = [jnp.where(first_core, near[k], far[k]) for k in range(EDGE_ROWS)]
    below = jnp.where(has_low, low[0], 0.5)
    below_mob = jnp.where(has_low, low[1], 1.0)
    above = jnp.where(has_high, high[0], 0.5)
    above_mob = jnp.where(has_high, high[1], 1.0)
    x = {i: qx[i] for i in range(1, 8)}
    x[0] = jnp.where(has_low, qx[0], 0.0)
    x[8] = high[5]
    z = {i: qz[i] for i in (0, 1, 6, 7)}
    z[-1], z[8] = low[3], high[3]
    y = {i: qy[i] for i in (0, 1, 6, 7)}
    y[-1], y[8] = low[4], high[4]
    p = {i: pore[i] for i in (0, 1, 2, 5, 6, 7)}
    p[-1], p[8] = low[2], high[2]
    m = {i: mob[i] for i in (0, 1, 2, 5, 6, 7)}
    m[-1], m[8] = below_mob, above_mob

    f = {-1: frac(below, below_mob), 0: mids[0], 7: mids[1], 8: frac(above, above_mob)}
    out_low = jnp.minimum(low[5], 0.0) / f[-1]
    out_high = jnp.maximum(high[6], 0.0) / f[8]
    face = {i: across(x[i], f[i - 1], f[i]) for i in (0, 8)}
    s = {
        -1: moved(below, p[-1], face[0] - low[5], f[-1], z[-1], y[-1]),
        0: mids[2] + p[0] * face[0],
        7: mids[3] - p[7] * face[8],
        8: moved(above, p[8], high[6] - face[8], f[8], z[8], y[8]),
    }

    f = {i: frac(s[i], m[i]) for i in (-1, 0, 7, 8)}
    rates = [rates_of([f[0], f[7]], hot, mask[...], weight[...])]
    f[1], f[6] = mids[4], mids[5]
    face = {i: across(x[i], f[i - 1], f[i]) for i in (0, 1, 7, 8)}
    face[-1] = low[6] + out_low * f[-1]
    face[9] = out_high * f[8] + high[7]
    s = {i: moved(s[i], p[i], face[i + 1] - face[i], f[i], z[i], y[i]) for i in (-1, 0, 7, 8)}
    s[1] = mids[6] + p[1] * face[1]
    s[6] = mids[7] - p[6] * face[7]

    f = {i: frac(s[i], m[i]) for i in (-1, 0, 1, 6, 7, 8)}
    rates.append(rates_of([f[0], f[7], f[1], f[6]], hot, mask[...], weight[...]))
    f[2], f[5] = mids[8], mids[9]
    face = {i: across(x[i], f[i - 1], f[i]) for i in (0, 1, 2, 6, 7, 8)}
    s = {i: moved(s[i], p[i], face[i + 1] - face[i], f[i], z[i], y[i]) for i in (0, 1, 6, 7)}
    s[2] = mids[10] + p[2] * face[2]
    s[5] = mids[11] - p[5] * face[6]
    for i in (0, 1, 2, 5, 6, 7):
        new_sat[i] = s[i]
    for j in range(2):
        new_sat[3 + j] = middle[j]
    f = {i: frac(s[i], m[i]) for i in (0, 1, 2, 5, 6, 7)}
    rates.append(
        rates_of([f[i] for pair in OUTER for i in pair], hot, mask[...], weight[...])
    )
    zero = jnp.zeros_like(rates[0])
    share = early[...] + jnp.concatenate(rates + [zero], axis=0)
    share = jnp.concatenate([share, share], axis=0)
    for j in range(shares.shape[0] // 8):
        shares[8 * j : 8 * j + 8, :] = share


def line_kernel(parts, out):
    members, per = 8, 4
    width = SUBSTEPS + 1
    rows = []
    for k in range(SUBSTEPS):
        total = parts[pl.ds(k, members, stride=per * width), :]
        for j in range(1, per):
            total = total + parts[pl.ds(width * j + k, members, stride=per * width), :]
        rows.append(total)
    errors = [parts[width * j + SUBSTEPS : width * j + SUBSTEPS + 1, :] for j in range(per)]
    rows.append(jnp.concatenate(errors * 2, axis=0))
    for j in range(out.shape[0]):
        for k, row in enumerate(rows):
            out[j, members * k : members * (k + 1), :] = row


def gram_kernel(parts, where, rates_out, gram):
    tile = where[0]
    own_x = where[2]
    own_z = where[3]
    groups, per, layer = 4, 4, 8
    rows = SUBSTEPS * layer
    wells = parts.shape[2]
    mine = rates_out.shape[2]
    sums = []
    for g in range(groups):
        total = parts[g * per, :rows]
        for j in range(1, per):
            total = total + parts[g * per + j, :rows]
        sums.append(total)
    packed = jnp.concatenate([parts[y, rows : rows + per] for y in range(per)], axis=0)
    tiles = packed.shape[0]
    lane = lax.broadcasted_iota(jnp.int32, packed.shape, 1)
    home = lane // mine == lax.broadcasted_iota(jnp.int32, packed.shape, 0)
    errors = []
    for k in range(SUBSTEPS):
        front = packed if k == 0 else pltpu.roll(packed, wells - mine * k, 1)
        moved = pltpu.roll(front, 0, 1, stride=mine, stride_axis=0)
        errors.append(jnp.sum(jnp.where(home, moved, 0.0), axis=0, keepdims=True))
    ensemble = groups * layer
    own = sums[0]
    for g in range(1, groups):
        own = jnp.where(own_x == g, sums[g], own)
    mask_z = lax.broadcasted_iota(jnp.int32, (layer, wells), 0) == own_z
    own_rates = []
    own_centered = []
    centered = []
    for k in range(SUBSTEPS):
        part = slice(k * layer, (k + 1) * layer)
        data = [total[part] / errors[k] for total in sums]
        mean = jnp.sum(data[0] + data[1] + data[2] + data[3], axis=0, keepdims=True) / ensemble
        centered.append(jnp.concatenate([d - mean for d in data], axis=0))
        row = jnp.sum(jnp.where(mask_z, own[part], 0.0), axis=0, keepdims=True)
        own_rates.append(row)
        own_centered.append(row / errors[k] - mean)
    gram[...] = lax.dot_general(
        jnp.concatenate(own_centered, axis=1),
        jnp.concatenate(centered, axis=1),
        (((1,), (1,)), ((), ())),
        precision=HIGHEST,
        preferred_element_type=jnp.float32,
    ) / (ensemble - 1.0)
    select = (
        lax.broadcasted_iota(jnp.int32, (mine, wells), 1)
        == lax.broadcasted_iota(jnp.int32, (mine, wells), 0) + tile * mine
    ).astype(jnp.float32)
    chosen = lax.dot_general(
        jnp.concatenate(own_rates, axis=0), select, (((1,), (1,)), ((), ())), precision=HIGHEST,
        preferred_element_type=jnp.float32,
    )
    for k in range(SUBSTEPS):
        rates_out[k] = chosen[k : k + 1]


VMEM = pl.BlockSpec(memory_space=pltpu.VMEM)
ANY = pl.BlockSpec(memory_space=pl.ANY)
SMEM = pl.BlockSpec(memory_space=pltpu.SMEM)


def shape(*dims):
    return jax.ShapeDtypeStruct(dims, jnp.float32)


def held(*dims):
    return pltpu.VMEM(dims, jnp.float32)


def body(
    saturation,
    mobility,
    pore_scale,
    flux_x,
    flux_y,
    flux_z,
    conn_cell,
    conn_well,
    conn_factor,
    obs_error,
):
    rows, layers, columns = saturation.shape[1:]
    fields = [
        a.reshape(rows, layers, columns)
        for a in (saturation, mobility, pore_scale, flux_x, flux_y, flux_z)
    ]
    tiles = lax.axis_size(TILE)
    tile = lax.axis_index(TILE)
    where = jnp.stack(
        [
            tile,
            jnp.full_like(tile, tiles - 1),
            lax.axis_index("x"),
            lax.axis_index("zl"),
            lax.axis_index("c"),
        ]
    ).astype(jnp.int32)
    far_out, near_out = pl.pallas_call(
        edge_kernel,
        out_shape=(held(EDGE_ROWS, layers, columns),) * 2,
        in_specs=[ANY] * 6,
        out_specs=(VMEM, VMEM),
        scratch_shapes=[pltpu.VMEM((rows, layers, columns), jnp.float32)] * 6
        + [pltpu.SemaphoreType.DMA((12,))],
        name="edges",
    )(*fields)
    pairs = [(i, i + 1) for i in range(1, tiles - 1, 2)]
    near = lax.ppermute(near_out, TILE, [(i, i ^ 1) for i in range(tiles)])
    far = lax.ppermute(far_out, TILE, pairs + [(j, i) for i, j in pairs])
    wells = obs_error.shape[0] * tiles
    count = conn_cell.shape[0]
    sat, mob, pore, qx, qy, qz = fields
    mids, middle, early, hot, mask, weight = pl.pallas_call(
        inside_kernel,
        out_shape=(
            shape(12, layers, columns),
            shape(2, layers, columns),
            shape(SUBSTEPS + 1, wells),
            jax.ShapeDtypeStruct((count, 6 * layers), jnp.bfloat16),
            shape(count, columns),
            shape(count, wells),
        ),
        in_specs=[VMEM] * 10 + [ANY] * 2,
        out_specs=(VMEM,) * 6,
        compiler_params=pltpu.CompilerParams(vmem_limit_bytes=32 * 1024 * 1024),
        name="inside",
    )(
        *fields,
        conn_cell.reshape(1, count),
        conn_well.reshape(1, count),
        conn_factor.reshape(1, count),
        obs_error.T,
        far_out,
        near_out,
    )
    new_saturation, shares = pl.pallas_call(
        outside_kernel,
        out_shape=(held(rows, layers, columns), held(128, wells)),
        in_specs=[VMEM] * 13 + [SMEM],
        out_specs=(VMEM, VMEM),
        compiler_params=pltpu.CompilerParams(vmem_limit_bytes=32 * 1024 * 1024),
        name="outside",
    )(mob, pore, qx, qy, qz, far, near, mids, middle, early, hot, mask, weight, where)
    line = lax.all_to_all(shares.reshape(32, 4, wells), LINE, 0, 0)
    line = pltpu.with_memory_space_constraint(line.reshape(128, wells), pltpu.VMEM)
    (spreads,) = pl.pallas_call(
        line_kernel,
        out_shape=(held(16, 32, wells),),
        in_specs=[VMEM],
        out_specs=(VMEM,),
        name="line_sums",
    )(line)
    plane = pltpu.with_memory_space_constraint(lax.all_to_all(spreads, PLANE, 0, 0), pltpu.VMEM)
    rates, gram = pl.pallas_call(
        gram_kernel,
        out_shape=(shape(SUBSTEPS, 1, obs_error.shape[0]), shape(1, 32)),
        in_specs=[VMEM, SMEM],
        out_specs=(VMEM, VMEM),
        name="gram_row",
    )(plane, where)
    return (
        new_saturation.reshape(saturation.shape),
        jnp.transpose(rates, (1, 2, 0)),
        gram,
    )


def solution(mesh):
    split = Mesh(mesh.devices.reshape(SIZES), AXES)
    in_specs = (P(MEMBER, TILE, None, None),) * 6 + (P(TILE),) * 3 + (P(TILE, None),)
    out_specs = (P(MEMBER, TILE, None, None), P(MEMBER, TILE, None), P(MEMBER, None))
    return jax.shard_map(body, mesh=split, in_specs=in_specs, out_specs=out_specs, check_vma=False)
```

```python
import jax
import jax.numpy as jnp
from jax import lax
from jax.experimental import pallas as pl
from jax.experimental.pallas import tpu as pltpu
from jax.sharding import Mesh
from jax.sharding import PartitionSpec as P

SUBSTEPS = 3
AXES = ("x", "zl", "y", "zh", "c")
SIZES = (4, 8, 4, 2, 2)
MEMBER = ("x", "zl")
TILE = ("y", "zh", "c")
LINE = ("zl", "zh", "c")
PLANE = ("x", "y")
EDGE_ROWS = 7
HIGHEST = lax.Precision.HIGHEST


def frac(sat, mob):
    wet = sat * sat
    dry = (1.0 - sat) * (1.0 - sat)
    return wet / (wet + mob * dry)


def inner(flux, axis):
    return jnp.where(lax.broadcasted_iota(jnp.int32, flux.shape, axis) > 0, flux, 0.0)


def across(flux, below, here):
    return flux * jnp.where(flux > 0.0, below, here)


def spread(flow, flux, axis):
    face = across(flux, pltpu.roll(flow, 1, axis), flow)
    return pltpu.roll(face, flow.shape[axis] - 1, axis) - face


def moved(sat, pore, net, flow, flux_z, flux_y):
    return sat - pore * (
        net + spread(flow, inner(flux_z, 0), 0) + spread(flow, inner(flux_y, 1), 1)
    )


def edge_kernel(sat, mob, pore, qx, qy, qz, far_out, near_out, extra_out, s, m, p, x, y, z, in_sem):
    first_core = lax.axis_index("c") == 0
    loads = []
    for j, start in enumerate((0, 5)):
        for k, (field, near) in enumerate(
            ((sat, s), (mob, m), (qx, x), (qy, y), (qz, z), (pore, p))
        ):
            part = pl.ds(start, 3)
            loads.append(
                pltpu.make_async_copy(field.at[part], near.at[part], in_sem.at[6 * j + k])
            )
    for load in loads:
        load.start()
    for load in loads:
        load.wait()
    f = [frac(s[i], m[i]) for i in range(3)]
    face_1 = across(x[1], f[0], f[1])
    flow_1 = frac(moved(s[1], p[1], across(x[2], f[1], f[2]) - face_1, f[1], z[1], y[1]), m[1])
    down = [field[0] for field in (s, m, p, z, y)]
    down += [face_1, x[0]]
    f = {i: frac(s[i], m[i]) for i in range(5, 8)}
    face_7 = across(x[7], f[6], f[7])
    flow_6 = frac(moved(s[6], p[6], face_7 - across(x[6], f[5], f[6]), f[6], z[6], y[6]), m[6])
    up = [field[7] for field in (s, m, p, z, y)]
    up += [face_7, jnp.maximum(x[7], 0.0) * flow_6]
    for k in range(EDGE_ROWS):
        near_out[k] = jnp.where(first_core, up[k], down[k])
        far_out[k] = jnp.where(first_core, down[k], up[k])
    extra_out[0] = jnp.minimum(x[1], 0.0) * flow_1


OUTER = ((0, 7), (1, 6), (2, 5))
INNER = ((3, 4), (2, 5), (1, 6))


def one_hot(row_of, pairs, layers):
    lane = lax.broadcasted_iota(jnp.int32, row_of.shape, 1)
    hots = []
    for first, second in pairs:
        target = jnp.where(lane < layers, lane + first * layers, lane + (second - 1) * layers)
        hots.append(jnp.where(row_of == target, 1.0, 0.0).astype(jnp.bfloat16))
    return jnp.concatenate(hots, axis=1)


def rates_of(flows, hot, mask, weight):
    stack = jnp.concatenate(flows, axis=0)
    big = stack.astype(jnp.bfloat16)
    rest = stack - big.astype(jnp.float32)
    middle = rest.astype(jnp.bfloat16)
    small = (rest - middle.astype(jnp.float32)).astype(jnp.bfloat16)
    found = mask * sum(
        jnp.dot(hot[:, : stack.shape[0]], part, preferred_element_type=jnp.float32)
        for part in (small, middle, big)
    )
    picked = jnp.sum(found, axis=1, keepdims=True)
    return jnp.sum(weight * picked, axis=0, keepdims=True)


def inside_kernel(
    sat, mob, pore, qx, qy, qz, cell, well, factor, obs, after, other, third, mids, middle, early, hot, mask, weight
):
    rows, layers, columns = sat.shape
    count = cell.shape[1]

    def column_of(row):
        return jnp.concatenate(
            [
                jnp.transpose(jnp.broadcast_to(row[:, j : j + columns], (columns, columns)))
                for j in range(0, count, columns)
            ],
            axis=0,
        )

    cells = column_of(cell[...])
    row_of = lax.div(cells, columns)
    lane = lax.broadcasted_iota(jnp.int32, cells.shape, 1)
    mask[...] = jnp.where(cells - row_of * columns == lane, 1.0, 0.0)
    hot[...] = one_hot(row_of, OUTER, layers)
    near = one_hot(row_of, INNER, layers)
    weight[...] = jnp.where(column_of(well[...]) == lane, column_of(factor[...]), 0.0)

    f = [frac(sat[i], mob[i]) for i in range(rows)]
    face = {i: across(qx[i], f[i - 1], f[i]) for i in range(1, rows)}
    mids[0] = f[0]
    mids[1] = f[7]
    mids[2] = moved(sat[0], pore[0], face[1], f[0], qz[0], qy[0])
    mids[3] = moved(sat[7], pore[7], -face[7], f[7], qz[7], qy[7])
    s = {i: moved(sat[i], pore[i], face[i + 1] - face[i], f[i], qz[i], qy[i]) for i in range(1, 7)}
    f = {i: frac(s[i], mob[i]) for i in range(1, 7)}
    rates = [rates_of([f[i] for pair in INNER for i in pair], near, mask[...], weight[...])]
    face = {i: across(qx[i], f[i - 1], f[i]) for i in range(2, 7)}
    mids[4] = f[1]
    mids[5] = f[6]
    mids[6] = moved(s[1], pore[1], face[2], f[1], qz[1], qy[1])
    mids[7] = moved(s[6], pore[6], -face[6], f[6], qz[6], qy[6])
    s = {i: moved(s[i], pore[i], face[i + 1] - face[i], f[i], qz[i], qy[i]) for i in range(2, 6)}
    f = {i: frac(s[i], mob[i]) for i in range(2, 6)}
    rates.append(rates_of([f[i] for pair in INNER[:2] for i in pair], near, mask[...], weight[...]))
    face = {i: across(qx[i], f[i - 1], f[i]) for i in range(3, 6)}
    mids[8] = f[2]
    mids[9] = f[5]
    mids[10] = moved(s[2], pore[2], face[3], f[2], qz[2], qy[2])
    mids[11] = moved(s[5], pore[5], -face[5], f[5], qz[5], qy[5])
    last = [moved(s[i], pore[i], face[i + 1] - face[i], f[i], qz[i], qy[i]) for i in (3, 4)]
    for j in range(2):
        middle[j] = last[j]
    flows = [frac(last[j], mob[3 + j]) for j in range(2)]
    rates.append(rates_of(flows, near, mask[...], weight[...]))
    errors = jnp.concatenate(
        [obs[k : k + 1, :] for k in range(SUBSTEPS)]
        + [jnp.zeros((1, columns - SUBSTEPS * obs.shape[1]), jnp.float32)],
        axis=1,
    )
    early[...] = jnp.concatenate(rates + [errors], axis=0)


def outside_kernel(
    mob, pore, qx, qy, qz, far, near, extra, mids, middle, early, hot, mask, weight, where,
    new_sat, shares, last_term, sem,
):
    extra_copy = pltpu.make_async_copy(extra, last_term, sem)
    extra_copy.start()
    tile = where[0]
    last = where[1]
    has_low = tile > 0
    has_high = tile < last
    first_core = where[4] == 0
    low = [jnp.where(first_core, far[k], near[k]) for k in range(EDGE_ROWS)]
    high = [jnp.where(first_core, near[k], far[k]) for k in range(EDGE_ROWS)]
    below = jnp.where(has_low, low[0], 0.5)
    below_mob = jnp.where(has_low, low[1], 1.0)
    above = jnp.where(has_high, high[0], 0.5)
    above_mob = jnp.where(has_high, high[1], 1.0)
    x = {i: qx[i] for i in range(1, 8)}
    x[0] = jnp.where(has_low, qx[0], 0.0)
    x[8] = high[6]
    z = {i: qz[i] for i in (0, 1, 6, 7)}
    z[-1], z[8] = low[3], high[3]
    y = {i: qy[i] for i in (0, 1, 6, 7)}
    y[-1], y[8] = low[4], high[4]
    p = {i: pore[i] for i in (0, 1, 2, 5, 6, 7)}
    p[-1], p[8] = low[2], high[2]
    m = {i: mob[i] for i in (0, 1, 2, 5, 6, 7)}
    m[-1], m[8] = below_mob, above_mob

    f = {-1: frac(below, below_mob), 0: mids[0], 7: mids[1], 8: frac(above, above_mob)}
    out_low = jnp.minimum(low[5], 0.0) / f[-1]
    out_high = jnp.maximum(high[5], 0.0) / f[8]
    face = {i: across(x[i], f[i - 1], f[i]) for i in (0, 8)}
    s = {
        -1: moved(below, p[-1], face[0] - low[5], f[-1], z[-1], y[-1]),
        0: mids[2] + p[0] * face[0],
        7: mids[3] - p[7] * face[8],
        8: moved(above, p[8], high[5] - face[8], f[8], z[8], y[8]),
    }

    f = {i: frac(s[i], m[i]) for i in (-1, 0, 7, 8)}
    rates = [rates_of([f[0], f[7]], hot, mask[...], weight[...])]
    f[1], f[6] = mids[4], mids[5]
    face = {i: across(x[i], f[i - 1], f[i]) for i in (0, 1, 7, 8)}
    face[-1] = low[6] + out_low * f[-1]
    extra_copy.wait()
    face[9] = out_high * f[8] + last_term[0]
    s = {i: moved(s[i], p[i], face[i + 1] - face[i], f[i], z[i], y[i]) for i in (-1, 0, 7, 8)}
    s[1] = mids[6] + p[1] * face[1]
    s[6] = mids[7] - p[6] * face[7]

    f = {i: frac(s[i], m[i]) for i in (-1, 0, 1, 6, 7, 8)}
    rates.append(rates_of([f[0], f[7], f[1], f[6]], hot, mask[...], weight[...]))
    f[2], f[5] = mids[8], mids[9]
    face = {i: across(x[i], f[i - 1], f[i]) for i in (0, 1, 2, 6, 7, 8)}
    s = {i: moved(s[i], p[i], face[i + 1] - face[i], f[i], z[i], y[i]) for i in (0, 1, 6, 7)}
    s[2] = mids[10] + p[2] * face[2]
    s[5] = mids[11] - p[5] * face[6]
    for i in (0, 1, 2, 5, 6, 7):
        new_sat[i] = s[i]
    for j in range(2):
        new_sat[3 + j] = middle[j]
    f = {i: frac(s[i], m[i]) for i in (0, 1, 2, 5, 6, 7)}
    rates.append(
        rates_of([f[i] for pair in OUTER for i in pair], hot, mask[...], weight[...])
    )
    zero = jnp.zeros_like(rates[0])
    share = early[...] + jnp.concatenate(rates + [zero], axis=0)
    share = jnp.concatenate([share, share], axis=0)
    for j in range(shares.shape[0] // 8):
        shares[8 * j : 8 * j + 8, :] = share


def line_kernel(parts, out):
    members, per = 8, 4
    width = SUBSTEPS + 1
    rows = []
    for k in range(SUBSTEPS):
        total = parts[pl.ds(k, members, stride=per * width), :]
        for j in range(1, per):
            total = total + parts[pl.ds(width * j + k, members, stride=per * width), :]
        rows.append(total)
    errors = [parts[width * j + SUBSTEPS : width * j + SUBSTEPS + 1, :] for j in range(per)]
    rows.append(jnp.concatenate(errors * 2, axis=0))
    for j in range(out.shape[0]):
        for k, row in enumerate(rows):
            out[j, members * k : members * (k + 1), :] = row


def gram_kernel(parts, where, rates_out, gram):
    tile = where[0]
    own_x = where[2]
    own_z = where[3]
    groups, per, layer = 4, 4, 8
    rows = SUBSTEPS * layer
    wells = parts.shape[2]
    mine = rates_out.shape[2]
    sums = []
    for g in range(groups):
        total = parts[g * per, :rows]
        for j in range(1, per):
            total = total + parts[g * per + j, :rows]
        sums.append(total)
    packed = jnp.concatenate([parts[y, rows : rows + per] for y in range(per)], axis=0)
    tiles = packed.shape[0]
    lane = lax.broadcasted_iota(jnp.int32, packed.shape, 1)
    home = lane // mine == lax.broadcasted_iota(jnp.int32, packed.shape, 0)
    errors = []
    for k in range(SUBSTEPS):
        front = packed if k == 0 else pltpu.roll(packed, wells - mine * k, 1)
        moved = pltpu.roll(front, 0, 1, stride=mine, stride_axis=0)
        errors.append(jnp.sum(jnp.where(home, moved, 0.0), axis=0, keepdims=True))
    ensemble = groups * layer
    own = sums[0]
    for g in range(1, groups):
        own = jnp.where(own_x == g, sums[g], own)
    mask_z = lax.broadcasted_iota(jnp.int32, (layer, wells), 0) == own_z
    own_rates = []
    own_centered = []
    centered = []
    for k in range(SUBSTEPS):
        part = slice(k * layer, (k + 1) * layer)
        data = [total[part] / errors[k] for total in sums]
        mean = jnp.sum(data[0] + data[1] + data[2] + data[3], axis=0, keepdims=True) / ensemble
        centered.append(jnp.concatenate([d - mean for d in data], axis=0))
        row = jnp.sum(jnp.where(mask_z, own[part], 0.0), axis=0, keepdims=True)
        own_rates.append(row)
        own_centered.append(row / errors[k] - mean)
    gram[...] = lax.dot_general(
        jnp.concatenate(own_centered, axis=1),
        jnp.concatenate(centered, axis=1),
        (((1,), (1,)), ((), ())),
        precision=HIGHEST,
        preferred_element_type=jnp.float32,
    ) / (ensemble - 1.0)
    select = (
        lax.broadcasted_iota(jnp.int32, (mine, wells), 1)
        == lax.broadcasted_iota(jnp.int32, (mine, wells), 0) + tile * mine
    ).astype(jnp.float32)
    chosen = lax.dot_general(
        jnp.concatenate(own_rates, axis=0), select, (((1,), (1,)), ((), ())), precision=HIGHEST,
        preferred_element_type=jnp.float32,
    )
    for k in range(SUBSTEPS):
        rates_out[k] = chosen[k : k + 1]


VMEM = pl.BlockSpec(memory_space=pltpu.VMEM)
ANY = pl.BlockSpec(memory_space=pl.ANY)
HBM = pl.BlockSpec(memory_space=pltpu.HBM)
SMEM = pl.BlockSpec(memory_space=pltpu.SMEM)


def shape(*dims):
    return jax.ShapeDtypeStruct(dims, jnp.float32)


def held(*dims):
    return pltpu.VMEM(dims, jnp.float32)


def body(
    saturation,
    mobility,
    pore_scale,
    flux_x,
    flux_y,
    flux_z,
    conn_cell,
    conn_well,
    conn_factor,
    obs_error,
):
    rows, layers, columns = saturation.shape[1:]
    fields = [
        a.reshape(rows, layers, columns)
        for a in (saturation, mobility, pore_scale, flux_x, flux_y, flux_z)
    ]
    tiles = lax.axis_size(TILE)
    tile = lax.axis_index(TILE)
    where = jnp.stack(
        [
            tile,
            jnp.full_like(tile, tiles - 1),
            lax.axis_index("x"),
            lax.axis_index("zl"),
            lax.axis_index("c"),
        ]
    ).astype(jnp.int32)
    far_out, near_out, extra_out = pl.pallas_call(
        edge_kernel,
        out_shape=(
            held(EDGE_ROWS, layers, columns),
            held(EDGE_ROWS, layers, columns),
            held(1, layers, columns),
        ),
        in_specs=[ANY] * 6,
        out_specs=(VMEM,) * 3,
        scratch_shapes=[pltpu.VMEM((rows, layers, columns), jnp.float32)] * 6
        + [pltpu.SemaphoreType.DMA((12,))],
        name="edges",
    )(*fields)
    pairs = [(i, i + 1) for i in range(1, tiles - 1, 2)]
    far, near, extra = (
        lax.ppermute(rows_out, TILE, moves)
        for rows_out, moves in (
            (far_out, pairs + [(j, i) for i, j in pairs]),
            (near_out, [(i, i ^ 1) for i in range(tiles)]),
            (extra_out, [(i + 1, i) for i in range(tiles - 1)]),
        )
    )
    wells = obs_error.shape[0] * tiles
    count = conn_cell.shape[0]
    sat, mob, pore, qx, qy, qz = fields
    mids, middle, early, hot, mask, weight = pl.pallas_call(
        inside_kernel,
        out_shape=(
            shape(12, layers, columns),
            shape(2, layers, columns),
            shape(SUBSTEPS + 1, wells),
            jax.ShapeDtypeStruct((count, 6 * layers), jnp.bfloat16),
            shape(count, columns),
            shape(count, wells),
        ),
        in_specs=[VMEM] * 10 + [ANY] * 3,
        out_specs=(VMEM,) * 6,
        compiler_params=pltpu.CompilerParams(vmem_limit_bytes=32 * 1024 * 1024),
        name="inside",
    )(
        *fields,
        conn_cell.reshape(1, count),
        conn_well.reshape(1, count),
        conn_factor.reshape(1, count),
        obs_error.T,
        far_out,
        near_out,
        extra_out,
    )
    new_saturation, shares = pl.pallas_call(
        outside_kernel,
        out_shape=(held(rows, layers, columns), held(128, wells)),
        in_specs=[VMEM] * 7 + [HBM] + [VMEM] * 6 + [SMEM],
        out_specs=(VMEM, VMEM),
        scratch_shapes=[
            pltpu.VMEM((1, layers, columns), jnp.float32),
            pltpu.SemaphoreType.DMA,
        ],
        compiler_params=pltpu.CompilerParams(vmem_limit_bytes=32 * 1024 * 1024),
        name="outside",
    )(mob, pore, qx, qy, qz, far, near, extra, mids, middle, early, hot, mask, weight, where)
    line = lax.all_to_all(shares.reshape(32, 4, wells), LINE, 0, 0)
    line = pltpu.with_memory_space_constraint(line.reshape(128, wells), pltpu.VMEM)
    (spreads,) = pl.pallas_call(
        line_kernel,
        out_shape=(held(16, 32, wells),),
        in_specs=[VMEM],
        out_specs=(VMEM,),
        name="line_sums",
    )(line)
    plane = pltpu.with_memory_space_constraint(lax.all_to_all(spreads, PLANE, 0, 0), pltpu.VMEM)
    rates, gram = pl.pallas_call(
        gram_kernel,
        out_shape=(shape(SUBSTEPS, 1, obs_error.shape[0]), shape(1, 32)),
        in_specs=[VMEM, SMEM],
        out_specs=(VMEM, VMEM),
        name="gram_row",
    )(plane, where)
    return (
        new_saturation.reshape(saturation.shape),
        jnp.transpose(rates, (1, 2, 0)),
        gram,
    )


def solution(mesh):
    split = Mesh(mesh.devices.reshape(SIZES), AXES)
    in_specs = (P(MEMBER, TILE, None, None),) * 6 + (P(TILE),) * 3 + (P(TILE, None),)
    out_specs = (P(MEMBER, TILE, None, None), P(MEMBER, TILE, None), P(MEMBER, None))
    return jax.shard_map(body, mesh=split, in_specs=in_specs, out_specs=out_specs, check_vma=False)
```

```python
import jax
import jax.numpy as jnp
from jax import lax
from jax.experimental import pallas as pl
from jax.experimental.pallas import tpu as pltpu
from jax.sharding import Mesh
from jax.sharding import PartitionSpec as P

SUBSTEPS = 3
AXES = ("x", "zl", "y", "zh", "c")
SIZES = (4, 8, 4, 2, 2)
MEMBER = ("x", "zl")
TILE = ("y", "zh", "c")
LINE = ("zl", "zh", "c")
PLANE = ("x", "y")
UP_ROWS = 7
DOWN_ROWS = 8
HIGHEST = lax.Precision.HIGHEST


def frac(sat, mob):
    wet = sat * sat
    dry = (1.0 - sat) * (1.0 - sat)
    return wet / (wet + mob * dry)


def inner(flux, axis):
    return jnp.where(lax.broadcasted_iota(jnp.int32, flux.shape, axis) > 0, flux, 0.0)


def across(flux, below, here):
    return flux * jnp.where(flux > 0.0, below, here)


def spread(flow, flux, axis):
    face = across(flux, pltpu.roll(flow, 1, axis), flow)
    return pltpu.roll(face, flow.shape[axis] - 1, axis) - face


def moved(sat, pore, net, flow, flux_z, flux_y):
    return sat - pore * (
        net + spread(flow, inner(flux_z, 0), 0) + spread(flow, inner(flux_y, 1), 1)
    )


def edge_kernel(sat, mob, pore, qx, qy, qz, up, down, s, m, p, x, y, z, in_sem):
    loads = []
    for j, start in enumerate((0, 5)):
        for k, (field, near) in enumerate(
            ((sat, s), (mob, m), (qx, x), (qy, y), (qz, z), (pore, p))
        ):
            part = pl.ds(start, 3)
            loads.append(
                pltpu.make_async_copy(field.at[part], near.at[part], in_sem.at[6 * j + k])
            )
    for load in loads:
        load.start()
    for load in loads:
        load.wait()
    f = [frac(s[i], m[i]) for i in range(3)]
    face_1 = across(x[1], f[0], f[1])
    flow_1 = frac(moved(s[1], p[1], across(x[2], f[1], f[2]) - face_1, f[1], z[1], y[1]), m[1])
    for k, near in enumerate((s, m, p, z, y, x)):
        down[k] = near[0]
    down[6] = face_1
    down[7] = jnp.minimum(x[1], 0.0) * flow_1
    f = {i: frac(s[i], m[i]) for i in range(5, 8)}
    face_7 = across(x[7], f[6], f[7])
    flow_6 = frac(moved(s[6], p[6], face_7 - across(x[6], f[5], f[6]), f[6], z[6], y[6]), m[6])
    for k, near in enumerate((s, m, p, z, y)):
        up[k] = near[7]
    up[5] = face_7
    up[6] = jnp.maximum(x[7], 0.0) * flow_6


OUTER = ((0, 7), (1, 6), (2, 5))
INNER = ((3, 4), (2, 5), (1, 6))


def one_hot(row_of, pairs, layers):
    lane = lax.broadcasted_iota(jnp.int32, row_of.shape, 1)
    hots = []
    for first, second in pairs:
        target = jnp.where(lane < layers, lane + first * layers, lane + (second - 1) * layers)
        hots.append(jnp.where(row_of == target, 1.0, 0.0).astype(jnp.bfloat16))
    return jnp.concatenate(hots, axis=1)


def rates_of(flows, hot, mask, weight):
    stack = jnp.concatenate(flows, axis=0)
    big = stack.astype(jnp.bfloat16)
    rest = stack - big.astype(jnp.float32)
    middle = rest.astype(jnp.bfloat16)
    small = (rest - middle.astype(jnp.float32)).astype(jnp.bfloat16)
    found = mask * sum(
        jnp.dot(hot[:, : stack.shape[0]], part, preferred_element_type=jnp.float32)
        for part in (small, middle, big)
    )
    picked = jnp.sum(found, axis=1, keepdims=True)
    return jnp.sum(weight * picked, axis=0, keepdims=True)


def inside_kernel(
    sat, mob, pore, qx, qy, qz, cell, well, factor, obs, after, mids, middle, early, hot, mask, weight
):
    rows, layers, columns = sat.shape
    count = cell.shape[1]

    def column_of(row):
        return jnp.concatenate(
            [
                jnp.transpose(jnp.broadcast_to(row[:, j : j + columns], (columns, columns)))
                for j in range(0, count, columns)
            ],
            axis=0,
        )

    cells = column_of(cell[...])
    row_of = lax.div(cells, columns)
    lane = lax.broadcasted_iota(jnp.int32, cells.shape, 1)
    mask[...] = jnp.where(cells - row_of * columns == lane, 1.0, 0.0)
    hot[...] = one_hot(row_of, OUTER, layers)
    near = one_hot(row_of, INNER, layers)
    weight[...] = jnp.where(column_of(well[...]) == lane, column_of(factor[...]), 0.0)

    f = [frac(sat[i], mob[i]) for i in range(rows)]
    face = {i: across(qx[i], f[i - 1], f[i]) for i in range(1, rows)}
    mids[0] = f[0]
    mids[1] = f[7]
    mids[2] = moved(sat[0], pore[0], face[1], f[0], qz[0], qy[0])
    mids[3] = moved(sat[7], pore[7], -face[7], f[7], qz[7], qy[7])
    s = {i: moved(sat[i], pore[i], face[i + 1] - face[i], f[i], qz[i], qy[i]) for i in range(1, 7)}
    f = {i: frac(s[i], mob[i]) for i in range(1, 7)}
    rates = [rates_of([f[i] for pair in INNER for i in pair], near, mask[...], weight[...])]
    face = {i: across(qx[i], f[i - 1], f[i]) for i in range(2, 7)}
    mids[4] = f[1]
    mids[5] = f[6]
    mids[6] = moved(s[1], pore[1], face[2], f[1], qz[1], qy[1])
    mids[7] = moved(s[6], pore[6], -face[6], f[6], qz[6], qy[6])
    s = {i: moved(s[i], pore[i], face[i + 1] - face[i], f[i], qz[i], qy[i]) for i in range(2, 6)}
    f = {i: frac(s[i], mob[i]) for i in range(2, 6)}
    rates.append(rates_of([f[i] for pair in INNER[:2] for i in pair], near, mask[...], weight[...]))
    face = {i: across(qx[i], f[i - 1], f[i]) for i in range(3, 6)}
    mids[8] = f[2]
    mids[9] = f[5]
    mids[10] = moved(s[2], pore[2], face[3], f[2], qz[2], qy[2])
    mids[11] = moved(s[5], pore[5], -face[5], f[5], qz[5], qy[5])
    last = [moved(s[i], pore[i], face[i + 1] - face[i], f[i], qz[i], qy[i]) for i in (3, 4)]
    for j in range(2):
        middle[j] = last[j]
    flows = [frac(last[j], mob[3 + j]) for j in range(2)]
    rates.append(rates_of(flows, near, mask[...], weight[...]))
    errors = jnp.concatenate(
        [obs[k : k + 1, :] for k in range(SUBSTEPS)]
        + [jnp.zeros((1, columns - SUBSTEPS * obs.shape[1]), jnp.float32)],
        axis=1,
    )
    early[...] = jnp.concatenate(rates + [errors], axis=0)


def outside_kernel(
    mob, pore, qx, qy, qz, low, high, mids, middle, early, hot, mask, weight, where, new_sat, shares
):
    tile = where[0]
    last = where[1]
    has_low = tile > 0
    has_high = tile < last
    below = jnp.where(has_low, low[0], 0.5)
    below_mob = jnp.where(has_low, low[1], 1.0)
    above = jnp.where(has_high, high[0], 0.5)
    above_mob = jnp.where(has_high, high[1], 1.0)
    x = {i: qx[i] for i in range(1, 8)}
    x[0] = jnp.where(has_low, qx[0], 0.0)
    x[8] = high[5]
    z = {i: qz[i] for i in (0, 1, 6, 7)}
    z[-1], z[8] = low[3], high[3]
    y = {i: qy[i] for i in (0, 1, 6, 7)}
    y[-1], y[8] = low[4], high[4]
    p = {i: pore[i] for i in (0, 1, 2, 5, 6, 7)}
    p[-1], p[8] = low[2], high[2]
    m = {i: mob[i] for i in (0, 1, 2, 5, 6, 7)}
    m[-1], m[8] = below_mob, above_mob

    f = {-1: frac(below, below_mob), 0: mids[0], 7: mids[1], 8: frac(above, above_mob)}
    out_low = jnp.minimum(low[5], 0.0) / f[-1]
    out_high = jnp.maximum(high[6], 0.0) / f[8]
    face = {i: across(x[i], f[i - 1], f[i]) for i in (0, 8)}
    s = {
        -1: moved(below, p[-1], face[0] - low[5], f[-1], z[-1], y[-1]),
        0: mids[2] + p[0] * face[0],
        7: mids[3] - p[7] * face[8],
        8: moved(above, p[8], high[6] - face[8], f[8], z[8], y[8]),
    }

    f = {i: frac(s[i], m[i]) for i in (-1, 0, 7, 8)}
    rates = [rates_of([f[0], f[7]], hot, mask[...], weight[...])]
    f[1], f[6] = mids[4], mids[5]
    face = {i: across(x[i], f[i - 1], f[i]) for i in (0, 1, 7, 8)}
    face[-1] = low[6] + out_low * f[-1]
    face[9] = out_high * f[8] + high[7]
    s = {i: moved(s[i], p[i], face[i + 1] - face[i], f[i], z[i], y[i]) for i in (-1, 0, 7, 8)}
    s[1] = mids[6] + p[1] * face[1]
    s[6] = mids[7] - p[6] * face[7]

    f = {i: frac(s[i], m[i]) for i in (-1, 0, 1, 6, 7, 8)}
    rates.append(rates_of([f[0], f[7], f[1], f[6]], hot, mask[...], weight[...]))
    f[2], f[5] = mids[8], mids[9]
    face = {i: across(x[i], f[i - 1], f[i]) for i in (0, 1, 2, 6, 7, 8)}
    s = {i: moved(s[i], p[i], face[i + 1] - face[i], f[i], z[i], y[i]) for i in (0, 1, 6, 7)}
    s[2] = mids[10] + p[2] * face[2]
    s[5] = mids[11] - p[5] * face[6]
    for i in (0, 1, 2, 5, 6, 7):
        new_sat[i] = s[i]
    for j in range(2):
        new_sat[3 + j] = middle[j]
    f = {i: frac(s[i], m[i]) for i in (0, 1, 2, 5, 6, 7)}
    rates.append(
        rates_of([f[i] for pair in OUTER for i in pair], hot, mask[...], weight[...])
    )
    zero = jnp.zeros_like(rates[0])
    share = early[...] + jnp.concatenate(rates + [zero], axis=0)
    share = jnp.concatenate([share, share], axis=0)
    for j in range(shares.shape[0] // 8):
        shares[8 * j : 8 * j + 8, :] = share


def line_kernel(parts, out):
    members, per = 8, 4
    width = SUBSTEPS + 1
    rows = []
    for k in range(SUBSTEPS):
        total = parts[pl.ds(k, members, stride=per * width), :]
        for j in range(1, per):
            total = total + parts[pl.ds(width * j + k, members, stride=per * width), :]
        rows.append(total)
    errors = [parts[width * j + SUBSTEPS : width * j + SUBSTEPS + 1, :] for j in range(per)]
    rows.append(jnp.concatenate(errors * 2, axis=0))
    for j in range(out.shape[0]):
        for k, row in enumerate(rows):
            out[j, members * k : members * (k + 1), :] = row


def gram_kernel(parts, where, rates_out, gram):
    tile = where[0]
    own_x = where[2]
    own_z = where[3]
    groups, per, layer = 4, 4, 8
    rows = SUBSTEPS * layer
    wells = parts.shape[2]
    mine = rates_out.shape[2]
    sums = []
    for g in range(groups):
        total = parts[g * per, :rows]
        for j in range(1, per):
            total = total + parts[g * per + j, :rows]
        sums.append(total)
    packed = jnp.concatenate([parts[y, rows : rows + per] for y in range(per)], axis=0)
    tiles = packed.shape[0]
    lane = lax.broadcasted_iota(jnp.int32, packed.shape, 1)
    home = lane // mine == lax.broadcasted_iota(jnp.int32, packed.shape, 0)
    errors = []
    for k in range(SUBSTEPS):
        front = packed if k == 0 else pltpu.roll(packed, wells - mine * k, 1)
        moved = pltpu.roll(front, 0, 1, stride=mine, stride_axis=0)
        errors.append(jnp.sum(jnp.where(home, moved, 0.0), axis=0, keepdims=True))
    ensemble = groups * layer
    own = sums[0]
    for g in range(1, groups):
        own = jnp.where(own_x == g, sums[g], own)
    mask_z = lax.broadcasted_iota(jnp.int32, (layer, wells), 0) == own_z
    own_rates = []
    own_centered = []
    centered = []
    for k in range(SUBSTEPS):
        part = slice(k * layer, (k + 1) * layer)
        data = [total[part] / errors[k] for total in sums]
        mean = jnp.sum(data[0] + data[1] + data[2] + data[3], axis=0, keepdims=True) / ensemble
        centered.append(jnp.concatenate([d - mean for d in data], axis=0))
        row = jnp.sum(jnp.where(mask_z, own[part], 0.0), axis=0, keepdims=True)
        own_rates.append(row)
        own_centered.append(row / errors[k] - mean)
    gram[...] = lax.dot_general(
        jnp.concatenate(own_centered, axis=1),
        jnp.concatenate(centered, axis=1),
        (((1,), (1,)), ((), ())),
        precision=HIGHEST,
        preferred_element_type=jnp.float32,
    ) / (ensemble - 1.0)
    select = (
        lax.broadcasted_iota(jnp.int32, (mine, wells), 1)
        == lax.broadcasted_iota(jnp.int32, (mine, wells), 0) + tile * mine
    ).astype(jnp.float32)
    chosen = lax.dot_general(
        jnp.concatenate(own_rates, axis=0), select, (((1,), (1,)), ((), ())), precision=HIGHEST,
        preferred_element_type=jnp.float32,
    )
    for k in range(SUBSTEPS):
        rates_out[k] = chosen[k : k + 1]


VMEM = pl.BlockSpec(memory_space=pltpu.VMEM)
ANY = pl.BlockSpec(memory_space=pl.ANY)
SMEM = pl.BlockSpec(memory_space=pltpu.SMEM)


def shape(*dims):
    return jax.ShapeDtypeStruct(dims, jnp.float32)


def held(*dims):
    return pltpu.VMEM(dims, jnp.float32)


def body(
    saturation,
    mobility,
    pore_scale,
    flux_x,
    flux_y,
    flux_z,
    conn_cell,
    conn_well,
    conn_factor,
    obs_error,
):
    rows, layers, columns = saturation.shape[1:]
    fields = [
        a.reshape(rows, layers, columns)
        for a in (saturation, mobility, pore_scale, flux_x, flux_y, flux_z)
    ]
    tiles = lax.axis_size(TILE)
    tile = lax.axis_index(TILE)
    where = jnp.stack(
        [tile, jnp.full_like(tile, tiles - 1), lax.axis_index("x"), lax.axis_index("zl")]
    ).astype(jnp.int32)
    up, down = pl.pallas_call(
        edge_kernel,
        out_shape=(held(UP_ROWS, layers, columns), held(DOWN_ROWS, layers, columns)),
        in_specs=[ANY] * 6,
        out_specs=(VMEM, VMEM),
        scratch_shapes=[pltpu.VMEM((rows, layers, columns), jnp.float32)] * 6
        + [pltpu.SemaphoreType.DMA((12,))],
        name="edges",
    )(*fields)
    low = lax.ppermute(up, TILE, [(i, i + 1) for i in range(tiles - 1)])
    high = lax.ppermute(down, TILE, [(i + 1, i) for i in range(tiles - 1)])
    wells = obs_error.shape[0] * tiles
    count = conn_cell.shape[0]
    sat, mob, pore, qx, qy, qz = fields
    mids, middle, early, hot, mask, weight = pl.pallas_call(
        inside_kernel,
        out_shape=(
            shape(12, layers, columns),
            shape(2, layers, columns),
            shape(SUBSTEPS + 1, wells),
            jax.ShapeDtypeStruct((count, 6 * layers), jnp.bfloat16),
            shape(count, columns),
            shape(count, wells),
        ),
        in_specs=[VMEM] * 10 + [ANY],
        out_specs=(VMEM,) * 6,
        compiler_params=pltpu.CompilerParams(vmem_limit_bytes=32 * 1024 * 1024),
        name="inside",
    )(
        *fields,
        conn_cell.reshape(1, count),
        conn_well.reshape(1, count),
        conn_factor.reshape(1, count),
        obs_error.T,
        up,
    )
    new_saturation, shares = pl.pallas_call(
        outside_kernel,
        out_shape=(held(rows, layers, columns), held(128, wells)),
        in_specs=[VMEM] * 13 + [SMEM],
        out_specs=(VMEM, VMEM),
        compiler_params=pltpu.CompilerParams(vmem_limit_bytes=32 * 1024 * 1024),
        name="outside",
    )(mob, pore, qx, qy, qz, low, high, mids, middle, early, hot, mask, weight, where)
    line = lax.all_to_all(shares.reshape(32, 4, wells), LINE, 0, 0)
    line = pltpu.with_memory_space_constraint(line.reshape(128, wells), pltpu.VMEM)
    (spreads,) = pl.pallas_call(
        line_kernel,
        out_shape=(held(16, 32, wells),),
        in_specs=[VMEM],
        out_specs=(VMEM,),
        name="line_sums",
    )(line)
    plane = pltpu.with_memory_space_constraint(lax.all_to_all(spreads, PLANE, 0, 0), pltpu.VMEM)
    rates, gram = pl.pallas_call(
        gram_kernel,
        out_shape=(shape(SUBSTEPS, 1, obs_error.shape[0]), shape(1, 32)),
        in_specs=[VMEM, SMEM],
        out_specs=(VMEM, VMEM),
        name="gram_row",
    )(plane, where)
    return (
        new_saturation.reshape(saturation.shape),
        jnp.transpose(rates, (1, 2, 0)),
        gram,
    )


def solution(mesh):
    split = Mesh(mesh.devices.reshape(SIZES), AXES)
    in_specs = (P(MEMBER, TILE, None, None),) * 6 + (P(TILE),) * 3 + (P(TILE, None),)
    out_specs = (P(MEMBER, TILE, None, None), P(MEMBER, TILE, None), P(MEMBER, None))
    return jax.shard_map(body, mesh=split, in_specs=in_specs, out_specs=out_specs, check_vma=False)
```

```python
import jax
import jax.numpy as jnp
from jax import lax
from jax.experimental import pallas as pl
from jax.experimental.pallas import tpu as pltpu
from jax.sharding import Mesh
from jax.sharding import PartitionSpec as P

SUBSTEPS = 3
AXES = ("x", "zl", "y", "zh", "c")
SIZES = (4, 8, 4, 2, 2)
MEMBER = ("x", "zl")
TILE = ("y", "zh", "c")
LINE = ("zl", "zh", "c")
PLANE = ("x", "y")
UP_ROWS = 7
DOWN_ROWS = 8
HIGHEST = lax.Precision.HIGHEST


def frac(sat, mob):
    wet = sat * sat
    dry = (1.0 - sat) * (1.0 - sat)
    return wet / (wet + mob * dry)


def inner(flux, axis):
    return jnp.where(lax.broadcasted_iota(jnp.int32, flux.shape, axis) > 0, flux, 0.0)


def across(flux, below, here):
    return flux * jnp.where(flux > 0.0, below, here)


def spread(flow, flux, axis):
    face = across(flux, pltpu.roll(flow, 1, axis), flow)
    return pltpu.roll(face, flow.shape[axis] - 1, axis) - face


def moved(sat, pore, net, flow, flux_z, flux_y):
    return sat - pore * (
        net + spread(flow, inner(flux_z, 0), 0) + spread(flow, inner(flux_y, 1), 1)
    )


def edge_kernel(sat, mob, pore, qx, qy, qz, up, down, s, m, p, x, y, z, sem):
    pieces = ((0, 3), (5, 3), (3, 2))
    loads = []
    for j, (start, size) in enumerate(pieces):
        for k, (field, near) in enumerate(
            ((sat, s), (mob, m), (qx, x), (qy, y), (qz, z), (pore, p))
        ):
            part = pl.ds(start, size)
            loads.append(pltpu.make_async_copy(field.at[part], near.at[part], sem.at[6 * j + k]))
    for load in loads:
        load.start()
    for load in loads[:12]:
        load.wait()
    f = [frac(s[i], m[i]) for i in range(3)]
    face_1 = across(x[1], f[0], f[1])
    flow_1 = frac(moved(s[1], p[1], across(x[2], f[1], f[2]) - face_1, f[1], z[1], y[1]), m[1])
    for k, near in enumerate((s, m, p, z, y, x)):
        down[k] = near[0]
    down[6] = face_1
    down[7] = jnp.minimum(x[1], 0.0) * flow_1
    f = {i: frac(s[i], m[i]) for i in range(5, 8)}
    face_7 = across(x[7], f[6], f[7])
    flow_6 = frac(moved(s[6], p[6], face_7 - across(x[6], f[5], f[6]), f[6], z[6], y[6]), m[6])
    for k, near in enumerate((s, m, p, z, y)):
        up[k] = near[7]
    up[5] = face_7
    up[6] = jnp.maximum(x[7], 0.0) * flow_6
    for load in loads[12:]:
        load.wait()


OUTER = ((0, 7), (1, 6), (2, 5))
INNER = ((3, 4), (2, 5), (1, 6))


def one_hot(row_of, pairs, layers):
    lane = lax.broadcasted_iota(jnp.int32, row_of.shape, 1)
    hots = []
    for first, second in pairs:
        target = jnp.where(lane < layers, lane + first * layers, lane + (second - 1) * layers)
        hots.append(jnp.where(row_of == target, 1.0, 0.0).astype(jnp.bfloat16))
    return jnp.concatenate(hots, axis=1)


def rates_of(flows, hot, mask, weight):
    stack = jnp.concatenate(flows, axis=0)
    big = stack.astype(jnp.bfloat16)
    rest = stack - big.astype(jnp.float32)
    small = rest.astype(jnp.bfloat16)
    found = mask * sum(
        jnp.dot(hot[:, : stack.shape[0]], part, preferred_element_type=jnp.float32)
        for part in (small, big)
    )
    picked = jnp.sum(found, axis=1, keepdims=True)
    return jnp.sum(weight * picked, axis=0, keepdims=True)


def inside_kernel(
    sat, mob, pore, qx, qy, qz, cell, well, factor, obs, after, mids, middle, early, hot, mask, weight
):
    rows, layers, columns = sat.shape
    count = cell.shape[1]

    def column_of(row):
        return jnp.concatenate(
            [
                jnp.transpose(jnp.broadcast_to(row[:, j : j + columns], (columns, columns)))
                for j in range(0, count, columns)
            ],
            axis=0,
        )

    cells = column_of(cell[...])
    row_of = lax.div(cells, columns)
    lane = lax.broadcasted_iota(jnp.int32, cells.shape, 1)
    mask[...] = jnp.where(cells - row_of * columns == lane, 1.0, 0.0)
    hot[...] = one_hot(row_of, OUTER, layers)
    near = one_hot(row_of, INNER, layers)
    weight[...] = jnp.where(column_of(well[...]) == lane, column_of(factor[...]), 0.0)

    f = [frac(sat[i], mob[i]) for i in range(rows)]
    face = {i: across(qx[i], f[i - 1], f[i]) for i in range(1, rows)}
    mids[0] = f[0]
    mids[1] = f[7]
    mids[2] = moved(sat[0], pore[0], face[1], f[0], qz[0], qy[0])
    mids[3] = moved(sat[7], pore[7], -face[7], f[7], qz[7], qy[7])
    s = {i: moved(sat[i], pore[i], face[i + 1] - face[i], f[i], qz[i], qy[i]) for i in range(1, 7)}
    f = {i: frac(s[i], mob[i]) for i in range(1, 7)}
    rates = [rates_of([f[i] for pair in INNER for i in pair], near, mask[...], weight[...])]
    face = {i: across(qx[i], f[i - 1], f[i]) for i in range(2, 7)}
    mids[4] = f[1]
    mids[5] = f[6]
    mids[6] = moved(s[1], pore[1], face[2], f[1], qz[1], qy[1])
    mids[7] = moved(s[6], pore[6], -face[6], f[6], qz[6], qy[6])
    s = {i: moved(s[i], pore[i], face[i + 1] - face[i], f[i], qz[i], qy[i]) for i in range(2, 6)}
    f = {i: frac(s[i], mob[i]) for i in range(2, 6)}
    rates.append(rates_of([f[i] for pair in INNER[:2] for i in pair], near, mask[...], weight[...]))
    face = {i: across(qx[i], f[i - 1], f[i]) for i in range(3, 6)}
    mids[8] = f[2]
    mids[9] = f[5]
    mids[10] = moved(s[2], pore[2], face[3], f[2], qz[2], qy[2])
    mids[11] = moved(s[5], pore[5], -face[5], f[5], qz[5], qy[5])
    last = [moved(s[i], pore[i], face[i + 1] - face[i], f[i], qz[i], qy[i]) for i in (3, 4)]
    for j in range(2):
        middle[j] = last[j]
    flows = [frac(last[j], mob[3 + j]) for j in range(2)]
    rates.append(rates_of(flows, near, mask[...], weight[...]))
    errors = jnp.concatenate(
        [obs[k : k + 1, :] for k in range(SUBSTEPS)]
        + [jnp.zeros((1, columns - SUBSTEPS * obs.shape[1]), jnp.float32)],
        axis=1,
    )
    early[...] = jnp.concatenate(rates + [errors], axis=0)


def outside_kernel(
    mob, pore, qx, qy, qz, low, high, mids, middle, early, hot, mask, weight, where, new_sat, shares
):
    tile = where[0]
    last = where[1]
    has_low = tile > 0
    has_high = tile < last
    below = jnp.where(has_low, low[0], 0.5)
    below_mob = jnp.where(has_low, low[1], 1.0)
    above = jnp.where(has_high, high[0], 0.5)
    above_mob = jnp.where(has_high, high[1], 1.0)
    x = {i: qx[i] for i in range(1, 8)}
    x[0] = jnp.where(has_low, qx[0], 0.0)
    x[8] = high[5]
    z = {i: qz[i] for i in (0, 1, 6, 7)}
    z[-1], z[8] = low[3], high[3]
    y = {i: qy[i] for i in (0, 1, 6, 7)}
    y[-1], y[8] = low[4], high[4]
    p = {i: pore[i] for i in (0, 1, 2, 5, 6, 7)}
    p[-1], p[8] = low[2], high[2]
    m = {i: mob[i] for i in (0, 1, 2, 5, 6, 7)}
    m[-1], m[8] = below_mob, above_mob

    f = {-1: frac(below, below_mob), 0: mids[0], 7: mids[1], 8: frac(above, above_mob)}
    out_low = jnp.minimum(low[5], 0.0) / f[-1]
    out_high = jnp.maximum(high[6], 0.0) / f[8]
    face = {i: across(x[i], f[i - 1], f[i]) for i in (0, 8)}
    s = {
        -1: moved(below, p[-1], face[0] - low[5], f[-1], z[-1], y[-1]),
        0: mids[2] + p[0] * face[0],
        7: mids[3] - p[7] * face[8],
        8: moved(above, p[8], high[6] - face[8], f[8], z[8], y[8]),
    }

    f = {i: frac(s[i], m[i]) for i in (-1, 0, 7, 8)}
    rates = [rates_of([f[0], f[7]], hot, mask[...], weight[...])]
    f[1], f[6] = mids[4], mids[5]
    face = {i: across(x[i], f[i - 1], f[i]) for i in (0, 1, 7, 8)}
    face[-1] = low[6] + out_low * f[-1]
    face[9] = out_high * f[8] + high[7]
    s = {i: moved(s[i], p[i], face[i + 1] - face[i], f[i], z[i], y[i]) for i in (-1, 0, 7, 8)}
    s[1] = mids[6] + p[1] * face[1]
    s[6] = mids[7] - p[6] * face[7]

    f = {i: frac(s[i], m[i]) for i in (-1, 0, 1, 6, 7, 8)}
    rates.append(rates_of([f[0], f[7], f[1], f[6]], hot, mask[...], weight[...]))
    f[2], f[5] = mids[8], mids[9]
    face = {i: across(x[i], f[i - 1], f[i]) for i in (0, 1, 2, 6, 7, 8)}
    s = {i: moved(s[i], p[i], face[i + 1] - face[i], f[i], z[i], y[i]) for i in (0, 1, 6, 7)}
    s[2] = mids[10] + p[2] * face[2]
    s[5] = mids[11] - p[5] * face[6]
    for i in (0, 1, 2, 5, 6, 7):
        new_sat[i] = s[i]
    for j in range(2):
        new_sat[3 + j] = middle[j]
    f = {i: frac(s[i], m[i]) for i in (0, 1, 2, 5, 6, 7)}
    rates.append(
        rates_of([f[i] for pair in OUTER for i in pair], hot, mask[...], weight[...])
    )
    zero = jnp.zeros_like(rates[0])
    share = early[...] + jnp.concatenate(rates + [zero], axis=0)
    share = jnp.concatenate([share, share], axis=0)
    for j in range(shares.shape[0] // 8):
        shares[8 * j : 8 * j + 8, :] = share


def line_kernel(parts, out):
    members, per = 8, 4
    width = SUBSTEPS + 1
    rows = []
    for k in range(SUBSTEPS):
        total = parts[pl.ds(k, members, stride=per * width), :]
        for j in range(1, per):
            total = total + parts[pl.ds(width * j + k, members, stride=per * width), :]
        rows.append(total)
    errors = [parts[width * j + SUBSTEPS : width * j + SUBSTEPS + 1, :] for j in range(per)]
    rows.append(jnp.concatenate(errors * 2, axis=0))
    for j in range(out.shape[0]):
        for k, row in enumerate(rows):
            out[j, members * k : members * (k + 1), :] = row


def gram_kernel(parts, where, rates_out, gram):
    tile = where[0]
    own_x = where[2]
    own_z = where[3]
    groups, per, layer = 4, 4, 8
    rows = SUBSTEPS * layer
    wells = parts.shape[2]
    mine = rates_out.shape[2]
    sums = []
    for g in range(groups):
        total = parts[g * per, :rows]
        for j in range(1, per):
            total = total + parts[g * per + j, :rows]
        sums.append(total)
    packed = jnp.concatenate([parts[y, rows : rows + per] for y in range(per)], axis=0)
    tiles = packed.shape[0]
    lane = lax.broadcasted_iota(jnp.int32, packed.shape, 1)
    home = lane // mine == lax.broadcasted_iota(jnp.int32, packed.shape, 0)
    errors = []
    for k in range(SUBSTEPS):
        front = packed if k == 0 else pltpu.roll(packed, wells - mine * k, 1)
        moved = pltpu.roll(front, 0, 1, stride=mine, stride_axis=0)
        errors.append(jnp.sum(jnp.where(home, moved, 0.0), axis=0, keepdims=True))
    ensemble = groups * layer
    own = sums[0]
    for g in range(1, groups):
        own = jnp.where(own_x == g, sums[g], own)
    lane = lax.broadcasted_iota(jnp.int32, (layer, wells), 1)
    sublane = lax.broadcasted_iota(jnp.int32, (layer, wells), 0)
    products = [jnp.zeros((layer, wells), jnp.float32)] * groups
    own_rates = []
    for k in range(SUBSTEPS):
        part = slice(k * layer, (k + 1) * layer)
        data = [total[part] / errors[k] for total in sums]
        mean = jnp.sum(data[0] + data[1] + data[2] + data[3], axis=0, keepdims=True) / ensemble
        row = jnp.sum(jnp.where(sublane == own_z, own[part], 0.0), axis=0, keepdims=True)
        own_rates.append(row)
        centered = row / errors[k] - mean
        products = [total + (d - mean) * centered for total, d in zip(products, data)]
    line = jnp.zeros((layer, wells), jnp.float32)
    for g in range(groups):
        dots = jnp.sum(products[g], axis=1, keepdims=True)
        line = line + jnp.where(lane == sublane + g * layer, dots, 0.0)
    line = jnp.sum(line, axis=0, keepdims=True) / (ensemble - 1.0)
    gram[...] = line[:, :ensemble]
    front = jnp.concatenate(own_rates + [jnp.zeros((layer - SUBSTEPS, wells), jnp.float32)], axis=0)
    front = pltpu.roll(front, lax.rem(wells - tile * mine, wells), 1)
    for k in range(SUBSTEPS):
        rates_out[k] = front[k : k + 1, :mine]


VMEM = pl.BlockSpec(memory_space=pltpu.VMEM)
ANY = pl.BlockSpec(memory_space=pl.ANY)
SMEM = pl.BlockSpec(memory_space=pltpu.SMEM)


def shape(*dims):
    return jax.ShapeDtypeStruct(dims, jnp.float32)


def held(*dims):
    return pltpu.VMEM(dims, jnp.float32)


def body(
    saturation,
    mobility,
    pore_scale,
    flux_x,
    flux_y,
    flux_z,
    conn_cell,
    conn_well,
    conn_factor,
    obs_error,
):
    rows, layers, columns = saturation.shape[1:]
    fields = [
        a.reshape(rows, layers, columns)
        for a in (saturation, mobility, pore_scale, flux_x, flux_y, flux_z)
    ]
    tiles = lax.axis_size(TILE)
    tile = lax.axis_index(TILE)
    where = jnp.stack(
        [tile, jnp.full_like(tile, tiles - 1), lax.axis_index("x"), lax.axis_index("zl")]
    ).astype(jnp.int32)
    up, down, *fields = pl.pallas_call(
        edge_kernel,
        out_shape=(held(UP_ROWS, layers, columns), held(DOWN_ROWS, layers, columns))
        + (held(rows, layers, columns),) * 6,
        in_specs=[ANY] * 6,
        out_specs=(VMEM,) * 8,
        scratch_shapes=[pltpu.SemaphoreType.DMA((18,))],
        name="edges",
    )(*fields)
    low = lax.ppermute(up, TILE, [(i, i + 1) for i in range(tiles - 1)])
    high = lax.ppermute(down, TILE, [(i + 1, i) for i in range(tiles - 1)])
    wells = obs_error.shape[0] * tiles
    count = conn_cell.shape[0]
    sat, mob, pore, qx, qy, qz = fields
    mids, middle, early, hot, mask, weight = pl.pallas_call(
        inside_kernel,
        out_shape=(
            shape(12, layers, columns),
            shape(2, layers, columns),
            shape(SUBSTEPS + 1, wells),
            jax.ShapeDtypeStruct((count, 6 * layers), jnp.bfloat16),
            shape(count, columns),
            shape(count, wells),
        ),
        in_specs=[VMEM] * 10 + [ANY],
        out_specs=(VMEM,) * 6,
        compiler_params=pltpu.CompilerParams(vmem_limit_bytes=32 * 1024 * 1024),
        name="inside",
    )(
        *fields,
        conn_cell.reshape(1, count),
        conn_well.reshape(1, count),
        conn_factor.reshape(1, count),
        obs_error.T,
        up,
    )
    new_saturation, shares = pl.pallas_call(
        outside_kernel,
        out_shape=(held(rows, layers, columns), held(128, wells)),
        in_specs=[VMEM] * 13 + [SMEM],
        out_specs=(VMEM, VMEM),
        compiler_params=pltpu.CompilerParams(vmem_limit_bytes=32 * 1024 * 1024),
        name="outside",
    )(mob, pore, qx, qy, qz, low, high, mids, middle, early, hot, mask, weight, where)
    line = lax.all_to_all(shares.reshape(32, 4, wells), LINE, 0, 0)
    line = pltpu.with_memory_space_constraint(line.reshape(128, wells), pltpu.VMEM)
    (spreads,) = pl.pallas_call(
        line_kernel,
        out_shape=(held(16, 32, wells),),
        in_specs=[VMEM],
        out_specs=(VMEM,),
        name="line_sums",
    )(line)
    plane = pltpu.with_memory_space_constraint(lax.all_to_all(spreads, PLANE, 0, 0), pltpu.VMEM)
    rates, gram = pl.pallas_call(
        gram_kernel,
        out_shape=(shape(SUBSTEPS, 1, obs_error.shape[0]), shape(1, 32)),
        in_specs=[VMEM, SMEM],
        out_specs=(VMEM, VMEM),
        name="gram_row",
    )(plane, where)
    return (
        new_saturation.reshape(saturation.shape),
        jnp.transpose(rates, (1, 2, 0)),
        gram,
    )


def solution(mesh):
    split = Mesh(mesh.devices.reshape(SIZES), AXES)
    in_specs = (P(MEMBER, TILE, None, None),) * 6 + (P(TILE),) * 3 + (P(TILE, None),)
    out_specs = (P(MEMBER, TILE, None, None), P(MEMBER, TILE, None), P(MEMBER, None))
    return jax.shard_map(body, mesh=split, in_specs=in_specs, out_specs=out_specs, check_vma=False)
```

```python
import jax
import jax.numpy as jnp
from jax import lax
from jax.experimental import pallas as pl
from jax.experimental.pallas import tpu as pltpu
from jax.sharding import Mesh
from jax.sharding import PartitionSpec as P

SUBSTEPS = 3
AXES = ("x", "zl", "y", "zh", "c")
SIZES = (4, 8, 4, 2, 2)
MEMBER = ("x", "zl")
TILE = ("y", "zh", "c")
LINE = ("zl", "zh", "c")
PLANE = ("x", "y")
UP_ROWS = 7
DOWN_ROWS = 8
HIGHEST = lax.Precision.HIGHEST


def frac(sat, mob):
    wet = sat * sat
    dry = (1.0 - sat) * (1.0 - sat)
    return wet / (wet + mob * dry)


def inner(flux, axis):
    return jnp.where(lax.broadcasted_iota(jnp.int32, flux.shape, axis) > 0, flux, 0.0)


def across(flux, below, here):
    return flux * jnp.where(flux > 0.0, below, here)


def spread(flow, flux, axis):
    face = across(flux, pltpu.roll(flow, 1, axis), flow)
    return pltpu.roll(face, flow.shape[axis] - 1, axis) - face


def moved(sat, pore, net, flow, flux_z, flux_y):
    return sat - pore * (
        net + spread(flow, inner(flux_z, 0), 0) + spread(flow, inner(flux_y, 1), 1)
    )


def edge_kernel(sat, mob, pore, qx, qy, qz, up, down, s, m, p, x, y, z, sem):
    fields = ((sat, s), (mob, m), (qx, x), (qy, y), (qz, z), (pore, p))
    wide, narrow = (0, 1, 2, 5, 6, 7), (0, 1, 6, 7)
    needed = (wide, wide, (0, 1, 2, 6, 7), narrow, narrow, narrow)
    loads = []
    rest = []
    for (field, near), rows in zip(fields, needed):
        for row in rows:
            index = len(loads)
            loads.append(pltpu.make_async_copy(field.at[row], near.at[row], sem.at[index]))
    for (field, near), rows in zip(fields, needed):
        index = len(loads) + len(rest)
        start = rows[len(rows) // 2 - 1] + 1 if len(rows) % 2 == 0 else rows[2] + 1
        part = pl.ds(start, 8 - len(rows))
        rest.append(pltpu.make_async_copy(field.at[part], near.at[part], sem.at[index]))
    for load in loads + rest:
        load.start()
    for load in loads:
        load.wait()
    f = [frac(s[i], m[i]) for i in range(3)]
    face_1 = across(x[1], f[0], f[1])
    flow_1 = frac(moved(s[1], p[1], across(x[2], f[1], f[2]) - face_1, f[1], z[1], y[1]), m[1])
    for k, near in enumerate((s, m, p, z, y, x)):
        down[k] = near[0]
    down[6] = face_1
    down[7] = jnp.minimum(x[1], 0.0) * flow_1
    f = {i: frac(s[i], m[i]) for i in range(5, 8)}
    face_7 = across(x[7], f[6], f[7])
    flow_6 = frac(moved(s[6], p[6], face_7 - across(x[6], f[5], f[6]), f[6], z[6], y[6]), m[6])
    for k, near in enumerate((s, m, p, z, y)):
        up[k] = near[7]
    up[5] = face_7
    up[6] = jnp.maximum(x[7], 0.0) * flow_6
    for load in rest:
        load.wait()


OUTER = ((0, 7), (1, 6), (2, 5))
INNER = ((3, 4), (2, 5), (1, 6))


def one_hot(row_of, pairs, layers):
    lane = lax.broadcasted_iota(jnp.int32, row_of.shape, 1)
    hots = []
    for first, second in pairs:
        target = jnp.where(lane < layers, lane + first * layers, lane + (second - 1) * layers)
        hots.append(jnp.where(row_of == target, 1.0, 0.0).astype(jnp.bfloat16))
    return jnp.concatenate(hots, axis=1)


def rates_of(flows, hot, mask, weight):
    stack = jnp.concatenate(flows, axis=0)
    big = stack.astype(jnp.bfloat16)
    rest = stack - big.astype(jnp.float32)
    small = rest.astype(jnp.bfloat16)
    found = mask * sum(
        jnp.dot(hot[:, : stack.shape[0]], part, preferred_element_type=jnp.float32)
        for part in (small, big)
    )
    picked = jnp.sum(found, axis=1, keepdims=True)
    return jnp.sum(weight * picked, axis=0, keepdims=True)


def inside_kernel(
    sat, mob, pore, qx, qy, qz, cell, well, factor, obs, after, mids, middle, early, hot, mask, weight
):
    rows, layers, columns = sat.shape
    count = cell.shape[1]

    def column_of(row):
        return jnp.concatenate(
            [
                jnp.transpose(jnp.broadcast_to(row[:, j : j + columns], (columns, columns)))
                for j in range(0, count, columns)
            ],
            axis=0,
        )

    cells = column_of(cell[...])
    row_of = lax.div(cells, columns)
    lane = lax.broadcasted_iota(jnp.int32, cells.shape, 1)
    mask[...] = jnp.where(cells - row_of * columns == lane, 1.0, 0.0)
    hot[...] = one_hot(row_of, OUTER, layers)
    near = one_hot(row_of, INNER, layers)
    weight[...] = jnp.where(column_of(well[...]) == lane, column_of(factor[...]), 0.0)

    f = [frac(sat[i], mob[i]) for i in range(rows)]
    face = {i: across(qx[i], f[i - 1], f[i]) for i in range(1, rows)}
    mids[0] = f[0]
    mids[1] = f[7]
    mids[2] = moved(sat[0], pore[0], face[1], f[0], qz[0], qy[0])
    mids[3] = moved(sat[7], pore[7], -face[7], f[7], qz[7], qy[7])
    s = {i: moved(sat[i], pore[i], face[i + 1] - face[i], f[i], qz[i], qy[i]) for i in range(1, 7)}
    f = {i: frac(s[i], mob[i]) for i in range(1, 7)}
    rates = [rates_of([f[i] for pair in INNER for i in pair], near, mask[...], weight[...])]
    face = {i: across(qx[i], f[i - 1], f[i]) for i in range(2, 7)}
    mids[4] = f[1]
    mids[5] = f[6]
    mids[6] = moved(s[1], pore[1], face[2], f[1], qz[1], qy[1])
    mids[7] = moved(s[6], pore[6], -face[6], f[6], qz[6], qy[6])
    s = {i: moved(s[i], pore[i], face[i + 1] - face[i], f[i], qz[i], qy[i]) for i in range(2, 6)}
    f = {i: frac(s[i], mob[i]) for i in range(2, 6)}
    rates.append(rates_of([f[i] for pair in INNER[:2] for i in pair], near, mask[...], weight[...]))
    face = {i: across(qx[i], f[i - 1], f[i]) for i in range(3, 6)}
    mids[8] = f[2]
    mids[9] = f[5]
    mids[10] = moved(s[2], pore[2], face[3], f[2], qz[2], qy[2])
    mids[11] = moved(s[5], pore[5], -face[5], f[5], qz[5], qy[5])
    last = [moved(s[i], pore[i], face[i + 1] - face[i], f[i], qz[i], qy[i]) for i in (3, 4)]
    for j in range(2):
        middle[j] = last[j]
    flows = [frac(last[j], mob[3 + j]) for j in range(2)]
    rates.append(rates_of(flows, near, mask[...], weight[...]))
    errors = jnp.concatenate(
        [obs[k : k + 1, :] for k in range(SUBSTEPS)]
        + [jnp.zeros((1, columns - SUBSTEPS * obs.shape[1]), jnp.float32)],
        axis=1,
    )
    early[...] = jnp.concatenate(rates + [errors], axis=0)


def outside_kernel(
    mob, pore, qx, qy, qz, low, high, mids, middle, early, hot, mask, weight, where, new_sat, shares
):
    tile = where[0]
    last = where[1]
    has_low = tile > 0
    has_high = tile < last
    below = jnp.where(has_low, low[0], 0.5)
    below_mob = jnp.where(has_low, low[1], 1.0)
    above = jnp.where(has_high, high[0], 0.5)
    above_mob = jnp.where(has_high, high[1], 1.0)
    x = {i: qx[i] for i in range(1, 8)}
    x[0] = jnp.where(has_low, qx[0], 0.0)
    x[8] = high[5]
    z = {i: qz[i] for i in (0, 1, 6, 7)}
    z[-1], z[8] = low[3], high[3]
    y = {i: qy[i] for i in (0, 1, 6, 7)}
    y[-1], y[8] = low[4], high[4]
    p = {i: pore[i] for i in (0, 1, 2, 5, 6, 7)}
    p[-1], p[8] = low[2], high[2]
    m = {i: mob[i] for i in (0, 1, 2, 5, 6, 7)}
    m[-1], m[8] = below_mob, above_mob

    f = {-1: frac(below, below_mob), 0: mids[0], 7: mids[1], 8: frac(above, above_mob)}
    out_low = jnp.minimum(low[5], 0.0) / f[-1]
    out_high = jnp.maximum(high[6], 0.0) / f[8]
    face = {i: across(x[i], f[i - 1], f[i]) for i in (0, 8)}
    s = {
        -1: moved(below, p[-1], face[0] - low[5], f[-1], z[-1], y[-1]),
        0: mids[2] + p[0] * face[0],
        7: mids[3] - p[7] * face[8],
        8: moved(above, p[8], high[6] - face[8], f[8], z[8], y[8]),
    }

    f = {i: frac(s[i], m[i]) for i in (-1, 0, 7, 8)}
    rates = [rates_of([f[0], f[7]], hot, mask[...], weight[...])]
    f[1], f[6] = mids[4], mids[5]
    face = {i: across(x[i], f[i - 1], f[i]) for i in (0, 1, 7, 8)}
    face[-1] = low[6] + out_low * f[-1]
    face[9] = out_high * f[8] + high[7]
    s = {i: moved(s[i], p[i], face[i + 1] - face[i], f[i], z[i], y[i]) for i in (-1, 0, 7, 8)}
    s[1] = mids[6] + p[1] * face[1]
    s[6] = mids[7] - p[6] * face[7]

    f = {i: frac(s[i], m[i]) for i in (-1, 0, 1, 6, 7, 8)}
    rates.append(rates_of([f[0], f[7], f[1], f[6]], hot, mask[...], weight[...]))
    f[2], f[5] = mids[8], mids[9]
    face = {i: across(x[i], f[i - 1], f[i]) for i in (0, 1, 2, 6, 7, 8)}
    s = {i: moved(s[i], p[i], face[i + 1] - face[i], f[i], z[i], y[i]) for i in (0, 1, 6, 7)}
    s[2] = mids[10] + p[2] * face[2]
    s[5] = mids[11] - p[5] * face[6]
    for i in (0, 1, 2, 5, 6, 7):
        new_sat[i] = s[i]
    for j in range(2):
        new_sat[3 + j] = middle[j]
    f = {i: frac(s[i], m[i]) for i in (0, 1, 2, 5, 6, 7)}
    rates.append(
        rates_of([f[i] for pair in OUTER for i in pair], hot, mask[...], weight[...])
    )
    zero = jnp.zeros_like(rates[0])
    share = early[...] + jnp.concatenate(rates + [zero], axis=0)
    share = jnp.concatenate([share, share], axis=0)
    for j in range(shares.shape[0] // 8):
        shares[8 * j : 8 * j + 8, :] = share


def line_kernel(parts, out):
    members, per = 8, 4
    width = SUBSTEPS + 1
    rows = []
    for k in range(SUBSTEPS):
        total = parts[pl.ds(k, members, stride=per * width), :]
        for j in range(1, per):
            total = total + parts[pl.ds(width * j + k, members, stride=per * width), :]
        rows.append(total)
    errors = [parts[width * j + SUBSTEPS : width * j + SUBSTEPS + 1, :] for j in range(per)]
    rows.append(jnp.concatenate(errors, axis=0))
    block = jnp.concatenate(rows, axis=0)
    size = block.shape[0]
    for j in range(out.shape[0] // size):
        out[size * j : size * (j + 1), :] = block


def gram_kernel(parts, where, rates_out, gram):
    tile = where[0]
    own_x = where[2]
    own_z = where[3]
    groups, per, layer = 4, 4, 8
    rows = SUBSTEPS * layer
    wells = parts.shape[1]
    mine = rates_out.shape[2]
    size = rows + per
    sums = []
    for g in range(groups):
        starts = [(g * per + j) * size for j in range(per)]
        total = parts[starts[0] : starts[0] + rows]
        for start in starts[1:]:
            total = total + parts[start : start + rows]
        sums.append(total)
    packed = jnp.concatenate(
        [parts[y * size + rows : (y + 1) * size] for y in range(per)], axis=0
    )
    tiles = packed.shape[0]
    lane = lax.broadcasted_iota(jnp.int32, packed.shape, 1)
    home = lane // mine == lax.broadcasted_iota(jnp.int32, packed.shape, 0)
    errors = []
    for k in range(SUBSTEPS):
        front = packed if k == 0 else pltpu.roll(packed, wells - mine * k, 1)
        moved = pltpu.roll(front, 0, 1, stride=mine, stride_axis=0)
        errors.append(jnp.sum(jnp.where(home, moved, 0.0), axis=0, keepdims=True))
    ensemble = groups * layer
    own = sums[0]
    for g in range(1, groups):
        own = jnp.where(own_x == g, sums[g], own)
    lane = lax.broadcasted_iota(jnp.int32, (layer, wells), 1)
    sublane = lax.broadcasted_iota(jnp.int32, (layer, wells), 0)
    products = [jnp.zeros((layer, wells), jnp.float32)] * groups
    own_rates = []
    for k in range(SUBSTEPS):
        part = slice(k * layer, (k + 1) * layer)
        data = [total[part] / errors[k] for total in sums]
        mean = jnp.sum(data[0] + data[1] + data[2] + data[3], axis=0, keepdims=True) / ensemble
        row = jnp.sum(jnp.where(sublane == own_z, own[part], 0.0), axis=0, keepdims=True)
        own_rates.append(row)
        centered = row / errors[k] - mean
        products = [total + (d - mean) * centered for total, d in zip(products, data)]
    line = jnp.zeros((layer, wells), jnp.float32)
    for g in range(groups):
        dots = jnp.sum(products[g], axis=1, keepdims=True)
        line = line + jnp.where(lane == sublane + g * layer, dots, 0.0)
    line = jnp.sum(line, axis=0, keepdims=True) / (ensemble - 1.0)
    gram[...] = line[:, :ensemble]
    front = jnp.concatenate(own_rates + [jnp.zeros((layer - SUBSTEPS, wells), jnp.float32)], axis=0)
    front = pltpu.roll(front, lax.rem(wells - tile * mine, wells), 1)
    for k in range(SUBSTEPS):
        rates_out[k] = front[k : k + 1, :mine]


VMEM = pl.BlockSpec(memory_space=pltpu.VMEM)
ANY = pl.BlockSpec(memory_space=pl.ANY)
SMEM = pl.BlockSpec(memory_space=pltpu.SMEM)


def shape(*dims):
    return jax.ShapeDtypeStruct(dims, jnp.float32)


def held(*dims):
    return pltpu.VMEM(dims, jnp.float32)


def body(
    saturation,
    mobility,
    pore_scale,
    flux_x,
    flux_y,
    flux_z,
    conn_cell,
    conn_well,
    conn_factor,
    obs_error,
):
    rows, layers, columns = saturation.shape[1:]
    fields = [
        a.reshape(rows, layers, columns)
        for a in (saturation, mobility, pore_scale, flux_x, flux_y, flux_z)
    ]
    tiles = lax.axis_size(TILE)
    tile = lax.axis_index(TILE)
    where = jnp.stack(
        [tile, jnp.full_like(tile, tiles - 1), lax.axis_index("x"), lax.axis_index("zl")]
    ).astype(jnp.int32)
    up, down, *fields = pl.pallas_call(
        edge_kernel,
        out_shape=(held(UP_ROWS, layers, columns), held(DOWN_ROWS, layers, columns))
        + (held(rows, layers, columns),) * 6,
        in_specs=[ANY] * 6,
        out_specs=(VMEM,) * 8,
        scratch_shapes=[pltpu.SemaphoreType.DMA((35,))],
        name="edges",
    )(*fields)
    low = lax.ppermute(up, TILE, [(i, i + 1) for i in range(tiles - 1)])
    high = lax.ppermute(down, TILE, [(i + 1, i) for i in range(tiles - 1)])
    wells = obs_error.shape[0] * tiles
    count = conn_cell.shape[0]
    sat, mob, pore, qx, qy, qz = fields
    mids, middle, early, hot, mask, weight = pl.pallas_call(
        inside_kernel,
        out_shape=(
            shape(12, layers, columns),
            shape(2, layers, columns),
            shape(SUBSTEPS + 1, wells),
            jax.ShapeDtypeStruct((count, 6 * layers), jnp.bfloat16),
            shape(count, columns),
            shape(count, wells),
        ),
        in_specs=[VMEM] * 10 + [ANY],
        out_specs=(VMEM,) * 6,
        compiler_params=pltpu.CompilerParams(vmem_limit_bytes=32 * 1024 * 1024),
        name="inside",
    )(
        *fields,
        conn_cell.reshape(1, count),
        conn_well.reshape(1, count),
        conn_factor.reshape(1, count),
        obs_error.T,
        up,
    )
    new_saturation, shares = pl.pallas_call(
        outside_kernel,
        out_shape=(held(rows, layers, columns), held(128, wells)),
        in_specs=[VMEM] * 13 + [SMEM],
        out_specs=(VMEM, VMEM),
        compiler_params=pltpu.CompilerParams(vmem_limit_bytes=32 * 1024 * 1024),
        name="outside",
    )(mob, pore, qx, qy, qz, low, high, mids, middle, early, hot, mask, weight, where)
    line = lax.all_to_all(shares.reshape(32, 4, wells), LINE, 0, 0)
    line = pltpu.with_memory_space_constraint(line.reshape(128, wells), pltpu.VMEM)
    (spreads,) = pl.pallas_call(
        line_kernel,
        out_shape=(held(16 * 28, wells),),
        in_specs=[VMEM],
        out_specs=(VMEM,),
        name="line_sums",
    )(line)
    plane = lax.all_to_all(spreads.reshape(16, 7, 4, wells), PLANE, 0, 0)
    plane = pltpu.with_memory_space_constraint(plane.reshape(16 * 28, wells), pltpu.VMEM)
    rates, gram = pl.pallas_call(
        gram_kernel,
        out_shape=(shape(SUBSTEPS, 1, obs_error.shape[0]), shape(1, 32)),
        in_specs=[VMEM, SMEM],
        out_specs=(VMEM, VMEM),
        name="gram_row",
    )(plane, where)
    return (
        new_saturation.reshape(saturation.shape),
        jnp.transpose(rates, (1, 2, 0)),
        gram,
    )


def solution(mesh):
    split = Mesh(mesh.devices.reshape(SIZES), AXES)
    in_specs = (P(MEMBER, TILE, None, None),) * 6 + (P(TILE),) * 3 + (P(TILE, None),)
    out_specs = (P(MEMBER, TILE, None, None), P(MEMBER, TILE, None), P(MEMBER, None))
    return jax.shard_map(body, mesh=split, in_specs=in_specs, out_specs=out_specs, check_vma=False)
```

```python
import jax
import jax.numpy as jnp
from jax import lax
from jax.experimental import pallas as pl
from jax.experimental.pallas import tpu as pltpu
from jax.sharding import Mesh
from jax.sharding import PartitionSpec as P

SUBSTEPS = 3
WELLS_DEV = 8
AXES = ("x", "zl", "y", "zh", "c")
SIZES = (4, 8, 4, 2, 2)
MEMBER = ("x", "zl")
TILE = ("y", "zh", "c")
PLANE = ("x", "y", "c")
LINE = ("zl", "zh")
UP_ROWS = 7
DOWN_ROWS = 8
HIGHEST = lax.Precision.HIGHEST


def frac(sat, mob):
    wet = sat * sat
    dry = (1.0 - sat) * (1.0 - sat)
    return wet / (wet + mob * dry)


def inner(flux, axis):
    return jnp.where(lax.broadcasted_iota(jnp.int32, flux.shape, axis) > 0, flux, 0.0)


def across(flux, below, here):
    return flux * jnp.where(flux > 0.0, below, here)


def spread(flow, flux, axis):
    face = across(flux, pltpu.roll(flow, 1, axis), flow)
    return pltpu.roll(face, flow.shape[axis] - 1, axis) - face


def moved(sat, pore, net, flow, flux_z, flux_y):
    return sat - pore * (
        net + spread(flow, inner(flux_z, 0), 0) + spread(flow, inner(flux_y, 1), 1)
    )


def edge_kernel(sat, mob, pore, qx, qy, qz, up, down, s, m, p, x, y, z, sem):
    pieces = ((0, 3), (5, 3), (3, 2))
    loads = []
    for j, (start, size) in enumerate(pieces):
        for k, (field, near) in enumerate(
            ((sat, s), (mob, m), (qx, x), (qy, y), (qz, z), (pore, p))
        ):
            part = pl.ds(start, size)
            loads.append(pltpu.make_async_copy(field.at[part], near.at[part], sem.at[6 * j + k]))
    for load in loads:
        load.start()
    for load in loads[:12]:
        load.wait()
    f = [frac(s[i], m[i]) for i in range(3)]
    face_1 = across(x[1], f[0], f[1])
    flow_1 = frac(moved(s[1], p[1], across(x[2], f[1], f[2]) - face_1, f[1], z[1], y[1]), m[1])
    for k, near in enumerate((s, m, p, z, y, x)):
        down[k] = near[0]
    down[6] = face_1
    down[7] = jnp.minimum(x[1], 0.0) * flow_1
    f = {i: frac(s[i], m[i]) for i in range(5, 8)}
    face_7 = across(x[7], f[6], f[7])
    flow_6 = frac(moved(s[6], p[6], face_7 - across(x[6], f[5], f[6]), f[6], z[6], y[6]), m[6])
    for k, near in enumerate((s, m, p, z, y)):
        up[k] = near[7]
    up[5] = face_7
    up[6] = jnp.maximum(x[7], 0.0) * flow_6
    for load in loads[12:]:
        load.wait()


OUTER = ((0, 7), (1, 6), (2, 5))
INNER = ((3, 4), (2, 5), (1, 6))


def one_hot(row_of, pairs, layers):
    lane = lax.broadcasted_iota(jnp.int32, row_of.shape, 1)
    hots = []
    for first, second in pairs:
        target = jnp.where(lane < layers, lane + first * layers, lane + (second - 1) * layers)
        hots.append(jnp.where(row_of == target, 1.0, 0.0).astype(jnp.bfloat16))
    return jnp.concatenate(hots, axis=1)


def rates_of(flows, hot, mask, weight):
    stack = jnp.concatenate(flows, axis=0)
    big = stack.astype(jnp.bfloat16)
    rest = stack - big.astype(jnp.float32)
    small = rest.astype(jnp.bfloat16)
    found = mask * sum(
        jnp.dot(hot[:, : stack.shape[0]], part, preferred_element_type=jnp.float32)
        for part in (small, big)
    )
    picked = jnp.sum(found, axis=1, keepdims=True)
    return jnp.sum(weight * picked, axis=0, keepdims=True)


def inside_kernel(
    sat, mob, pore, qx, qy, qz, cell, well, factor, obs, after, mids, middle, early, hot, mask, weight
):
    rows, layers, columns = sat.shape
    count = cell.shape[1]

    def column_of(row):
        return jnp.concatenate(
            [
                jnp.transpose(jnp.broadcast_to(row[:, j : j + columns], (columns, columns)))
                for j in range(0, count, columns)
            ],
            axis=0,
        )

    cells = column_of(cell[...])
    row_of = lax.div(cells, columns)
    lane = lax.broadcasted_iota(jnp.int32, cells.shape, 1)
    mask[...] = jnp.where(cells - row_of * columns == lane, 1.0, 0.0)
    hot[...] = one_hot(row_of, OUTER, layers)
    near = one_hot(row_of, INNER, layers)
    weight[...] = jnp.where(column_of(well[...]) == lane, column_of(factor[...]), 0.0)

    f = [frac(sat[i], mob[i]) for i in range(rows)]
    face = {i: across(qx[i], f[i - 1], f[i]) for i in range(1, rows)}
    mids[0] = f[0]
    mids[1] = f[7]
    mids[2] = moved(sat[0], pore[0], face[1], f[0], qz[0], qy[0])
    mids[3] = moved(sat[7], pore[7], -face[7], f[7], qz[7], qy[7])
    s = {i: moved(sat[i], pore[i], face[i + 1] - face[i], f[i], qz[i], qy[i]) for i in range(1, 7)}
    f = {i: frac(s[i], mob[i]) for i in range(1, 7)}
    rates = [rates_of([f[i] for pair in INNER for i in pair], near, mask[...], weight[...])]
    face = {i: across(qx[i], f[i - 1], f[i]) for i in range(2, 7)}
    mids[4] = f[1]
    mids[5] = f[6]
    mids[6] = moved(s[1], pore[1], face[2], f[1], qz[1], qy[1])
    mids[7] = moved(s[6], pore[6], -face[6], f[6], qz[6], qy[6])
    s = {i: moved(s[i], pore[i], face[i + 1] - face[i], f[i], qz[i], qy[i]) for i in range(2, 6)}
    f = {i: frac(s[i], mob[i]) for i in range(2, 6)}
    rates.append(rates_of([f[i] for pair in INNER[:2] for i in pair], near, mask[...], weight[...]))
    face = {i: across(qx[i], f[i - 1], f[i]) for i in range(3, 6)}
    mids[8] = f[2]
    mids[9] = f[5]
    mids[10] = moved(s[2], pore[2], face[3], f[2], qz[2], qy[2])
    mids[11] = moved(s[5], pore[5], -face[5], f[5], qz[5], qy[5])
    last = [moved(s[i], pore[i], face[i + 1] - face[i], f[i], qz[i], qy[i]) for i in (3, 4)]
    for j in range(2):
        middle[j] = last[j]
    flows = [frac(last[j], mob[3 + j]) for j in range(2)]
    rates.append(rates_of(flows, near, mask[...], weight[...]))
    errors = jnp.concatenate(
        [obs[k : k + 1, :] for k in range(SUBSTEPS)]
        + [jnp.zeros((1, columns - SUBSTEPS * obs.shape[1]), jnp.float32)],
        axis=1,
    )
    early[...] = jnp.concatenate(rates + [errors], axis=0)


def outside_kernel(
    mob, pore, qx, qy, qz, low, high, mids, middle, early, hot, mask, weight, where, new_sat, shares
):
    tile = where[0]
    last = where[1]
    has_low = tile > 0
    has_high = tile < last
    below = jnp.where(has_low, low[0], 0.5)
    below_mob = jnp.where(has_low, low[1], 1.0)
    above = jnp.where(has_high, high[0], 0.5)
    above_mob = jnp.where(has_high, high[1], 1.0)
    x = {i: qx[i] for i in range(1, 8)}
    x[0] = jnp.where(has_low, qx[0], 0.0)
    x[8] = high[5]
    z = {i: qz[i] for i in (0, 1, 6, 7)}
    z[-1], z[8] = low[3], high[3]
    y = {i: qy[i] for i in (0, 1, 6, 7)}
    y[-1], y[8] = low[4], high[4]
    p = {i: pore[i] for i in (0, 1, 2, 5, 6, 7)}
    p[-1], p[8] = low[2], high[2]
    m = {i: mob[i] for i in (0, 1, 2, 5, 6, 7)}
    m[-1], m[8] = below_mob, above_mob

    f = {-1: frac(below, below_mob), 0: mids[0], 7: mids[1], 8: frac(above, above_mob)}
    out_low = jnp.minimum(low[5], 0.0) / f[-1]
    out_high = jnp.maximum(high[6], 0.0) / f[8]
    face = {i: across(x[i], f[i - 1], f[i]) for i in (0, 8)}
    s = {
        -1: moved(below, p[-1], face[0] - low[5], f[-1], z[-1], y[-1]),
        0: mids[2] + p[0] * face[0],
        7: mids[3] - p[7] * face[8],
        8: moved(above, p[8], high[6] - face[8], f[8], z[8], y[8]),
    }

    f = {i: frac(s[i], m[i]) for i in (-1, 0, 7, 8)}
    rates = [rates_of([f[0], f[7]], hot, mask[...], weight[...])]
    f[1], f[6] = mids[4], mids[5]
    face = {i: across(x[i], f[i - 1], f[i]) for i in (0, 1, 7, 8)}
    face[-1] = low[6] + out_low * f[-1]
    face[9] = out_high * f[8] + high[7]
    s = {i: moved(s[i], p[i], face[i + 1] - face[i], f[i], z[i], y[i]) for i in (-1, 0, 7, 8)}
    s[1] = mids[6] + p[1] * face[1]
    s[6] = mids[7] - p[6] * face[7]

    f = {i: frac(s[i], m[i]) for i in (-1, 0, 1, 6, 7, 8)}
    rates.append(rates_of([f[0], f[7], f[1], f[6]], hot, mask[...], weight[...]))
    f[2], f[5] = mids[8], mids[9]
    face = {i: across(x[i], f[i - 1], f[i]) for i in (0, 1, 2, 6, 7, 8)}
    s = {i: moved(s[i], p[i], face[i + 1] - face[i], f[i], z[i], y[i]) for i in (0, 1, 6, 7)}
    s[2] = mids[10] + p[2] * face[2]
    s[5] = mids[11] - p[5] * face[6]
    for i in (0, 1, 2, 5, 6, 7):
        new_sat[i] = s[i]
    for j in range(2):
        new_sat[3 + j] = middle[j]
    f = {i: frac(s[i], m[i]) for i in (0, 1, 2, 5, 6, 7)}
    rates.append(
        rates_of([f[i] for pair in OUTER for i in pair], hot, mask[...], weight[...])
    )
    wells = shares.shape[1]
    home = lax.broadcasted_iota(jnp.int32, (1, wells), 1) // WELLS_DEV == tile
    errors = []
    for k in range(SUBSTEPS):
        shift = lax.rem(WELLS_DEV * (tile + 16 - k), wells)
        errors.append(jnp.where(home, pltpu.roll(early[SUBSTEPS : SUBSTEPS + 1], shift, 1), 0.0))
    rates = [early[k : k + 1] + rates[k] for k in range(SUBSTEPS)]
    share = jnp.concatenate(rates + errors + [jnp.zeros((2, wells), jnp.float32)], axis=0)
    for j in range(shares.shape[0] // 8):
        shares[8 * j : 8 * j + 8, :] = share


def plane_kernel(parts, out):
    groups, per, width = 4, 8, 8
    rows = []
    for k in range(SUBSTEPS):
        total = parts[pl.ds(k, groups, stride=per * width), :]
        for j in range(1, per):
            total = total + parts[pl.ds(width * j + k, groups, stride=per * width), :]
        rows.append(total)
    errors = parts[SUBSTEPS : SUBSTEPS + 4]
    for j in range(1, per):
        errors = errors + parts[width * j + SUBSTEPS : width * j + SUBSTEPS + 4]
    block = jnp.concatenate(rows + [errors], axis=0)
    size = block.shape[0]
    for j in range(out.shape[0] // size):
        out[size * j : size * (j + 1), :] = block


def gram_kernel(parts, where, rates_out, gram):
    tile = where[0]
    own_x = where[2]
    own_z = where[3]
    groups, per, layer, size = 4, 2, 8, 16
    wells = parts.shape[1]
    mine = rates_out.shape[2]

    def member_rows(row):
        total = parts[pl.ds(row, layer, stride=per * size), :]
        return total + parts[pl.ds(size + row, layer, stride=per * size), :]

    sums = [
        jnp.concatenate([member_rows(groups * k + g) for k in range(SUBSTEPS)], axis=0)
        for g in range(groups)
    ]
    first = groups * SUBSTEPS
    errors = [
        parts[first + k : first + k + 1] + parts[size + first + k : size + first + k + 1]
        for k in range(SUBSTEPS)
    ]
    ensemble = groups * layer
    own = sums[0]
    for g in range(1, groups):
        own = jnp.where(own_x == g, sums[g], own)
    lane = lax.broadcasted_iota(jnp.int32, (layer, wells), 1)
    sublane = lax.broadcasted_iota(jnp.int32, (layer, wells), 0)
    products = [jnp.zeros((layer, wells), jnp.float32)] * groups
    own_rates = []
    for k in range(SUBSTEPS):
        part = slice(k * layer, (k + 1) * layer)
        data = [total[part] / errors[k] for total in sums]
        mean = jnp.sum(data[0] + data[1] + data[2] + data[3], axis=0, keepdims=True) / ensemble
        row = jnp.sum(jnp.where(sublane == own_z, own[part], 0.0), axis=0, keepdims=True)
        own_rates.append(row)
        centered = row / errors[k] - mean
        products = [total + (d - mean) * centered for total, d in zip(products, data)]
    line = jnp.zeros((layer, wells), jnp.float32)
    for g in range(groups):
        dots = jnp.sum(products[g], axis=1, keepdims=True)
        line = line + jnp.where(lane == sublane + g * layer, dots, 0.0)
    line = jnp.sum(line, axis=0, keepdims=True) / (ensemble - 1.0)
    gram[...] = line[:, :ensemble]
    front = jnp.concatenate(own_rates + [jnp.zeros((layer - SUBSTEPS, wells), jnp.float32)], axis=0)
    front = pltpu.roll(front, lax.rem(wells - tile * mine, wells), 1)
    for k in range(SUBSTEPS):
        rates_out[k] = front[k : k + 1, :mine]


VMEM = pl.BlockSpec(memory_space=pltpu.VMEM)
ANY = pl.BlockSpec(memory_space=pl.ANY)
SMEM = pl.BlockSpec(memory_space=pltpu.SMEM)


def shape(*dims):
    return jax.ShapeDtypeStruct(dims, jnp.float32)


def held(*dims):
    return pltpu.VMEM(dims, jnp.float32)


def body(
    saturation,
    mobility,
    pore_scale,
    flux_x,
    flux_y,
    flux_z,
    conn_cell,
    conn_well,
    conn_factor,
    obs_error,
):
    rows, layers, columns = saturation.shape[1:]
    fields = [
        a.reshape(rows, layers, columns)
        for a in (saturation, mobility, pore_scale, flux_x, flux_y, flux_z)
    ]
    tiles = lax.axis_size(TILE)
    tile = lax.axis_index(TILE)
    where = jnp.stack(
        [tile, jnp.full_like(tile, tiles - 1), lax.axis_index("x"), lax.axis_index("zl")]
    ).astype(jnp.int32)
    up, down, *fields = pl.pallas_call(
        edge_kernel,
        out_shape=(held(UP_ROWS, layers, columns), held(DOWN_ROWS, layers, columns))
        + (held(rows, layers, columns),) * 6,
        in_specs=[ANY] * 6,
        out_specs=(VMEM,) * 8,
        scratch_shapes=[pltpu.SemaphoreType.DMA((18,))],
        name="edges",
    )(*fields)
    low = lax.ppermute(up, TILE, [(i, i + 1) for i in range(tiles - 1)])
    high = lax.ppermute(down, TILE, [(i + 1, i) for i in range(tiles - 1)])
    wells = obs_error.shape[0] * tiles
    count = conn_cell.shape[0]
    sat, mob, pore, qx, qy, qz = fields
    mids, middle, early, hot, mask, weight = pl.pallas_call(
        inside_kernel,
        out_shape=(
            shape(12, layers, columns),
            shape(2, layers, columns),
            shape(SUBSTEPS + 1, wells),
            jax.ShapeDtypeStruct((count, 6 * layers), jnp.bfloat16),
            shape(count, columns),
            shape(count, wells),
        ),
        in_specs=[VMEM] * 10 + [ANY],
        out_specs=(VMEM,) * 6,
        compiler_params=pltpu.CompilerParams(vmem_limit_bytes=32 * 1024 * 1024),
        name="inside",
    )(
        *fields,
        conn_cell.reshape(1, count),
        conn_well.reshape(1, count),
        conn_factor.reshape(1, count),
        obs_error.T,
        up,
    )
    new_saturation, shares = pl.pallas_call(
        outside_kernel,
        out_shape=(held(rows, layers, columns), held(256, wells)),
        in_specs=[VMEM] * 13 + [SMEM],
        out_specs=(VMEM, VMEM),
        compiler_params=pltpu.CompilerParams(vmem_limit_bytes=32 * 1024 * 1024),
        name="outside",
    )(mob, pore, qx, qy, qz, low, high, mids, middle, early, hot, mask, weight, where)
    plane = lax.all_to_all(shares.reshape(32, 8, wells), PLANE, 0, 0)
    plane = pltpu.with_memory_space_constraint(plane.reshape(256, wells), pltpu.VMEM)
    (spreads,) = pl.pallas_call(
        plane_kernel,
        out_shape=(held(256, wells),),
        in_specs=[VMEM],
        out_specs=(VMEM,),
        name="plane_sums",
    )(plane)
    line = lax.all_to_all(spreads.reshape(16, 16, wells), LINE, 0, 0)
    line = pltpu.with_memory_space_constraint(line.reshape(256, wells), pltpu.VMEM)
    rates, gram = pl.pallas_call(
        gram_kernel,
        out_shape=(shape(SUBSTEPS, 1, obs_error.shape[0]), shape(1, 32)),
        in_specs=[VMEM, SMEM],
        out_specs=(VMEM, VMEM),
        name="gram_row",
    )(line, where)
    return (
        new_saturation.reshape(saturation.shape),
        jnp.transpose(rates, (1, 2, 0)),
        gram,
    )


def solution(mesh):
    split = Mesh(mesh.devices.reshape(SIZES), AXES)
    in_specs = (P(MEMBER, TILE, None, None),) * 6 + (P(TILE),) * 3 + (P(TILE, None),)
    out_specs = (P(MEMBER, TILE, None, None), P(MEMBER, TILE, None), P(MEMBER, None))
    return jax.shard_map(body, mesh=split, in_specs=in_specs, out_specs=out_specs, check_vma=False)
```

```python
import jax
import jax.numpy as jnp
from jax import lax
from jax.experimental import pallas as pl
from jax.experimental.pallas import tpu as pltpu
from jax.sharding import Mesh
from jax.sharding import PartitionSpec as P

SUBSTEPS = 3
AXES = ("x", "zl", "y", "zh", "c")
SIZES = (4, 8, 4, 2, 2)
MEMBER = ("x", "zl")
TILE = ("y", "zh", "c")
LINE = ("zl", "zh", "c")
PLANE = ("x", "y")
UP_ROWS = 7
DOWN_ROWS = 8
HIGHEST = lax.Precision.HIGHEST


def frac(sat, mob):
    wet = sat * sat
    dry = (1.0 - sat) * (1.0 - sat)
    return wet / (wet + mob * dry)


def inner(flux, axis):
    return jnp.where(lax.broadcasted_iota(jnp.int32, flux.shape, axis) > 0, flux, 0.0)


def across(flux, below, here):
    return flux * jnp.where(flux > 0.0, below, here)


def spread(flow, flux, axis):
    face = across(flux, pltpu.roll(flow, 1, axis), flow)
    return pltpu.roll(face, flow.shape[axis] - 1, axis) - face


def moved(sat, pore, net, flow, flux_z, flux_y):
    return sat - pore * (
        net + spread(flow, inner(flux_z, 0), 0) + spread(flow, inner(flux_y, 1), 1)
    )


def edge_kernel(sat, mob, pore, qx, qy, qz, up, down, s, m, p, x, y, z, sem):
    pieces = ((0, 3), (5, 3), (3, 2))
    loads = []
    for j, (start, size) in enumerate(pieces):
        for k, (field, near) in enumerate(
            ((sat, s), (mob, m), (qx, x), (qy, y), (qz, z), (pore, p))
        ):
            part = pl.ds(start, size)
            loads.append(pltpu.make_async_copy(field.at[part], near.at[part], sem.at[6 * j + k]))
    for load in loads:
        load.start()
    for load in loads[:12]:
        load.wait()
    f = [frac(s[i], m[i]) for i in range(3)]
    face_1 = across(x[1], f[0], f[1])
    flow_1 = frac(moved(s[1], p[1], across(x[2], f[1], f[2]) - face_1, f[1], z[1], y[1]), m[1])
    for k, near in enumerate((s, m, p, z, y, x)):
        down[k] = near[0]
    down[6] = face_1
    down[7] = jnp.minimum(x[1], 0.0) * flow_1
    f = {i: frac(s[i], m[i]) for i in range(5, 8)}
    face_7 = across(x[7], f[6], f[7])
    flow_6 = frac(moved(s[6], p[6], face_7 - across(x[6], f[5], f[6]), f[6], z[6], y[6]), m[6])
    for k, near in enumerate((s, m, p, z, y)):
        up[k] = near[7]
    up[5] = face_7
    up[6] = jnp.maximum(x[7], 0.0) * flow_6
    for load in loads[12:]:
        load.wait()


OUTER = ((0, 7), (1, 6), (2, 5))
INNER = ((3, 4), (2, 5), (1, 6))


def one_hot(row_of, pairs, layers):
    lane = lax.broadcasted_iota(jnp.int32, row_of.shape, 1)
    hots = []
    for first, second in pairs:
        target = jnp.where(lane < layers, lane + first * layers, lane + (second - 1) * layers)
        hots.append(jnp.where(row_of == target, 1.0, 0.0).astype(jnp.bfloat16))
    return jnp.concatenate(hots, axis=1)


def rates_of(flows, hot, mask, weight):
    stack = jnp.concatenate(flows, axis=0)
    big = stack.astype(jnp.bfloat16)
    rest = stack - big.astype(jnp.float32)
    small = rest.astype(jnp.bfloat16)
    found = mask * sum(
        jnp.dot(hot[:, : stack.shape[0]], part, preferred_element_type=jnp.float32)
        for part in (small, big)
    )
    picked = jnp.sum(found, axis=1, keepdims=True)
    return jnp.sum(weight * picked, axis=0, keepdims=True)


def inside_kernel(
    sat, mob, pore, qx, qy, qz, cell, well, factor, obs, after, mids, middle, early, hot, mask, weight
):
    rows, layers, columns = sat.shape
    count = cell.shape[1]

    def column_of(row):
        return jnp.concatenate(
            [
                jnp.transpose(jnp.broadcast_to(row[:, j : j + columns], (columns, columns)))
                for j in range(0, count, columns)
            ],
            axis=0,
        )

    cells = column_of(cell[...])
    row_of = lax.div(cells, columns)
    lane = lax.broadcasted_iota(jnp.int32, cells.shape, 1)
    mask[...] = jnp.where(cells - row_of * columns == lane, 1.0, 0.0)
    hot[...] = one_hot(row_of, OUTER, layers)
    near = one_hot(row_of, INNER, layers)
    weight[...] = jnp.where(column_of(well[...]) == lane, column_of(factor[...]), 0.0)

    f = [frac(sat[i], mob[i]) for i in range(rows)]
    face = {i: across(qx[i], f[i - 1], f[i]) for i in range(1, rows)}
    mids[0] = f[0]
    mids[1] = f[7]
    mids[2] = moved(sat[0], pore[0], face[1], f[0], qz[0], qy[0])
    mids[3] = moved(sat[7], pore[7], -face[7], f[7], qz[7], qy[7])
    s = {i: moved(sat[i], pore[i], face[i + 1] - face[i], f[i], qz[i], qy[i]) for i in range(1, 7)}
    f = {i: frac(s[i], mob[i]) for i in range(1, 7)}
    rates = [rates_of([f[i] for pair in INNER for i in pair], near, mask[...], weight[...])]
    face = {i: across(qx[i], f[i - 1], f[i]) for i in range(2, 7)}
    mids[4] = f[1]
    mids[5] = f[6]
    mids[6] = moved(s[1], pore[1], face[2], f[1], qz[1], qy[1])
    mids[7] = moved(s[6], pore[6], -face[6], f[6], qz[6], qy[6])
    s = {i: moved(s[i], pore[i], face[i + 1] - face[i], f[i], qz[i], qy[i]) for i in range(2, 6)}
    f = {i: frac(s[i], mob[i]) for i in range(2, 6)}
    rates.append(rates_of([f[i] for pair in INNER[:2] for i in pair], near, mask[...], weight[...]))
    face = {i: across(qx[i], f[i - 1], f[i]) for i in range(3, 6)}
    mids[8] = f[2]
    mids[9] = f[5]
    mids[10] = moved(s[2], pore[2], face[3], f[2], qz[2], qy[2])
    mids[11] = moved(s[5], pore[5], -face[5], f[5], qz[5], qy[5])
    last = [moved(s[i], pore[i], face[i + 1] - face[i], f[i], qz[i], qy[i]) for i in (3, 4)]
    for j in range(2):
        middle[j] = last[j]
    flows = [frac(last[j], mob[3 + j]) for j in range(2)]
    rates.append(rates_of(flows, near, mask[...], weight[...]))
    errors = jnp.concatenate(
        [obs[k : k + 1, :] for k in range(SUBSTEPS)]
        + [jnp.zeros((1, columns - SUBSTEPS * obs.shape[1]), jnp.float32)],
        axis=1,
    )
    early[...] = jnp.concatenate(rates + [errors], axis=0)


def outside_kernel(
    mob, pore, qx, qy, qz, low, high, mids, middle, early, hot, mask, weight, where, new_sat, shares
):
    tile = where[0]
    last = where[1]
    has_low = tile > 0
    has_high = tile < last
    below = jnp.where(has_low, low[0], 0.5)
    below_mob = jnp.where(has_low, low[1], 1.0)
    above = jnp.where(has_high, high[0], 0.5)
    above_mob = jnp.where(has_high, high[1], 1.0)
    x = {i: qx[i] for i in range(1, 8)}
    x[0] = jnp.where(has_low, qx[0], 0.0)
    x[8] = high[5]
    z = {i: qz[i] for i in (0, 1, 6, 7)}
    z[-1], z[8] = low[3], high[3]
    y = {i: qy[i] for i in (0, 1, 6, 7)}
    y[-1], y[8] = low[4], high[4]
    p = {i: pore[i] for i in (0, 1, 2, 5, 6, 7)}
    p[-1], p[8] = low[2], high[2]
    m = {i: mob[i] for i in (0, 1, 2, 5, 6, 7)}
    m[-1], m[8] = below_mob, above_mob

    f = {-1: frac(below, below_mob), 0: mids[0], 7: mids[1], 8: frac(above, above_mob)}
    out_low = jnp.minimum(low[5], 0.0) / f[-1]
    out_high = jnp.maximum(high[6], 0.0) / f[8]
    face = {i: across(x[i], f[i - 1], f[i]) for i in (0, 8)}
    s = {
        -1: moved(below, p[-1], face[0] - low[5], f[-1], z[-1], y[-1]),
        0: mids[2] + p[0] * face[0],
        7: mids[3] - p[7] * face[8],
        8: moved(above, p[8], high[6] - face[8], f[8], z[8], y[8]),
    }

    f = {i: frac(s[i], m[i]) for i in (-1, 0, 7, 8)}
    rates = [rates_of([f[0], f[7]], hot, mask[...], weight[...])]
    f[1], f[6] = mids[4], mids[5]
    face = {i: across(x[i], f[i - 1], f[i]) for i in (0, 1, 7, 8)}
    face[-1] = low[6] + out_low * f[-1]
    face[9] = out_high * f[8] + high[7]
    s = {i: moved(s[i], p[i], face[i + 1] - face[i], f[i], z[i], y[i]) for i in (-1, 0, 7, 8)}
    s[1] = mids[6] + p[1] * face[1]
    s[6] = mids[7] - p[6] * face[7]

    f = {i: frac(s[i], m[i]) for i in (-1, 0, 1, 6, 7, 8)}
    rates.append(rates_of([f[0], f[7], f[1], f[6]], hot, mask[...], weight[...]))
    f[2], f[5] = mids[8], mids[9]
    face = {i: across(x[i], f[i - 1], f[i]) for i in (0, 1, 2, 6, 7, 8)}
    s = {i: moved(s[i], p[i], face[i + 1] - face[i], f[i], z[i], y[i]) for i in (0, 1, 6, 7)}
    s[2] = mids[10] + p[2] * face[2]
    s[5] = mids[11] - p[5] * face[6]
    for i in (0, 1, 2, 5, 6, 7):
        new_sat[i] = s[i]
    for j in range(2):
        new_sat[3 + j] = middle[j]
    f = {i: frac(s[i], m[i]) for i in (0, 1, 2, 5, 6, 7)}
    rates.append(
        rates_of([f[i] for pair in OUTER for i in pair], hot, mask[...], weight[...])
    )
    zero = jnp.zeros_like(rates[0])
    share = early[...] + jnp.concatenate(rates + [zero], axis=0)
    share = jnp.concatenate([share, share], axis=0)
    for j in range(shares.shape[0] // 8):
        shares[8 * j : 8 * j + 8, :] = share


def line_kernel(parts, out):
    members, per = 8, 4
    width = SUBSTEPS + 1
    rows = []
    for k in range(SUBSTEPS):
        total = parts[pl.ds(k, members, stride=per * width), :]
        for j in range(1, per):
            total = total + parts[pl.ds(width * j + k, members, stride=per * width), :]
        rows.append(total)
    errors = [parts[width * j + SUBSTEPS : width * j + SUBSTEPS + 1, :] for j in range(per)]
    rows.append(jnp.concatenate(errors, axis=0))
    block = jnp.concatenate(rows, axis=0)
    size = block.shape[0]
    for j in range(out.shape[0] // size):
        out[size * j : size * (j + 1), :] = block


def gram_kernel(parts, where, rates_out, gram):
    tile = where[0]
    own_x = where[2]
    own_z = where[3]
    groups, per, layer = 4, 4, 8
    rows = SUBSTEPS * layer
    wells = parts.shape[1]
    mine = rates_out.shape[2]
    size = rows + per
    sums = []
    for g in range(groups):
        starts = [(g * per + j) * size for j in range(per)]
        total = parts[starts[0] : starts[0] + rows]
        for start in starts[1:]:
            total = total + parts[start : start + rows]
        sums.append(total)
    packed = jnp.concatenate(
        [parts[y * size + rows : (y + 1) * size] for y in range(per)], axis=0
    )
    tiles = packed.shape[0]
    lane = lax.broadcasted_iota(jnp.int32, packed.shape, 1)
    home = lane // mine == lax.broadcasted_iota(jnp.int32, packed.shape, 0)
    errors = []
    for k in range(SUBSTEPS):
        front = packed if k == 0 else pltpu.roll(packed, wells - mine * k, 1)
        moved = pltpu.roll(front, 0, 1, stride=mine, stride_axis=0)
        errors.append(jnp.sum(jnp.where(home, moved, 0.0), axis=0, keepdims=True))
    ensemble = groups * layer
    own = sums[0]
    for g in range(1, groups):
        own = jnp.where(own_x == g, sums[g], own)
    lane = lax.broadcasted_iota(jnp.int32, (layer, wells), 1)
    sublane = lax.broadcasted_iota(jnp.int32, (layer, wells), 0)
    products = [jnp.zeros((layer, wells), jnp.float32)] * groups
    own_rates = []
    for k in range(SUBSTEPS):
        part = slice(k * layer, (k + 1) * layer)
        scale = 1.0 / errors[k]
        data = [total[part] * scale for total in sums]
        mean = jnp.sum(data[0] + data[1] + data[2] + data[3], axis=0, keepdims=True) * (1.0 / ensemble)
        row = jnp.sum(jnp.where(sublane == own_z, own[part], 0.0), axis=0, keepdims=True)
        own_rates.append(row)
        centered = row * scale - mean
        products = [total + (d - mean) * centered for total, d in zip(products, data)]
    line = jnp.zeros((layer, wells), jnp.float32)
    for g in range(groups):
        dots = jnp.sum(products[g], axis=1, keepdims=True)
        line = line + jnp.where(lane == sublane + g * layer, dots, 0.0)
    line = jnp.sum(line, axis=0, keepdims=True) * (1.0 / (ensemble - 1.0))
    gram[...] = line[:, :ensemble]
    front = jnp.concatenate(own_rates + [jnp.zeros((layer - SUBSTEPS, wells), jnp.float32)], axis=0)
    front = pltpu.roll(front, lax.rem(wells - tile * mine, wells), 1)
    for k in range(SUBSTEPS):
        rates_out[k] = front[k : k + 1, :mine]


VMEM = pl.BlockSpec(memory_space=pltpu.VMEM)
ANY = pl.BlockSpec(memory_space=pl.ANY)
SMEM = pl.BlockSpec(memory_space=pltpu.SMEM)


def shape(*dims):
    return jax.ShapeDtypeStruct(dims, jnp.float32)


def held(*dims):
    return pltpu.VMEM(dims, jnp.float32)


def body(
    saturation,
    mobility,
    pore_scale,
    flux_x,
    flux_y,
    flux_z,
    conn_cell,
    conn_well,
    conn_factor,
    obs_error,
):
    rows, layers, columns = saturation.shape[1:]
    fields = [
        a.reshape(rows, layers, columns)
        for a in (saturation, mobility, pore_scale, flux_x, flux_y, flux_z)
    ]
    tiles = lax.axis_size(TILE)
    tile = lax.axis_index(TILE)
    where = jnp.stack(
        [tile, jnp.full_like(tile, tiles - 1), lax.axis_index("x"), lax.axis_index("zl")]
    ).astype(jnp.int32)
    up, down, *fields = pl.pallas_call(
        edge_kernel,
        out_shape=(held(UP_ROWS, layers, columns), held(DOWN_ROWS, layers, columns))
        + (held(rows, layers, columns),) * 6,
        in_specs=[ANY] * 6,
        out_specs=(VMEM,) * 8,
        scratch_shapes=[pltpu.SemaphoreType.DMA((18,))],
        name="edges",
    )(*fields)
    low = lax.ppermute(up, TILE, [(i, i + 1) for i in range(tiles - 1)])
    high = lax.ppermute(down, TILE, [(i + 1, i) for i in range(tiles - 1)])
    wells = obs_error.shape[0] * tiles
    count = conn_cell.shape[0]
    sat, mob, pore, qx, qy, qz = fields
    mids, middle, early, hot, mask, weight = pl.pallas_call(
        inside_kernel,
        out_shape=(
            shape(12, layers, columns),
            shape(2, layers, columns),
            shape(SUBSTEPS + 1, wells),
            jax.ShapeDtypeStruct((count, 6 * layers), jnp.bfloat16),
            shape(count, columns),
            shape(count, wells),
        ),
        in_specs=[VMEM] * 10 + [ANY],
        out_specs=(VMEM,) * 6,
        compiler_params=pltpu.CompilerParams(vmem_limit_bytes=32 * 1024 * 1024),
        name="inside",
    )(
        *fields,
        conn_cell.reshape(1, count),
        conn_well.reshape(1, count),
        conn_factor.reshape(1, count),
        obs_error.T,
        up,
    )
    new_saturation, shares = pl.pallas_call(
        outside_kernel,
        out_shape=(held(rows, layers, columns), held(128, wells)),
        in_specs=[VMEM] * 13 + [SMEM],
        out_specs=(VMEM, VMEM),
        compiler_params=pltpu.CompilerParams(vmem_limit_bytes=32 * 1024 * 1024),
        name="outside",
    )(mob, pore, qx, qy, qz, low, high, mids, middle, early, hot, mask, weight, where)
    line = lax.all_to_all(shares.reshape(32, 4, wells), LINE, 0, 0)
    line = pltpu.with_memory_space_constraint(line.reshape(128, wells), pltpu.VMEM)
    (spreads,) = pl.pallas_call(
        line_kernel,
        out_shape=(held(16 * 28, wells),),
        in_specs=[VMEM],
        out_specs=(VMEM,),
        name="line_sums",
    )(line)
    plane = lax.all_to_all(spreads.reshape(16, 7, 4, wells), PLANE, 0, 0)
    plane = pltpu.with_memory_space_constraint(plane.reshape(16 * 28, wells), pltpu.VMEM)
    rates, gram = pl.pallas_call(
        gram_kernel,
        out_shape=(shape(SUBSTEPS, 1, obs_error.shape[0]), shape(1, 32)),
        in_specs=[VMEM, SMEM],
        out_specs=(VMEM, VMEM),
        name="gram_row",
    )(plane, where)
    return (
        new_saturation.reshape(saturation.shape),
        jnp.transpose(rates, (1, 2, 0)),
        gram,
    )


def solution(mesh):
    split = Mesh(mesh.devices.reshape(SIZES), AXES)
    in_specs = (P(MEMBER, TILE, None, None),) * 6 + (P(TILE),) * 3 + (P(TILE, None),)
    out_specs = (P(MEMBER, TILE, None, None), P(MEMBER, TILE, None), P(MEMBER, None))
    return jax.shard_map(body, mesh=split, in_specs=in_specs, out_specs=out_specs, check_vma=False)
```

```python
import jax
import jax.numpy as jnp
from jax import lax
from jax.experimental import pallas as pl
from jax.experimental.pallas import tpu as pltpu
from jax.sharding import Mesh
from jax.sharding import PartitionSpec as P

SUBSTEPS = 3
AXES = ("x", "zl", "y", "zh", "c")
SIZES = (4, 8, 4, 2, 2)
MEMBER = ("x", "zl")
TILE = ("y", "zh", "c")
LINE = ("zl", "zh", "c")
PLANE = ("x", "y")
UP_ROWS = 7
DOWN_ROWS = 8
HIGHEST = lax.Precision.HIGHEST


def frac(sat, mob):
    wet = sat * sat
    dry = (1.0 - sat) * (1.0 - sat)
    return wet / (wet + mob * dry)


def inner(flux, axis):
    return jnp.where(lax.broadcasted_iota(jnp.int32, flux.shape, axis) > 0, flux, 0.0)


def across(flux, below, here):
    return flux * jnp.where(flux > 0.0, below, here)


def spread(flow, flux, axis):
    face = across(flux, pltpu.roll(flow, 1, axis), flow)
    return pltpu.roll(face, flow.shape[axis] - 1, axis) - face


def moved(sat, pore, net, flow, flux_z, flux_y):
    return sat - pore * (
        net + spread(flow, inner(flux_z, 0), 0) + spread(flow, inner(flux_y, 1), 1)
    )


def edge_kernel(sat, mob, pore, qx, qy, qz, up, down, s, m, p, x, y, z, sem):
    pieces = ((0, 3), (5, 3), (3, 2))
    loads = []
    for j, (start, size) in enumerate(pieces):
        for k, (field, near) in enumerate(
            ((sat, s), (mob, m), (qx, x), (qy, y), (qz, z), (pore, p))
        ):
            part = pl.ds(start, size)
            loads.append(pltpu.make_async_copy(field.at[part], near.at[part], sem.at[6 * j + k]))
    for load in loads:
        load.start()
    for load in loads[:12]:
        load.wait()
    f = [frac(s[i], m[i]) for i in range(3)]
    face_1 = across(x[1], f[0], f[1])
    flow_1 = frac(moved(s[1], p[1], across(x[2], f[1], f[2]) - face_1, f[1], z[1], y[1]), m[1])
    for k, near in enumerate((s, m, p, z, y, x)):
        down[k] = near[0]
    down[6] = face_1
    down[7] = jnp.minimum(x[1], 0.0) * flow_1
    f = {i: frac(s[i], m[i]) for i in range(5, 8)}
    face_7 = across(x[7], f[6], f[7])
    flow_6 = frac(moved(s[6], p[6], face_7 - across(x[6], f[5], f[6]), f[6], z[6], y[6]), m[6])
    for k, near in enumerate((s, m, p, z, y)):
        up[k] = near[7]
    up[5] = face_7
    up[6] = jnp.maximum(x[7], 0.0) * flow_6
    for load in loads[12:]:
        load.wait()


OUTER = ((0, 7), (1, 6), (2, 5))
INNER = ((3, 4), (2, 5), (1, 6))


def one_hot(row_of, pairs, layers):
    lane = lax.broadcasted_iota(jnp.int32, row_of.shape, 1)
    hots = []
    for first, second in pairs:
        target = jnp.where(lane < layers, lane + first * layers, lane + (second - 1) * layers)
        hots.append(jnp.where(row_of == target, 1.0, 0.0).astype(jnp.bfloat16))
    return jnp.concatenate(hots, axis=1)


def rates_of(flows, hot, mask, weight):
    stack = jnp.concatenate(flows, axis=0)
    big = stack.astype(jnp.bfloat16)
    rest = stack - big.astype(jnp.float32)
    small = rest.astype(jnp.bfloat16)
    found = mask * sum(
        jnp.dot(hot[:, : stack.shape[0]], part, preferred_element_type=jnp.float32)
        for part in (small, big)
    )
    picked = jnp.sum(found, axis=1, keepdims=True)
    return jnp.sum(weight * picked, axis=0, keepdims=True)


def inside_kernel(
    sat, mob, pore, qx, qy, qz, cell, well, factor, obs, after, mids, middle, early, hot, mask, weight
):
    rows, layers, columns = sat.shape
    count = cell.shape[1]

    def column_of(row):
        return jnp.concatenate(
            [
                jnp.transpose(jnp.broadcast_to(row[:, j : j + columns], (columns, columns)))
                for j in range(0, count, columns)
            ],
            axis=0,
        )

    cells = column_of(cell[...])
    row_of = lax.div(cells, columns)
    lane = lax.broadcasted_iota(jnp.int32, cells.shape, 1)
    mask[...] = jnp.where(cells - row_of * columns == lane, 1.0, 0.0)
    hot[...] = one_hot(row_of, OUTER, layers)
    near = one_hot(row_of, INNER, layers)
    weight[...] = jnp.where(column_of(well[...]) == lane, column_of(factor[...]), 0.0)

    f = [frac(sat[i], mob[i]) for i in range(rows)]
    face = {i: across(qx[i], f[i - 1], f[i]) for i in range(1, rows)}
    mids[0] = f[0]
    mids[1] = f[7]
    mids[2] = moved(sat[0], pore[0], face[1], f[0], qz[0], qy[0])
    mids[3] = moved(sat[7], pore[7], -face[7], f[7], qz[7], qy[7])
    s = {i: moved(sat[i], pore[i], face[i + 1] - face[i], f[i], qz[i], qy[i]) for i in range(1, 7)}
    f = {i: frac(s[i], mob[i]) for i in range(1, 7)}
    rates = [rates_of([f[i] for pair in INNER for i in pair], near, mask[...], weight[...])]
    face = {i: across(qx[i], f[i - 1], f[i]) for i in range(2, 7)}
    mids[4] = f[1]
    mids[5] = f[6]
    mids[6] = moved(s[1], pore[1], face[2], f[1], qz[1], qy[1])
    mids[7] = moved(s[6], pore[6], -face[6], f[6], qz[6], qy[6])
    s = {i: moved(s[i], pore[i], face[i + 1] - face[i], f[i], qz[i], qy[i]) for i in range(2, 6)}
    f = {i: frac(s[i], mob[i]) for i in range(2, 6)}
    rates.append(rates_of([f[i] for pair in INNER[:2] for i in pair], near, mask[...], weight[...]))
    face = {i: across(qx[i], f[i - 1], f[i]) for i in range(3, 6)}
    mids[8] = f[2]
    mids[9] = f[5]
    mids[10] = moved(s[2], pore[2], face[3], f[2], qz[2], qy[2])
    mids[11] = moved(s[5], pore[5], -face[5], f[5], qz[5], qy[5])
    last = [moved(s[i], pore[i], face[i + 1] - face[i], f[i], qz[i], qy[i]) for i in (3, 4)]
    for j in range(2):
        middle[j] = last[j]
    flows = [frac(last[j], mob[3 + j]) for j in range(2)]
    rates.append(rates_of(flows, near, mask[...], weight[...]))
    errors = jnp.concatenate(
        [obs[k : k + 1, :] for k in range(SUBSTEPS)]
        + [jnp.zeros((1, columns - SUBSTEPS * obs.shape[1]), jnp.float32)],
        axis=1,
    )
    early[...] = jnp.concatenate(rates + [errors], axis=0)


def outside_kernel(
    mob, pore, qx, qy, qz, low, high, mids, middle, early, hot, mask, weight, where, new_sat, shares
):
    tile = where[0]
    last = where[1]
    has_low = tile > 0
    has_high = tile < last
    below = jnp.where(has_low, low[0], 0.5)
    below_mob = jnp.where(has_low, low[1], 1.0)
    above = jnp.where(has_high, high[0], 0.5)
    above_mob = jnp.where(has_high, high[1], 1.0)
    x = {i: qx[i] for i in range(1, 8)}
    x[0] = jnp.where(has_low, qx[0], 0.0)
    x[8] = high[5]
    z = {i: qz[i] for i in (0, 1, 6, 7)}
    z[-1], z[8] = low[3], high[3]
    y = {i: qy[i] for i in (0, 1, 6, 7)}
    y[-1], y[8] = low[4], high[4]
    p = {i: pore[i] for i in (0, 1, 2, 5, 6, 7)}
    p[-1], p[8] = low[2], high[2]
    m = {i: mob[i] for i in (0, 1, 2, 5, 6, 7)}
    m[-1], m[8] = below_mob, above_mob

    f = {-1: frac(below, below_mob), 0: mids[0], 7: mids[1], 8: frac(above, above_mob)}
    out_low = jnp.minimum(low[5], 0.0) / f[-1]
    out_high = jnp.maximum(high[6], 0.0) / f[8]
    face = {i: across(x[i], f[i - 1], f[i]) for i in (0, 8)}
    s = {
        -1: moved(below, p[-1], face[0] - low[5], f[-1], z[-1], y[-1]),
        0: mids[2] + p[0] * face[0],
        7: mids[3] - p[7] * face[8],
        8: moved(above, p[8], high[6] - face[8], f[8], z[8], y[8]),
    }

    f = {i: frac(s[i], m[i]) for i in (-1, 0, 7, 8)}
    rates = [rates_of([f[0], f[7]], hot, mask[...], weight[...])]
    f[1], f[6] = mids[4], mids[5]
    face = {i: across(x[i], f[i - 1], f[i]) for i in (0, 1, 7, 8)}
    face[-1] = low[6] + out_low * f[-1]
    face[9] = out_high * f[8] + high[7]
    s = {i: moved(s[i], p[i], face[i + 1] - face[i], f[i], z[i], y[i]) for i in (-1, 0, 7, 8)}
    s[1] = mids[6] + p[1] * face[1]
    s[6] = mids[7] - p[6] * face[7]

    f = {i: frac(s[i], m[i]) for i in (-1, 0, 1, 6, 7, 8)}
    rates.append(rates_of([f[0], f[7], f[1], f[6]], hot, mask[...], weight[...]))
    f[2], f[5] = mids[8], mids[9]
    face = {i: across(x[i], f[i - 1], f[i]) for i in (0, 1, 2, 6, 7, 8)}
    s = {i: moved(s[i], p[i], face[i + 1] - face[i], f[i], z[i], y[i]) for i in (0, 1, 6, 7)}
    s[2] = mids[10] + p[2] * face[2]
    s[5] = mids[11] - p[5] * face[6]
    for i in (0, 1, 2, 5, 6, 7):
        new_sat[i] = s[i]
    for j in range(2):
        new_sat[3 + j] = middle[j]
    f = {i: frac(s[i], m[i]) for i in (0, 1, 2, 5, 6, 7)}
    rates.append(
        rates_of([f[i] for pair in OUTER for i in pair], hot, mask[...], weight[...])
    )
    zero = jnp.zeros_like(rates[0])
    share = early[...] + jnp.concatenate(rates + [zero], axis=0)
    share = jnp.concatenate([share, share], axis=0)
    for j in range(shares.shape[0] // 8):
        shares[8 * j : 8 * j + 8, :] = share


def line_kernel(parts, out):
    members, per = 8, 4
    width = SUBSTEPS + 1
    rows = []
    for k in range(SUBSTEPS):
        total = parts[pl.ds(k, members, stride=per * width), :]
        for j in range(1, per):
            total = total + parts[pl.ds(width * j + k, members, stride=per * width), :]
        rows.append(total)
    errors = [parts[width * j + SUBSTEPS : width * j + SUBSTEPS + 1, :] for j in range(per)]
    rows.append(jnp.concatenate(errors, axis=0))
    block = jnp.concatenate(rows, axis=0)
    size = block.shape[0]
    for j in range(out.shape[0] // size):
        out[size * j : size * (j + 1), :] = block


def gram_kernel(parts, where, sat, rates_out, gram, sat_out, sem):
    writing = pltpu.make_async_copy(sat, sat_out, sem)
    writing.start()
    tile = where[0]
    own_x = where[2]
    own_z = where[3]
    groups, per, layer = 4, 4, 8
    rows = SUBSTEPS * layer
    wells = parts.shape[1]
    mine = rates_out.shape[2]
    size = rows + per
    sums = []
    for g in range(groups):
        starts = [(g * per + j) * size for j in range(per)]
        total = parts[starts[0] : starts[0] + rows]
        for start in starts[1:]:
            total = total + parts[start : start + rows]
        sums.append(total)
    packed = jnp.concatenate(
        [parts[y * size + rows : (y + 1) * size] for y in range(per)], axis=0
    )
    tiles = packed.shape[0]
    lane = lax.broadcasted_iota(jnp.int32, packed.shape, 1)
    home = lane // mine == lax.broadcasted_iota(jnp.int32, packed.shape, 0)
    errors = []
    for k in range(SUBSTEPS):
        front = packed if k == 0 else pltpu.roll(packed, wells - mine * k, 1)
        moved = pltpu.roll(front, 0, 1, stride=mine, stride_axis=0)
        errors.append(jnp.sum(jnp.where(home, moved, 0.0), axis=0, keepdims=True))
    ensemble = groups * layer
    own = sums[0]
    for g in range(1, groups):
        own = jnp.where(own_x == g, sums[g], own)
    lane = lax.broadcasted_iota(jnp.int32, (layer, wells), 1)
    sublane = lax.broadcasted_iota(jnp.int32, (layer, wells), 0)
    products = [jnp.zeros((layer, wells), jnp.float32)] * groups
    own_rates = []
    for k in range(SUBSTEPS):
        part = slice(k * layer, (k + 1) * layer)
        scale = 1.0 / errors[k]
        data = [total[part] * scale for total in sums]
        mean = jnp.sum(data[0] + data[1] + data[2] + data[3], axis=0, keepdims=True) * (1.0 / ensemble)
        row = jnp.sum(jnp.where(sublane == own_z, own[part], 0.0), axis=0, keepdims=True)
        own_rates.append(row)
        centered = row * scale - mean
        products = [total + (d - mean) * centered for total, d in zip(products, data)]
    line = jnp.zeros((layer, wells), jnp.float32)
    for g in range(groups):
        dots = jnp.sum(products[g], axis=1, keepdims=True)
        line = line + jnp.where(lane == sublane + g * layer, dots, 0.0)
    line = jnp.sum(line, axis=0, keepdims=True) * (1.0 / (ensemble - 1.0))
    gram[...] = line[:, :ensemble]
    front = jnp.concatenate(own_rates + [jnp.zeros((layer - SUBSTEPS, wells), jnp.float32)], axis=0)
    front = pltpu.roll(front, lax.rem(wells - tile * mine, wells), 1)
    for k in range(SUBSTEPS):
        rates_out[k] = front[k : k + 1, :mine]
    writing.wait()


VMEM = pl.BlockSpec(memory_space=pltpu.VMEM)
ANY = pl.BlockSpec(memory_space=pl.ANY)
SMEM = pl.BlockSpec(memory_space=pltpu.SMEM)


def shape(*dims):
    return jax.ShapeDtypeStruct(dims, jnp.float32)


def held(*dims):
    return pltpu.VMEM(dims, jnp.float32)


def body(
    saturation,
    mobility,
    pore_scale,
    flux_x,
    flux_y,
    flux_z,
    conn_cell,
    conn_well,
    conn_factor,
    obs_error,
):
    rows, layers, columns = saturation.shape[1:]
    fields = [
        a.reshape(rows, layers, columns)
        for a in (saturation, mobility, pore_scale, flux_x, flux_y, flux_z)
    ]
    tiles = lax.axis_size(TILE)
    tile = lax.axis_index(TILE)
    where = jnp.stack(
        [tile, jnp.full_like(tile, tiles - 1), lax.axis_index("x"), lax.axis_index("zl")]
    ).astype(jnp.int32)
    up, down, *fields = pl.pallas_call(
        edge_kernel,
        out_shape=(held(UP_ROWS, layers, columns), held(DOWN_ROWS, layers, columns))
        + (held(rows, layers, columns),) * 6,
        in_specs=[ANY] * 6,
        out_specs=(VMEM,) * 8,
        scratch_shapes=[pltpu.SemaphoreType.DMA((18,))],
        name="edges",
    )(*fields)
    low = lax.ppermute(up, TILE, [(i, i + 1) for i in range(tiles - 1)])
    high = lax.ppermute(down, TILE, [(i + 1, i) for i in range(tiles - 1)])
    wells = obs_error.shape[0] * tiles
    count = conn_cell.shape[0]
    sat, mob, pore, qx, qy, qz = fields
    mids, middle, early, hot, mask, weight = pl.pallas_call(
        inside_kernel,
        out_shape=(
            shape(12, layers, columns),
            shape(2, layers, columns),
            shape(SUBSTEPS + 1, wells),
            jax.ShapeDtypeStruct((count, 6 * layers), jnp.bfloat16),
            shape(count, columns),
            shape(count, wells),
        ),
        in_specs=[VMEM] * 10 + [ANY],
        out_specs=(VMEM,) * 6,
        compiler_params=pltpu.CompilerParams(vmem_limit_bytes=32 * 1024 * 1024),
        name="inside",
    )(
        *fields,
        conn_cell.reshape(1, count),
        conn_well.reshape(1, count),
        conn_factor.reshape(1, count),
        obs_error.T,
        up,
    )
    new_saturation, shares = pl.pallas_call(
        outside_kernel,
        out_shape=(held(rows, layers, columns), held(128, wells)),
        in_specs=[VMEM] * 13 + [SMEM],
        out_specs=(VMEM, VMEM),
        compiler_params=pltpu.CompilerParams(vmem_limit_bytes=32 * 1024 * 1024),
        name="outside",
    )(mob, pore, qx, qy, qz, low, high, mids, middle, early, hot, mask, weight, where)
    line = lax.all_to_all(shares.reshape(32, 4, wells), LINE, 0, 0)
    line = pltpu.with_memory_space_constraint(line.reshape(128, wells), pltpu.VMEM)
    (spreads,) = pl.pallas_call(
        line_kernel,
        out_shape=(held(16 * 28, wells),),
        in_specs=[VMEM],
        out_specs=(VMEM,),
        name="line_sums",
    )(line)
    plane = lax.all_to_all(spreads.reshape(16, 7, 4, wells), PLANE, 0, 0)
    plane = pltpu.with_memory_space_constraint(plane.reshape(16 * 28, wells), pltpu.VMEM)
    rates, gram, new_saturation = pl.pallas_call(
        gram_kernel,
        out_shape=(
            shape(SUBSTEPS, 1, obs_error.shape[0]),
            shape(1, 32),
            shape(rows, layers, columns),
        ),
        in_specs=[VMEM, SMEM, VMEM],
        out_specs=(VMEM, VMEM, ANY),
        scratch_shapes=[pltpu.SemaphoreType.DMA],
        name="gram_row",
    )(plane, where, pltpu.with_memory_space_constraint(new_saturation, pltpu.VMEM))
    return (
        new_saturation.reshape(saturation.shape),
        jnp.transpose(rates, (1, 2, 0)),
        gram,
    )


def solution(mesh):
    split = Mesh(mesh.devices.reshape(SIZES), AXES)
    in_specs = (P(MEMBER, TILE, None, None),) * 6 + (P(TILE),) * 3 + (P(TILE, None),)
    out_specs = (P(MEMBER, TILE, None, None), P(MEMBER, TILE, None), P(MEMBER, None))
    return jax.shard_map(body, mesh=split, in_specs=in_specs, out_specs=out_specs, check_vma=False)
```

```python
import jax
import jax.numpy as jnp
from jax import lax
from jax.experimental import pallas as pl
from jax.experimental.pallas import tpu as pltpu
from jax.sharding import Mesh
from jax.sharding import PartitionSpec as P

SUBSTEPS = 3
AXES = ("x", "zl", "y", "zh", "c")
SIZES = (4, 8, 4, 2, 2)
MEMBER = ("x", "zl")
TILE = ("y", "zh", "c")
LINE = ("zl", "zh", "c")
PLANE = ("x", "y")
UP_ROWS = 7
DOWN_ROWS = 8
HIGHEST = lax.Precision.HIGHEST


def frac(sat, mob):
    wet = sat * sat
    dry = (1.0 - sat) * (1.0 - sat)
    return wet / (wet + mob * dry)


def inner(flux, axis):
    return jnp.where(lax.broadcasted_iota(jnp.int32, flux.shape, axis) > 0, flux, 0.0)


def across(flux, below, here):
    return flux * jnp.where(flux > 0.0, below, here)


def spread(flow, flux, axis):
    face = across(flux, pltpu.roll(flow, 1, axis), flow)
    return pltpu.roll(face, flow.shape[axis] - 1, axis) - face


def moved(sat, pore, net, flow, flux_z, flux_y):
    return sat - pore * (
        net + spread(flow, inner(flux_z, 0), 0) + spread(flow, inner(flux_y, 1), 1)
    )


def edge_kernel(sat, mob, pore, qx, qy, qz, up, down, s, m, p, x, y, z, sem):
    pieces = ((0, 3), (5, 3), (3, 2))
    loads = []
    for j, (start, size) in enumerate(pieces):
        for k, (field, near) in enumerate(
            ((sat, s), (mob, m), (qx, x), (qy, y), (qz, z), (pore, p))
        ):
            part = pl.ds(start, size)
            loads.append(pltpu.make_async_copy(field.at[part], near.at[part], sem.at[6 * j + k]))
    for load in loads:
        load.start()
    for load in loads[:12]:
        load.wait()
    f = [frac(s[i], m[i]) for i in range(3)]
    face_1 = across(x[1], f[0], f[1])
    flow_1 = frac(moved(s[1], p[1], across(x[2], f[1], f[2]) - face_1, f[1], z[1], y[1]), m[1])
    for k, near in enumerate((s, m, p, z, y, x)):
        down[k] = near[0]
    down[6] = face_1
    down[7] = jnp.minimum(x[1], 0.0) * flow_1
    f = {i: frac(s[i], m[i]) for i in range(5, 8)}
    face_7 = across(x[7], f[6], f[7])
    flow_6 = frac(moved(s[6], p[6], face_7 - across(x[6], f[5], f[6]), f[6], z[6], y[6]), m[6])
    for k, near in enumerate((s, m, p, z, y)):
        up[k] = near[7]
    up[5] = face_7
    up[6] = jnp.maximum(x[7], 0.0) * flow_6
    for load in loads[12:]:
        load.wait()


OUTER = ((0, 7), (1, 6), (2, 5))
INNER = ((3, 4), (2, 5), (1, 6))


def one_hot(row_of, pairs, layers):
    lane = lax.broadcasted_iota(jnp.int32, row_of.shape, 1)
    hots = []
    for first, second in pairs:
        target = jnp.where(lane < layers, lane + first * layers, lane + (second - 1) * layers)
        hots.append(jnp.where(row_of == target, 1.0, 0.0).astype(jnp.bfloat16))
    return jnp.concatenate(hots, axis=1)


def rates_of(flows, hot, mask, weight):
    stack = jnp.concatenate(flows, axis=0)
    big = stack.astype(jnp.bfloat16)
    rest = stack - big.astype(jnp.float32)
    small = rest.astype(jnp.bfloat16)
    found = mask * sum(
        jnp.dot(hot[:, : stack.shape[0]], part, preferred_element_type=jnp.float32)
        for part in (small, big)
    )
    picked = jnp.sum(found, axis=1, keepdims=True)
    return jnp.sum(weight * picked, axis=0, keepdims=True)


def inside_kernel(
    sat, mob, pore, qx, qy, qz, cell, well, factor, obs, after, mids, middle, early, hot, mask, weight
):
    rows, layers, columns = sat.shape
    count = cell.shape[1]

    def column_of(row):
        return jnp.concatenate(
            [
                jnp.transpose(jnp.broadcast_to(row[:, j : j + columns], (columns, columns)))
                for j in range(0, count, columns)
            ],
            axis=0,
        )

    cells = column_of(cell[...])
    row_of = lax.div(cells, columns)
    lane = lax.broadcasted_iota(jnp.int32, cells.shape, 1)
    mask[...] = jnp.where(cells - row_of * columns == lane, 1.0, 0.0)
    hot[...] = one_hot(row_of, OUTER, layers)
    near = one_hot(row_of, INNER, layers)
    weight[...] = jnp.where(column_of(well[...]) == lane, column_of(factor[...]), 0.0)

    f = [frac(sat[i], mob[i]) for i in range(rows)]
    face = {i: across(qx[i], f[i - 1], f[i]) for i in range(1, rows)}
    mids[0] = f[0]
    mids[1] = f[7]
    mids[2] = moved(sat[0], pore[0], face[1], f[0], qz[0], qy[0])
    mids[3] = moved(sat[7], pore[7], -face[7], f[7], qz[7], qy[7])
    s = {i: moved(sat[i], pore[i], face[i + 1] - face[i], f[i], qz[i], qy[i]) for i in range(1, 7)}
    f = {i: frac(s[i], mob[i]) for i in range(1, 7)}
    rates = [rates_of([f[i] for pair in INNER for i in pair], near, mask[...], weight[...])]
    face = {i: across(qx[i], f[i - 1], f[i]) for i in range(2, 7)}
    mids[4] = f[1]
    mids[5] = f[6]
    mids[6] = moved(s[1], pore[1], face[2], f[1], qz[1], qy[1])
    mids[7] = moved(s[6], pore[6], -face[6], f[6], qz[6], qy[6])
    s = {i: moved(s[i], pore[i], face[i + 1] - face[i], f[i], qz[i], qy[i]) for i in range(2, 6)}
    f = {i: frac(s[i], mob[i]) for i in range(2, 6)}
    rates.append(rates_of([f[i] for pair in INNER[:2] for i in pair], near, mask[...], weight[...]))
    face = {i: across(qx[i], f[i - 1], f[i]) for i in range(3, 6)}
    mids[8] = f[2]
    mids[9] = f[5]
    mids[10] = moved(s[2], pore[2], face[3], f[2], qz[2], qy[2])
    mids[11] = moved(s[5], pore[5], -face[5], f[5], qz[5], qy[5])
    last = [moved(s[i], pore[i], face[i + 1] - face[i], f[i], qz[i], qy[i]) for i in (3, 4)]
    for j in range(2):
        middle[j] = last[j]
    flows = [frac(last[j], mob[3 + j]) for j in range(2)]
    rates.append(rates_of(flows, near, mask[...], weight[...]))
    errors = jnp.concatenate(
        [obs[k : k + 1, :] for k in range(SUBSTEPS)]
        + [jnp.zeros((1, columns - SUBSTEPS * obs.shape[1]), jnp.float32)],
        axis=1,
    )
    early[...] = jnp.concatenate(rates + [errors], axis=0)


def outside_kernel(
    mob, pore, qx, qy, qz, low, high, mids, middle, early, hot, mask, weight, where, new_sat, shares
):
    tile = where[0]
    last = where[1]
    has_low = tile > 0
    has_high = tile < last
    below = jnp.where(has_low, low[0], 0.5)
    below_mob = jnp.where(has_low, low[1], 1.0)
    above = jnp.where(has_high, high[0], 0.5)
    above_mob = jnp.where(has_high, high[1], 1.0)
    x = {i: qx[i] for i in range(1, 8)}
    x[0] = jnp.where(has_low, qx[0], 0.0)
    x[8] = high[5]
    z = {i: qz[i] for i in (0, 1, 6, 7)}
    z[-1], z[8] = low[3], high[3]
    y = {i: qy[i] for i in (0, 1, 6, 7)}
    y[-1], y[8] = low[4], high[4]
    p = {i: pore[i] for i in (0, 1, 2, 5, 6, 7)}
    p[-1], p[8] = low[2], high[2]
    m = {i: mob[i] for i in (0, 1, 2, 5, 6, 7)}
    m[-1], m[8] = below_mob, above_mob

    f = {-1: frac(below, below_mob), 0: mids[0], 7: mids[1], 8: frac(above, above_mob)}
    out_low = jnp.minimum(low[5], 0.0) / f[-1]
    out_high = jnp.maximum(high[6], 0.0) / f[8]
    face = {i: across(x[i], f[i - 1], f[i]) for i in (0, 8)}
    s = {
        -1: moved(below, p[-1], face[0] - low[5], f[-1], z[-1], y[-1]),
        0: mids[2] + p[0] * face[0],
        7: mids[3] - p[7] * face[8],
        8: moved(above, p[8], high[6] - face[8], f[8], z[8], y[8]),
    }

    f = {i: frac(s[i], m[i]) for i in (-1, 0, 7, 8)}
    rates = [rates_of([f[0], f[7]], hot, mask[...], weight[...])]
    f[1], f[6] = mids[4], mids[5]
    face = {i: across(x[i], f[i - 1], f[i]) for i in (0, 1, 7, 8)}
    face[-1] = low[6] + out_low * f[-1]
    face[9] = out_high * f[8] + high[7]
    s = {i: moved(s[i], p[i], face[i + 1] - face[i], f[i], z[i], y[i]) for i in (-1, 0, 7, 8)}
    s[1] = mids[6] + p[1] * face[1]
    s[6] = mids[7] - p[6] * face[7]

    f = {i: frac(s[i], m[i]) for i in (-1, 0, 1, 6, 7, 8)}
    rates.append(rates_of([f[0], f[7], f[1], f[6]], hot, mask[...], weight[...]))
    f[2], f[5] = mids[8], mids[9]
    face = {i: across(x[i], f[i - 1], f[i]) for i in (0, 1, 2, 6, 7, 8)}
    s = {i: moved(s[i], p[i], face[i + 1] - face[i], f[i], z[i], y[i]) for i in (0, 1, 6, 7)}
    s[2] = mids[10] + p[2] * face[2]
    s[5] = mids[11] - p[5] * face[6]
    for i in (0, 1, 2, 5, 6, 7):
        new_sat[i] = s[i]
    for j in range(2):
        new_sat[3 + j] = middle[j]
    f = {i: frac(s[i], m[i]) for i in (0, 1, 2, 5, 6, 7)}
    rates.append(
        rates_of([f[i] for pair in OUTER for i in pair], hot, mask[...], weight[...])
    )
    zero = jnp.zeros_like(rates[0])
    share = early[...] + jnp.concatenate(rates + [zero], axis=0)
    share = jnp.concatenate([share, share], axis=0)
    for j in range(shares.shape[0] // 8):
        shares[8 * j : 8 * j + 8, :] = share


def line_kernel(parts, out):
    members, per = 8, 4
    width = SUBSTEPS + 1
    rows = []
    for k in range(SUBSTEPS):
        total = parts[pl.ds(k, members, stride=per * width), :]
        for j in range(1, per):
            total = total + parts[pl.ds(width * j + k, members, stride=per * width), :]
        rows.append(total)
    errors = [parts[width * j + SUBSTEPS : width * j + SUBSTEPS + 1, :] for j in range(per)]
    rows.append(jnp.concatenate(errors, axis=0))
    block = jnp.concatenate(rows, axis=0)
    size = block.shape[0]
    for j in range(out.shape[0] // size):
        out[size * j : size * (j + 1), :] = block


def gram_kernel(parts, where, sat, rates_hbm, gram_hbm, sat_out, rates_out, gram, sem):
    writing = pltpu.make_async_copy(sat, sat_out, sem.at[0])
    writing.start()
    tile = where[0]
    own_x = where[2]
    own_z = where[3]
    groups, per, layer = 4, 4, 8
    rows = SUBSTEPS * layer
    wells = parts.shape[1]
    mine = rates_out.shape[2]
    size = rows + per
    sums = []
    for g in range(groups):
        starts = [(g * per + j) * size for j in range(per)]
        total = parts[starts[0] : starts[0] + rows]
        for start in starts[1:]:
            total = total + parts[start : start + rows]
        sums.append(total)
    packed = jnp.concatenate(
        [parts[y * size + rows : (y + 1) * size] for y in range(per)], axis=0
    )
    tiles = packed.shape[0]
    lane = lax.broadcasted_iota(jnp.int32, packed.shape, 1)
    home = lane // mine == lax.broadcasted_iota(jnp.int32, packed.shape, 0)
    errors = []
    for k in range(SUBSTEPS):
        front = packed if k == 0 else pltpu.roll(packed, wells - mine * k, 1)
        moved = pltpu.roll(front, 0, 1, stride=mine, stride_axis=0)
        errors.append(jnp.sum(jnp.where(home, moved, 0.0), axis=0, keepdims=True))
    ensemble = groups * layer
    own = sums[0]
    for g in range(1, groups):
        own = jnp.where(own_x == g, sums[g], own)
    lane = lax.broadcasted_iota(jnp.int32, (layer, wells), 1)
    sublane = lax.broadcasted_iota(jnp.int32, (layer, wells), 0)
    products = [jnp.zeros((layer, wells), jnp.float32)] * groups
    own_rates = []
    for k in range(SUBSTEPS):
        part = slice(k * layer, (k + 1) * layer)
        scale = 1.0 / errors[k]
        data = [total[part] * scale for total in sums]
        mean = jnp.sum(data[0] + data[1] + data[2] + data[3], axis=0, keepdims=True) * (1.0 / ensemble)
        row = jnp.sum(jnp.where(sublane == own_z, own[part], 0.0), axis=0, keepdims=True)
        own_rates.append(row)
        centered = row * scale - mean
        products = [total + (d - mean) * centered for total, d in zip(products, data)]
    line = jnp.zeros((layer, wells), jnp.float32)
    for g in range(groups):
        dots = jnp.sum(products[g], axis=1, keepdims=True)
        line = line + jnp.where(lane == sublane + g * layer, dots, 0.0)
    line = jnp.sum(line, axis=0, keepdims=True) * (1.0 / (ensemble - 1.0))
    gram[...] = line[:, :ensemble]
    front = jnp.concatenate(own_rates + [jnp.zeros((layer - SUBSTEPS, wells), jnp.float32)], axis=0)
    front = pltpu.roll(front, lax.rem(wells - tile * mine, wells), 1)
    for k in range(SUBSTEPS):
        rates_out[k] = front[k : k + 1, :mine]
    results = [
        pltpu.make_async_copy(rates_out, rates_hbm, sem.at[1]),
        pltpu.make_async_copy(gram, gram_hbm, sem.at[2]),
    ]
    for result in results:
        result.start()
    writing.wait()
    for result in results:
        result.wait()


VMEM = pl.BlockSpec(memory_space=pltpu.VMEM)
ANY = pl.BlockSpec(memory_space=pl.ANY)
SMEM = pl.BlockSpec(memory_space=pltpu.SMEM)


def shape(*dims):
    return jax.ShapeDtypeStruct(dims, jnp.float32)


def held(*dims):
    return pltpu.VMEM(dims, jnp.float32)


def body(
    saturation,
    mobility,
    pore_scale,
    flux_x,
    flux_y,
    flux_z,
    conn_cell,
    conn_well,
    conn_factor,
    obs_error,
):
    rows, layers, columns = saturation.shape[1:]
    fields = [
        a.reshape(rows, layers, columns)
        for a in (saturation, mobility, pore_scale, flux_x, flux_y, flux_z)
    ]
    tiles = lax.axis_size(TILE)
    tile = lax.axis_index(TILE)
    where = jnp.stack(
        [tile, jnp.full_like(tile, tiles - 1), lax.axis_index("x"), lax.axis_index("zl")]
    ).astype(jnp.int32)
    up, down, *fields = pl.pallas_call(
        edge_kernel,
        out_shape=(held(UP_ROWS, layers, columns), held(DOWN_ROWS, layers, columns))
        + (held(rows, layers, columns),) * 6,
        in_specs=[ANY] * 6,
        out_specs=(VMEM,) * 8,
        scratch_shapes=[pltpu.SemaphoreType.DMA((18,))],
        name="edges",
    )(*fields)
    low = lax.ppermute(up, TILE, [(i, i + 1) for i in range(tiles - 1)])
    high = lax.ppermute(down, TILE, [(i + 1, i) for i in range(tiles - 1)])
    wells = obs_error.shape[0] * tiles
    count = conn_cell.shape[0]
    sat, mob, pore, qx, qy, qz = fields
    mids, middle, early, hot, mask, weight = pl.pallas_call(
        inside_kernel,
        out_shape=(
            shape(12, layers, columns),
            shape(2, layers, columns),
            shape(SUBSTEPS + 1, wells),
            jax.ShapeDtypeStruct((count, 6 * layers), jnp.bfloat16),
            shape(count, columns),
            shape(count, wells),
        ),
        in_specs=[VMEM] * 10 + [ANY],
        out_specs=(VMEM,) * 6,
        compiler_params=pltpu.CompilerParams(vmem_limit_bytes=32 * 1024 * 1024),
        name="inside",
    )(
        *fields,
        conn_cell.reshape(1, count),
        conn_well.reshape(1, count),
        conn_factor.reshape(1, count),
        obs_error.T,
        up,
    )
    new_saturation, shares = pl.pallas_call(
        outside_kernel,
        out_shape=(held(rows, layers, columns), held(128, wells)),
        in_specs=[VMEM] * 13 + [SMEM],
        out_specs=(VMEM, VMEM),
        compiler_params=pltpu.CompilerParams(vmem_limit_bytes=32 * 1024 * 1024),
        name="outside",
    )(mob, pore, qx, qy, qz, low, high, mids, middle, early, hot, mask, weight, where)
    line = lax.all_to_all(shares.reshape(32, 4, wells), LINE, 0, 0)
    line = pltpu.with_memory_space_constraint(line.reshape(128, wells), pltpu.VMEM)
    (spreads,) = pl.pallas_call(
        line_kernel,
        out_shape=(held(16 * 28, wells),),
        in_specs=[VMEM],
        out_specs=(VMEM,),
        name="line_sums",
    )(line)
    plane = lax.all_to_all(spreads.reshape(16, 7, 4, wells), PLANE, 0, 0)
    plane = pltpu.with_memory_space_constraint(plane.reshape(16 * 28, wells), pltpu.VMEM)
    rates, gram, new_saturation = pl.pallas_call(
        gram_kernel,
        out_shape=(
            shape(SUBSTEPS, 1, obs_error.shape[0]),
            shape(1, 32),
            shape(rows, layers, columns),
        ),
        in_specs=[VMEM, SMEM, VMEM],
        out_specs=(ANY,) * 3,
        scratch_shapes=[
            pltpu.VMEM((SUBSTEPS, 1, obs_error.shape[0]), jnp.float32),
            pltpu.VMEM((1, 32), jnp.float32),
            pltpu.SemaphoreType.DMA((3,)),
        ],
        name="gram_row",
    )(plane, where, pltpu.with_memory_space_constraint(new_saturation, pltpu.VMEM))
    return (
        new_saturation.reshape(saturation.shape),
        jnp.transpose(rates, (1, 2, 0)),
        gram,
    )


def solution(mesh):
    split = Mesh(mesh.devices.reshape(SIZES), AXES)
    in_specs = (P(MEMBER, TILE, None, None),) * 6 + (P(TILE),) * 3 + (P(TILE, None),)
    out_specs = (P(MEMBER, TILE, None, None), P(MEMBER, TILE, None), P(MEMBER, None))
    return jax.shard_map(body, mesh=split, in_specs=in_specs, out_specs=out_specs, check_vma=False)
```
